32 devices in a mesh: dp: 8 (over y, x, core), tensor: 4 (over z).
Axes of the slice: x: 2, y: 2, z: 4, core: 2. Of those that a mesh axis runs over, the one named last changes fastest.
Arguments:
- inputs: bfloat16 [8, 1024, 768], P('dp', 'tensor'), may hold values from -6 to 6
- ln_gain: float32 [768], P(('dp', 'tensor')), may hold values from 0.25 to 1.75
- ln_bias: float32 [768], P(('dp', 'tensor')), may hold values from -1.5 to 1.5
- w_qkv: bfloat16 [768, 3, 768], P('dp', None, 'tensor'), may hold values from -1.5 to 1.5, as said below
- b_qkv: bfloat16 [3, 12, 64], P(None, 'tensor', 'dp'), may hold values from -2.5 to 2.5
- w_out: bfloat16 [768, 768], P('tensor', 'dp'), may hold values from -0.875 to 0.875
- w_in: bfloat16 [768, 3072], P('dp', 'tensor'), may hold values from -0.21875 to 0.21875
- b_in: bfloat16 [24, 128], P('tensor', 'dp'), may hold values from -2.5 to 2.5
- w_down: bfloat16 [3072, 768], P('tensor', 'dp'), may hold values from -0.109375 to 0.109375
- out_bias: float32 [2, 768], P(None, ('dp', 'tensor')), may hold values from -2.5 to 2.5
- cotangent: bfloat16 [8, 1024, 768], P('dp', 'tensor'), may hold values from -6 to 6
Outputs:
- outputs: bfloat16 [8, 1024, 768], P('dp', 'tensor')
- input_grad: bfloat16 [8, 1024, 768], P('dp', 'tensor')
- ln_gain_grad: float32 [768], P(('dp', 'tensor'))
- ln_bias_grad: float32 [768], P(('dp', 'tensor'))
- w_qkv_grad: float32 [768, 3, 768], P('dp', None, 'tensor')
- b_qkv_grad: float32 [3, 12, 64], P(None, 'tensor', 'dp')
- w_out_grad: float32 [768, 768], P('tensor', 'dp')
- w_in_grad: float32 [768, 3072], P('dp', 'tensor')
- b_in_grad: float32 [24, 128], P('tensor', 'dp')
- w_down_grad: float32 [3072, 768], P('tensor', 'dp')
- out_bias_grad: float32 [2, 768], P(None, ('dp', 'tensor'))
The draws below stay inside these ranges and needn't reach their ends.
Inputs may be any that keep to these rules, and one draw needn't show every extreme that they name: `w_qkv`: projection weights of the queries, keys and values.
All inputs are finite; a program needn't handle non-finite values.
Results may differ from the reference program's by a relative error of at most 0.0082.
Values may be sent and summed in bfloat16 or wider, within the bound.
No kernel may reach another device: no remote copies, remote signals or barrier semaphores. Data moves between devices by JAX's collectives and lax.ppermute only.
A program may use at most 128 MiB of HBM per device.

```python
import math
import jax
import jax.numpy as jnp
from jax import lax

D = 768
H = 12
HD = 64
FF = 3072
ROT = 16
LEN = 1024
SEQS = 8


def draw_w_qkv(key, part):
    key_base = jax.random.fold_in(key, 0)
    base_rows = jax.random.normal(key_base, (D, 3, D), jnp.float32) * D ** (-0.5)
    return jnp.clip(base_rows, -1.5, 1.5).astype(jnp.bfloat16)


def with_spikes(drawn, rng, source, target, shards_of, factor):
    owner, partner = [(jnp.arange(drawn.shape[axis_at]) // (drawn.shape[axis_at] // shards_of)).reshape([-1 if axis == axis_at else 1 for axis in range(drawn.ndim)]) for axis_at in (source, target)]
    chosen = jax.random.permutation(rng, shards_of)[partner]
    strong = (owner == chosen) | (owner == (partner + shards_of // 2) % shards_of)
    return jnp.where(strong, factor * drawn, drawn)


def levels(own_key, dims, cuts, smallest, largest):
    level, own = 1.0, jax.random.fold_in(own_key, 6)
    for dim, shards_of in cuts:
        steps = jnp.exp(jax.random.uniform(jax.random.fold_in(own, dim), (shards_of,), jnp.float32, smallest / len(cuts), largest / len(cuts)))
        level = level * jnp.repeat(steps, dims[dim] // shards_of).reshape([-1 if axis == dim else 1 for axis in range(len(dims))])
    return level


def normal_values(rng, extent, deviation, most, shards=(), dtype=jnp.bfloat16):
    loudness = levels(rng, extent, shards, -0.22, 0.18) if shards else 1.0
    result = jax.random.normal(rng, extent, jnp.float32) * deviation * loudness
    return jnp.minimum(jnp.maximum(result, -most), most).astype(dtype)


def heavy_noise(key, extent, width, reach, pieces, heavy, dtype=jnp.bfloat16):
    entries = width * jax.random.normal(key, extent, jnp.float32)
    if pieces:
        entries = entries * levels(key, extent, pieces, -0.22, 0.18)
    return jnp.clip(with_spikes(entries, jax.random.fold_in(key, 3), *heavy), -reach, reach).astype(dtype)


def setup_inputs(seed: int = 0) -> dict:
    arg_keys = jax.random.split(jax.random.key(seed), 12)
    return {
        "inputs": normal_values(arg_keys[0], (SEQS, LEN, D), 1.0, 6.0, ((0, 8), (1, 4))),
        "ln_gain": jnp.clip(1.0 + 0.15 * jax.random.normal(arg_keys[1], (D,), jnp.float32), 0.25, 1.75),
        "ln_bias": normal_values(arg_keys[2], (D,), 0.3, 1.5, ((0, 32),), jnp.float32),
        "w_qkv": draw_w_qkv(jax.random.fold_in(arg_keys[11], 71), 0),
        "b_qkv": normal_values(arg_keys[4], (3, H, HD), 0.5, 2.5, ((1, 4), (2, 8))),
        "w_out": normal_values(arg_keys[5], (D, D), (D // 16) ** -0.5, 0.875, ((0, 4), (1, 8))),
        "w_in": normal_values(arg_keys[6], (D, FF), D ** -0.5, 0.21875, ((0, 8), (1, 4))),
        "b_in": normal_values(arg_keys[7], (FF // 128, 128), 0.5, 2.5, ((0, 4), (1, 8))),
        "w_down": normal_values(arg_keys[8], (FF, D), FF ** -0.5, 0.109375, ((0, 4), (1, 8))),
        "out_bias": normal_values(arg_keys[9], (2, D), 0.5, 2.5, ((1, 32),), jnp.float32),
        "cotangent": heavy_noise(arg_keys[10], (SEQS, LEN, D), 1.0, 6.0, ((0, 8), (1, 4)), (0, 2, 8, 2.0)),
    }


EPS = 1e-05
ROOT_HALF = 0.7071067811865476
INV_ROOT_TAU = 0.3989422804014327
NEG_BIG = -1e+30

def rotary_tables(length, rot_dims):
    half_rot = rot_dims // 2
    position = jnp.arange(length).astype(jnp.float32)
    inv_freq = jnp.exp(jnp.arange(half_rot).astype(jnp.float32) * (-2.0 * math.log(10000.0) / rot_dims))
    angles = position[:, None] * inv_freq[None, :]
    return (jnp.cos(angles), jnp.sin(angles))

def rotate(tensor_in, cosine_table, sine_table, rot_dims, direction):
    half_rot = rot_dims // 2
    first_half = tensor_in[..., :half_rot]
    second_half = tensor_in[..., half_rot:rot_dims]
    cos_rows = cosine_table[:, None, :]
    sin_rows = sine_table[:, None, :] * direction
    return jnp.concatenate([first_half * cos_rows - second_half * sin_rows, second_half * cos_rows + first_half * sin_rows, tensor_in[..., rot_dims:]], axis=-1)

def gelu_parts(pre_act):
    normal_cdf = 0.5 * (1.0 + lax.erf(pre_act * ROOT_HALF))
    normal_pdf = jnp.exp(-0.5 * pre_act * pre_act) * INV_ROOT_TAU
    return (pre_act * normal_cdf, normal_cdf + pre_act * normal_pdf)

def masked_scores(q_rows, key_rows, first_row, block_rows, length):
    scores = jnp.einsum('qhd,khd->hqk', q_rows.astype(jnp.float32), key_rows.astype(jnp.float32)) / math.sqrt(HD)
    key_pos = jnp.arange(length)
    allowed = (first_row + jnp.arange(block_rows))[:, None] >= key_pos[None, :]
    return jnp.where(allowed[None], scores, NEG_BIG)

def attend(queries, key_rows, value_rows):
    length = queries.shape[0]
    block_rows = min(512, length)

    def one_block(first_row):
        q_rows = lax.dynamic_slice_in_dim(queries, first_row, block_rows, 0)
        scores = masked_scores(q_rows, key_rows, first_row, block_rows, length)
        row_max = lax.optimization_barrier(jnp.max(scores, axis=-1, keepdims=True))
        exponent = jnp.exp(scores - row_max)
        row_total = lax.optimization_barrier(jnp.sum(exponent, axis=-1, keepdims=True))
        attn_probs = (exponent / row_total).astype(jnp.bfloat16)
        context = jnp.einsum('hqk,khd->qhd', attn_probs.astype(jnp.float32), value_rows.astype(jnp.float32))
        return (context.astype(jnp.bfloat16), (row_max + jnp.log(row_total))[..., 0])
    starts = (jnp.arange(length // block_rows) * block_rows).astype(jnp.int32)
    context, logsum = lax.map(one_block, starts)
    return (context.reshape(queries.shape), logsum)

def attend_back(queries, key_rows, value_rows, logsum, ctx_grad):
    length = queries.shape[0]
    block_rows = min(512, length)

    def one_block(carry, block_index):
        key_grad, value_grad = carry
        first_row = block_index * block_rows
        q_rows = lax.dynamic_slice_in_dim(queries, first_row, block_rows, 0)
        d_rows = lax.dynamic_slice_in_dim(ctx_grad, first_row, block_rows, 0).astype(jnp.float32)
        scores = masked_scores(q_rows, key_rows, first_row, block_rows, length)
        attn_probs = jnp.exp(scores - logsum[block_index][..., None])
        low_probs = attn_probs.astype(jnp.bfloat16).astype(jnp.float32)
        value_grad = value_grad + jnp.einsum('hqk,qhd->khd', low_probs, d_rows)
        prob_grad = jnp.einsum('qhd,khd->hqk', d_rows, value_rows.astype(jnp.float32))
        row_dot = lax.optimization_barrier(jnp.sum(attn_probs * prob_grad, axis=-1, keepdims=True))
        score_grad = (attn_probs * (prob_grad - row_dot) / math.sqrt(HD)).astype(jnp.bfloat16).astype(jnp.float32)
        query_grad = jnp.einsum('hqk,khd->qhd', score_grad, key_rows.astype(jnp.float32))
        key_grad = key_grad + jnp.einsum('hqk,qhd->khd', score_grad, q_rows.astype(jnp.float32))
        return ((key_grad, value_grad), query_grad)
    zero_grads = jnp.zeros(queries.shape, jnp.float32)
    (key_grad, value_grad), query_grad = lax.scan(one_block, (zero_grads, zero_grads), jnp.arange(length // block_rows).astype(jnp.int32))
    return (query_grad.reshape(queries.shape), key_grad, value_grad)

def reference(inputs, ln_gain, ln_bias, w_qkv, b_qkv, w_out, w_in, b_in, w_down, out_bias, cotangent):
    cosine_table, sine_table = rotary_tables(LEN, ROT)
    qkv_matrix = w_qkv.reshape(D, 3 * D)
    qkv_bias = b_qkv.astype(jnp.float32)
    in_bias = b_in.astype(jnp.float32).reshape(FF)

    def one_sequence(totals, sequence_data):
        input_rows, cot_rows = sequence_data
        input_full = input_rows.astype(jnp.float32)
        centred = input_full - lax.optimization_barrier(jnp.mean(input_full, axis=-1, keepdims=True))
        inv_sigma = lax.rsqrt(lax.optimization_barrier(jnp.mean(centred * centred, axis=-1, keepdims=True)) + EPS)
        unit_rows = centred * inv_sigma
        normed = (unit_rows * ln_gain + ln_bias).astype(jnp.bfloat16)
        projected = jnp.dot(normed, qkv_matrix, preferred_element_type=jnp.float32).reshape(LEN, 3, H, HD) + qkv_bias
        queries = rotate(projected[:, 0], cosine_table, sine_table, ROT, 1.0).astype(jnp.bfloat16)
        key_rows = rotate(projected[:, 1], cosine_table, sine_table, ROT, 1.0).astype(jnp.bfloat16)
        value_rows = projected[:, 2].astype(jnp.bfloat16)
        context, logsum = attend(queries, key_rows, value_rows)
        flat_ctx = context.reshape(LEN, D)
        pre_act = jnp.dot(normed, w_in, preferred_element_type=jnp.float32) + in_bias
        activated, slopes = gelu_parts(pre_act)
        hidden = activated.astype(jnp.bfloat16)
        branch = jnp.dot(flat_ctx, w_out, preferred_element_type=jnp.float32) + jnp.dot(hidden, w_down, preferred_element_type=jnp.float32)
        out_seq = (input_full + branch + out_bias[0] + out_bias[1]).astype(jnp.bfloat16)
        cot_full = cot_rows.astype(jnp.float32)
        grad_down = jnp.dot(hidden.T, cot_rows, preferred_element_type=jnp.float32)
        pre_grad = jnp.dot(cot_rows, w_down.T, preferred_element_type=jnp.float32) * slopes
        pre_low = pre_grad.astype(jnp.bfloat16)
        grad_in = jnp.dot(normed.T, pre_low, preferred_element_type=jnp.float32)
        grad_in_bias = lax.optimization_barrier(jnp.sum(pre_grad, axis=0))
        grad_out = jnp.dot(flat_ctx.T, cot_rows, preferred_element_type=jnp.float32)
        ctx_grad = jnp.dot(cot_rows, w_out.T, preferred_element_type=jnp.float32).astype(jnp.bfloat16).reshape(LEN, H, HD)
        query_grad, key_grad, value_grad = attend_back(queries, key_rows, value_rows, logsum, ctx_grad)
        proj_grad = jnp.stack([rotate(query_grad, cosine_table, sine_table, ROT, -1.0), rotate(key_grad, cosine_table, sine_table, ROT, -1.0), value_grad], axis=1)
        grad_qkv_bias = lax.optimization_barrier(jnp.sum(proj_grad, axis=0))
        proj_low = proj_grad.astype(jnp.bfloat16).reshape(LEN, 3 * D)
        grad_qkv = jnp.dot(normed.T, proj_low, preferred_element_type=jnp.float32)
        norm_grad = jnp.dot(proj_low, qkv_matrix.T, preferred_element_type=jnp.float32) + jnp.dot(pre_low, w_in.T, preferred_element_type=jnp.float32)
        unit_grad = norm_grad * ln_gain
        input_grad = cot_full + inv_sigma * (unit_grad - lax.optimization_barrier(jnp.mean(unit_grad, axis=-1, keepdims=True)) - unit_rows * lax.optimization_barrier(jnp.mean(unit_grad * unit_rows, axis=-1, keepdims=True)))
        parts = (lax.optimization_barrier(jnp.sum(norm_grad * unit_rows, axis=0)), lax.optimization_barrier(jnp.sum(norm_grad, axis=0)), grad_qkv, grad_qkv_bias, grad_out, grad_in, grad_in_bias, grad_down, lax.optimization_barrier(jnp.sum(cot_full, axis=0)))
        new_totals = tuple((old + part for old, part in zip(totals, parts)))
        return (new_totals, (out_seq, input_grad.astype(jnp.bfloat16)))
    start_totals = (jnp.zeros((D,), jnp.float32), jnp.zeros((D,), jnp.float32), jnp.zeros((D, 3 * D), jnp.float32), jnp.zeros((3, H, HD), jnp.float32), jnp.zeros((D, D), jnp.float32), jnp.zeros((D, FF), jnp.float32), jnp.zeros((FF,), jnp.float32), jnp.zeros((FF, D), jnp.float32), jnp.zeros((D,), jnp.float32))
    totals, (outputs, input_grad) = lax.scan(one_sequence, start_totals, (inputs, cotangent))
    gain_grad, shift_grad, grad_qkv, grad_qkv_bias, grad_out, grad_in, grad_in_bias, grad_down, bias_grad = totals
    return (outputs, input_grad, gain_grad, shift_grad, grad_qkv.reshape(D, 3, D), grad_qkv_bias, grad_out, grad_in, grad_in_bias.reshape(FF // 128, 128), grad_down, jnp.stack([bias_grad, bias_grad]))
```

```python
import functools
import math

import jax
import jax.numpy as jnp
from jax import lax
from jax.experimental import pallas as pl
from jax.experimental.pallas import tpu as pltpu
from jax.sharding import PartitionSpec as P

ROT = 16
EPS = 1e-05
ROOT_HALF = 0.7071067811865476
INV_ROOT_TAU = 0.3989422804014327
NEG_BIG = -1e30
F32 = jnp.float32
BF16 = jnp.bfloat16


def dot(a, b, contract, out=F32):
    return lax.dot_general(
        a, b, (((contract[0],), (contract[1],)), ((), ())), preferred_element_type=out
    )


def swap(x, axis_name, size, step):
    return lax.ppermute(x, axis_name, [(i, i ^ step) for i in range(size)])


def bit_of(axis_name, step):
    return (lax.axis_index(axis_name) // step) % 2


def gather_bits(x, size, axis, steps):
    done = []
    for step in steps:
        other = swap(x, "dp", size, step)
        mine_first = bit_of("dp", step) == 0
        low = jnp.where(mine_first, x, other)
        high = jnp.where(mine_first, other, x)
        place = axis + sum(1 for s in done if s > step)
        x = jnp.stack([low, high], axis=place)
        done.append(step)
    shape = x.shape
    levels = len(steps)
    return x.reshape(shape[:axis] + (size,) + shape[axis + levels :])


def scatter_bits(x, size, axis, steps, wire):
    shape = x.shape
    levels = len(steps)
    x = x.reshape(shape[:axis] + (2,) * levels + shape[axis + 1 :])
    left = sorted(steps, reverse=True)
    for step in steps:
        place = axis + left.index(step)
        bit = bit_of("dp", step)
        keep = lax.dynamic_index_in_dim(x, bit, place, keepdims=False)
        send = lax.dynamic_index_in_dim(x, 1 - bit, place, keepdims=False)
        got = swap(send.astype(wire), "dp", size, step)
        x = keep + got.astype(F32)
        left.remove(step)
    return x


def rotate_rows(x, cosine, sine):
    half = ROT // 2
    first, second = x[:half], x[half:ROT]
    return jnp.concatenate(
        [first * cosine - second * sine, second * cosine + first * sine, x[ROT:]], axis=0
    )


def causal(block):
    key_pos = lax.broadcasted_iota(jnp.int32, (block, block), 0)
    query_pos = lax.broadcasted_iota(jnp.int32, (block, block), 1)
    return key_pos <= query_pos


def forward_kernel(scale, block, q_ref, k_ref, v_ref, cos_ref, sin_ref, ctx_ref, lse_ref):
    length = q_ref.shape[1]
    cosine, sine = cos_ref[...], sin_ref[...]
    queries = (rotate_rows(q_ref[...], cosine, sine).astype(BF16).astype(F32) * scale).astype(BF16)
    keys = jnp.transpose(rotate_rows(k_ref[...], cosine, sine)).astype(BF16)
    values = v_ref[...].astype(BF16)
    allowed = causal(block)
    for step in range(length // block):
        here = slice(step * block, (step + 1) * block)
        q_cols = queries[:, here]
        near = jnp.where(allowed, dot(keys[here], q_cols, (1, 0)), NEG_BIG)
        top = jnp.max(near, axis=0, keepdims=True)
        if step:
            far = dot(keys[: step * block], q_cols, (1, 0))
            top = jnp.maximum(top, jnp.max(far, axis=0, keepdims=True))
        near = jnp.exp(near - top)
        total = jnp.sum(near, axis=0, keepdims=True)
        context = dot(values[:, here], near.astype(BF16), (1, 0))
        if step:
            far = jnp.exp(far - top)
            total = total + jnp.sum(far, axis=0, keepdims=True)
            context = context + dot(values[:, : step * block], far.astype(BF16), (1, 0))
        ctx_ref[:, here] = (context / total).astype(BF16)
        lse_ref[0, :, here] = jnp.broadcast_to(top + jnp.log(total), (8, block))


def backward_kernel(
    scale, block, q_ref, k_ref, v_ref, cos_ref, sin_ref, lse_ref, grad_ref,
    dq_ref, dk_ref, dv_ref, sum_ref, keys_acc, values_acc,
):
    length = q_ref.shape[1]
    cosine, sine = cos_ref[...], sin_ref[...]
    rotated_q = rotate_rows(q_ref[...], cosine, sine).astype(BF16).astype(F32)
    queries = (rotated_q * scale).astype(BF16)
    query_rows = jnp.transpose(rotated_q).astype(BF16)
    rotated_k = rotate_rows(k_ref[...], cosine, sine)
    keys_t = rotated_k.astype(BF16)
    keys = jnp.transpose(rotated_k).astype(BF16)
    values = jnp.transpose(v_ref[...]).astype(BF16)
    grad_t = grad_ref[...]
    grad_rows = jnp.transpose(grad_t.astype(F32)).astype(BF16)
    allowed = causal(block)
    keys_acc[...] = jnp.zeros_like(keys_acc)
    values_acc[...] = jnp.zeros_like(values_acc)
    query_sum = 0.0
    for step in range(length // block):
        here = slice(step * block, (step + 1) * block)
        upto = slice(0, (step + 1) * block)
        lse = lse_ref[0, 0:1, here]
        scores = dot(keys[upto], queries[:, here], (1, 0))
        probs = jnp.exp(scores - lse)
        low = jnp.where(allowed, probs[here], 0.0)
        probs = jnp.concatenate([probs[: step * block], low], axis=0) if step else low
        values_acc[upto, :] += dot(probs.astype(BF16), grad_rows[here], (1, 0))
        prob_grad = dot(values[upto], grad_t[:, here], (1, 0))
        row_dot = jnp.sum(probs * prob_grad, axis=0, keepdims=True)
        score_grad = (probs * (prob_grad - row_dot) * scale).astype(BF16)
        keys_acc[upto, :] += dot(score_grad, query_rows[here], (1, 0))
        dq = dot(keys_t[:, upto], score_grad, (1, 0))
        dq = rotate_rows(dq, cosine[:, here], -sine[:, here])
        dq_ref[:, here] = dq.astype(BF16)
        query_sum = query_sum + jnp.sum(dq, axis=1, keepdims=True)
    dk = rotate_rows(jnp.transpose(keys_acc[...]), cosine, -sine)
    dv = jnp.transpose(values_acc[...])
    dk_ref[...] = dk.astype(BF16)
    dv_ref[...] = dv.astype(BF16)
    sums = [query_sum, jnp.sum(dk, axis=1, keepdims=True), jnp.sum(dv, axis=1, keepdims=True)]
    for place, part in enumerate(sums):
        sum_ref[0, 0, place] = jnp.broadcast_to(part, (part.shape[0], 128))


def attention_specs(heads, head_dim, length):
    def part(which):
        return pl.BlockSpec((head_dim, length), lambda s, h: (which * heads + h, s))

    table = pl.BlockSpec((ROT // 2, length), lambda s, h: (0, 0))
    return [part(0), part(1), part(2), table, table]


def attend(proj_t, cosine, sine, seqs, heads, head_dim, length):
    block = min(256, length)
    scale = 1.0 / math.sqrt(head_dim)
    per_head = pl.BlockSpec((head_dim, length), lambda s, h: (h, s))
    lse_spec = pl.BlockSpec((1, 8, length), lambda s, h: (h, 0, s))
    work = seqs * heads * length * length
    return pl.pallas_call(
        functools.partial(forward_kernel, scale, block),
        grid=(seqs, heads),
        in_specs=attention_specs(heads, head_dim, length),
        out_specs=[per_head, lse_spec],
        out_shape=[
            jax.ShapeDtypeStruct((heads * head_dim, seqs * length), BF16),
            jax.ShapeDtypeStruct((heads, 8, seqs * length), F32),
        ],
        cost_estimate=pl.CostEstimate(
            flops=4 * work * head_dim, bytes_accessed=proj_t.size * 4, transcendentals=work
        ),
        name="attend_forward",
    )(proj_t, proj_t, proj_t, cosine, sine)


def attend_back(proj_t, cosine, sine, lse, ctx_grad_t, seqs, heads, head_dim, length):
    block = min(256, length)
    scale = 1.0 / math.sqrt(head_dim)
    per_head = pl.BlockSpec((head_dim, length), lambda s, h: (h, s))
    lse_spec = pl.BlockSpec((1, 8, length), lambda s, h: (h, 0, s))
    sum_spec = pl.BlockSpec((1, 1, 3, head_dim, 128), lambda s, h: (s, h, 0, 0, 0))
    flat = jax.ShapeDtypeStruct((heads * head_dim, seqs * length), BF16)
    work = seqs * heads * length * length
    return pl.pallas_call(
        functools.partial(backward_kernel, scale, block),
        grid=(seqs, heads),
        in_specs=attention_specs(heads, head_dim, length) + [lse_spec, per_head],
        out_specs=[per_head, per_head, per_head, sum_spec],
        out_shape=[
            flat,
            flat,
            flat,
            jax.ShapeDtypeStruct((seqs, heads, 3, head_dim, 128), F32),
        ],
        scratch_shapes=[pltpu.VMEM((length, head_dim), F32)] * 2,
        cost_estimate=pl.CostEstimate(
            flops=10 * work * head_dim, bytes_accessed=proj_t.size * 6, transcendentals=work
        ),
        name="attend_backward",
    )(proj_t, proj_t, proj_t, cosine, sine, lse, ctx_grad_t)


def rotary_tables(length):
    half_rot = ROT // 2
    position = jnp.arange(length).astype(F32)
    inv_freq = jnp.exp(jnp.arange(half_rot).astype(F32) * (-2.0 * math.log(10000.0) / ROT))
    angles = inv_freq[:, None] * position[None, :]
    return jnp.cos(angles), jnp.sin(angles)


def body(
    dp, tensor, inputs, ln_gain, ln_bias, w_qkv, b_qkv, w_out, w_in, b_in, w_down, out_bias,
    cotangent,
):
    model = inputs.shape[-1]
    heads, head_dim = b_qkv.shape[1], b_qkv.shape[2] * dp
    width = heads * head_dim
    hidden_units = w_in.shape[1]
    seqs, length = inputs.shape[0], inputs.shape[1] * tensor
    rows = seqs * length
    own = ln_gain.shape[0]
    share = own * tensor
    slow = [1 << b for b in range(1, dp.bit_length() - 1)]
    ways = (slow + [1], slow[::-1] + [1])
    me_z = lax.axis_index("tensor")

    full_in = lax.all_gather(inputs, "tensor", axis=1, tiled=True).reshape(rows, model)
    full_cot = lax.all_gather(cotangent, "tensor", axis=1, tiled=True).reshape(rows, model)

    vector = jnp.stack([ln_gain, ln_bias, out_bias[0] + out_bias[1]])
    by_z = [vector]
    for k in range(1, tensor):
        by_z.append(
            lax.ppermute(vector, "tensor", [(i, (i + k) % tensor) for i in range(tensor)])
        )
    by_z = jnp.stack(by_z)
    order = (me_z - jnp.arange(tensor)) % tensor
    by_z = jnp.take(by_z, order, axis=0).transpose(1, 0, 2)
    small = jnp.concatenate(
        [by_z.reshape(-1), b_qkv.astype(F32).reshape(-1), b_in.astype(F32).reshape(-1)]
    )
    used = small.shape[0]
    padded = -(-used // 1024) * 1024
    small = jnp.pad(small, (0, padded - used)).reshape(-1, 128)
    small = gather_bits(small, dp, 0, ways[0]).reshape(dp, padded)
    norm_rows = small[:, : 3 * share].reshape(dp, 3, share).transpose(1, 0, 2).reshape(3, model)
    gain, shift, out_shift = norm_rows[0], norm_rows[1], norm_rows[2]
    at = 3 * share
    qkv_count = b_qkv.size
    qkv_bias = (
        small[:, at : at + qkv_count]
        .reshape(dp, 3, heads, head_dim // dp)
        .transpose(1, 2, 0, 3)
        .reshape(3 * width)
    )
    at += qkv_count
    in_groups, in_each = b_in.shape
    in_bias = (
        small[:, at : at + b_in.size]
        .reshape(dp, in_groups, in_each)
        .transpose(1, 0, 2)
        .reshape(hidden_units)
    )

    qkv_full = gather_bits(w_qkv.transpose(1, 0, 2), dp, 1, ways[1]).reshape(3, model, width)
    in_full = gather_bits(w_in, dp, 0, ways[0]).reshape(model, hidden_units)
    down_t = gather_bits(w_down.T, dp, 0, ways[1]).reshape(model, hidden_units)
    out_t = gather_bits(w_out.T, dp, 0, ways[0]).reshape(model, width)
    qkv_matrix = qkv_full.transpose(1, 0, 2).reshape(model, 3 * width)

    wide = full_in.astype(F32)
    centred = wide - jnp.mean(wide, axis=-1, keepdims=True)
    inv_sigma = lax.rsqrt(jnp.mean(centred * centred, axis=-1, keepdims=True) + EPS)
    unit_rows = centred * inv_sigma
    normed = (unit_rows * gain + shift).astype(BF16)
    proj_t = dot(qkv_matrix, normed, (0, 1)) + qkv_bias[:, None]
    cosine, sine = rotary_tables(length)
    ctx_t, lse = attend(proj_t, cosine, sine, seqs, heads, head_dim, length)
    pre_act = dot(normed, in_full, (1, 0)) + in_bias
    normal_cdf = 0.5 * (1.0 + lax.erf(pre_act * ROOT_HALF))
    normal_pdf = jnp.exp(-0.5 * pre_act * pre_act) * INV_ROOT_TAU
    hidden = (pre_act * normal_cdf).astype(BF16)
    slopes = normal_cdf + pre_act * normal_pdf
    branch = dot(ctx_t, out_t, (0, 1)) + dot(hidden, down_t, (1, 1))
    summed = lax.psum_scatter(
        branch.astype(BF16).reshape(seqs, length, model),
        "tensor",
        scatter_dimension=1,
        tiled=True,
    )
    outputs = (inputs.astype(F32) + summed.astype(F32) + out_shift).astype(BF16)

    pre_grad = dot(full_cot, down_t, (1, 0)) * slopes
    pre_low = pre_grad.astype(BF16)
    grad_in_bias = jnp.sum(pre_grad, axis=0)
    ctx_grad_t = dot(out_t, full_cot, (0, 1)).astype(BF16)
    dq_t, dk_t, dv_t, sums = attend_back(
        proj_t, cosine, sine, lse, ctx_grad_t, seqs, heads, head_dim, length
    )
    proj_low_t = jnp.concatenate([dq_t, dk_t, dv_t], axis=0)
    grad_qkv_bias = jnp.sum(sums[..., 0], axis=0).transpose(1, 0, 2)
    norm_grad = dot(proj_low_t, qkv_matrix, (0, 1)) + dot(pre_low, in_full, (1, 1))
    own_grad = lax.psum_scatter(
        norm_grad.astype(BF16).reshape(seqs, length, model),
        "tensor",
        scatter_dimension=1,
        tiled=True,
    ).astype(F32)
    gain_part = jnp.sum(norm_grad * unit_rows, axis=0)
    shift_part = jnp.sum(norm_grad, axis=0)
    bias_part = jnp.sum(full_cot.astype(F32), axis=0)

    grad_down_t = dot(full_cot, hidden, (0, 0))
    grad_in = dot(normed, pre_low, (0, 0))
    grad_out_t = dot(full_cot, ctx_t, (0, 1))
    grad_qkv = dot(normed, proj_low_t, (0, 1)).reshape(model, 3, width).transpose(1, 0, 2)

    back = ([1] + slow[::-1], [1] + slow)
    part = model // dp
    in_out = scatter_bits(grad_in.reshape(dp, part, hidden_units), dp, 0, back[0], BF16)
    down_out = scatter_bits(grad_down_t.reshape(dp, part, hidden_units), dp, 0, back[1], BF16).T
    out_out = scatter_bits(grad_out_t.reshape(dp, part, width), dp, 0, back[0], BF16).T
    qkv_out = scatter_bits(grad_qkv.reshape(3, dp, part, width), dp, 1, back[1], BF16)
    qkv_out = qkv_out.transpose(1, 0, 2)

    small = jnp.concatenate(
        [
            jnp.stack([gain_part, shift_part, bias_part])
            .reshape(3, dp, share)
            .transpose(1, 0, 2)
            .reshape(dp, -1),
            grad_qkv_bias.reshape(3, heads, dp, head_dim // dp)
            .transpose(2, 0, 1, 3)
            .reshape(dp, -1),
            grad_in_bias.reshape(in_groups, dp, in_each).transpose(1, 0, 2).reshape(dp, -1),
        ],
        axis=1,
    )
    small = jnp.pad(small, ((0, 0), (0, padded - used))).reshape(dp, -1, 128)
    small = scatter_bits(small, dp, 0, back[0], F32).reshape(-1)
    vector = small[: 3 * share].reshape(3, tensor, own)
    mine = lax.dynamic_index_in_dim(vector, me_z, 1, keepdims=False)
    pair = mine[:2]
    for k in range(1, tensor):
        piece = lax.dynamic_index_in_dim(vector[:2], (me_z + k) % tensor, 1, keepdims=False)
        pair = pair + lax.ppermute(
            piece, "tensor", [(i, (i + k) % tensor) for i in range(tensor)]
        )
    bias_grad = jnp.stack([mine[2], mine[2]])
    at = 3 * share
    qkv_bias_out = small[at : at + qkv_count].reshape(b_qkv.shape)
    at += qkv_count
    in_bias_out = small[at : at + b_in.size].reshape(b_in.shape)

    local = inputs.astype(F32)
    local = local - jnp.mean(local, axis=-1, keepdims=True)
    local_inv = lax.rsqrt(jnp.mean(local * local, axis=-1, keepdims=True) + EPS)
    local = local * local_inv
    unit_grad = own_grad * gain
    input_grad = cotangent.astype(F32) + local_inv * (
        unit_grad
        - jnp.mean(unit_grad, axis=-1, keepdims=True)
        - local * jnp.mean(unit_grad * local, axis=-1, keepdims=True)
    )
    return (
        outputs,
        input_grad.astype(BF16),
        pair[0],
        pair[1],
        qkv_out,
        qkv_bias_out,
        out_out,
        in_out,
        in_bias_out,
        down_out,
        bias_grad,
    )


def solution(mesh):
    tokens = P("dp", "tensor", None)
    vector = P(("dp", "tensor"))
    qkv, qkv_bias = P("dp", None, "tensor"), P(None, "tensor", "dp")
    by_out, by_in, pair = P("tensor", "dp"), P("dp", "tensor"), P(None, ("dp", "tensor"))
    return jax.shard_map(
        functools.partial(body, mesh.shape["dp"], mesh.shape["tensor"]),
        mesh=mesh,
        in_specs=(
            tokens, vector, vector, qkv, qkv_bias, by_out, by_in, by_out, by_out, pair, tokens,
        ),
        out_specs=(
            tokens, tokens, vector, vector, qkv, qkv_bias, by_out, by_in, by_out, by_out, pair,
        ),
        check_vma=False,
    )
```

```python
import functools
import math

import jax
import jax.numpy as jnp
from jax import lax
from jax.experimental import pallas as pl
from jax.experimental.pallas import tpu as pltpu
from jax.sharding import PartitionSpec as P

ROT = 16
EPS = 1e-05
ROOT_HALF = 0.7071067811865476
INV_ROOT_TAU = 0.3989422804014327
NEG_BIG = -1e30
F32 = jnp.float32
BF16 = jnp.bfloat16


def dot(a, b, contract, out=F32):
    return lax.dot_general(
        a, b, (((contract[0],), (contract[1],)), ((), ())), preferred_element_type=out
    )


def swap(x, axis_name, size, step):
    return lax.ppermute(x, axis_name, [(i, i ^ step) for i in range(size)])


def bit_of(axis_name, step):
    return (lax.axis_index(axis_name) // step) % 2


def gather_bits(x, size, axis, steps):
    done = []
    for step in steps:
        other = swap(x, "dp", size, step)
        mine_first = bit_of("dp", step) == 0
        low = jnp.where(mine_first, x, other)
        high = jnp.where(mine_first, other, x)
        place = axis + sum(1 for s in done if s > step)
        x = jnp.stack([low, high], axis=place)
        done.append(step)
    shape = x.shape
    levels = len(steps)
    return x.reshape(shape[:axis] + (size,) + shape[axis + levels :])


def scatter_bits(x, axis, steps, wire, size, unit):
    shape = x.shape
    levels = len(steps)
    x = x.reshape(shape[:axis] + (2,) * levels + shape[axis + 1 :])
    left = sorted(steps, reverse=True)
    for step in steps:
        place = axis + left.index(step)
        bit = bit_of("dp", step * unit)
        keep = lax.dynamic_index_in_dim(x, bit, place, keepdims=False)
        send = lax.dynamic_index_in_dim(x, 1 - bit, place, keepdims=False)
        got = swap(send.astype(wire), "dp", size, step * unit)
        x = keep + got.astype(F32)
        left.remove(step)
    return x


def rotate_rows(x, cosine, sine):
    half = ROT // 2
    first, second = x[:half], x[half:ROT]
    return jnp.concatenate(
        [first * cosine - second * sine, second * cosine + first * sine, x[ROT:]], axis=0
    )


def normalize(x):
    wide = x.astype(F32)
    centred = wide - jnp.mean(wide, axis=-1, keepdims=True)
    inv_sigma = lax.rsqrt(jnp.mean(centred * centred, axis=-1, keepdims=True) + EPS)
    return centred * inv_sigma, inv_sigma


def enter_kernel(
    heads, head_dim, x_ref, vec_ref, in_bias_ref, qkv_bias_ref, first_ref, second_ref,
    cos_ref, sin_ref, normed_t_ref, proj_t_ref, hidden_ref, slope_ref,
):
    width = heads * head_dim
    hidden_units = hidden_ref.shape[1]
    unit, _ = normalize(x_ref[...])
    wide = unit * vec_ref[0:1] + vec_ref[1:2]
    normed = wide.astype(BF16)
    normed_t_ref[...] = jnp.transpose(normed)
    projected = dot(normed, second_ref[:, hidden_units:], (1, 0)) + qkv_bias_ref[...]
    projected = jnp.transpose(projected)
    cosine, sine = cos_ref[...], sin_ref[...]
    for place in range(2 * heads):
        rows = slice(place * head_dim, (place + 1) * head_dim)
        proj_t_ref[rows] = rotate_rows(projected[rows], cosine, sine).astype(BF16)
    proj_t_ref[2 * width :] = projected[2 * width :].astype(BF16)
    pre_act = dot(normed, first_ref[:, :hidden_units], (1, 0)) + in_bias_ref[...]
    normal_cdf = 0.5 * (1.0 + lax.erf(pre_act * ROOT_HALF))
    normal_pdf = jnp.exp(-0.5 * pre_act * pre_act) * INV_ROOT_TAU
    hidden_ref[...] = (pre_act * normal_cdf).astype(BF16)
    slope_ref[...] = normal_cdf + pre_act * normal_pdf


def causal(block):
    key_pos = lax.broadcasted_iota(jnp.int32, (block, block), 0)
    query_pos = lax.broadcasted_iota(jnp.int32, (block, block), 1)
    return key_pos <= query_pos


def forward_kernel(scale, block, q_ref, k_ref, v_ref, ctx_ref, lse_ref):
    length = q_ref.shape[1]
    queries = q_ref[...] * jnp.asarray(scale, BF16)
    keys = jnp.transpose(k_ref[...])
    values = v_ref[...]
    allowed = causal(block)
    for step in range(length // block):
        here = slice(step * block, (step + 1) * block)
        q_cols = queries[:, here]
        near = jnp.where(allowed, dot(keys[here], q_cols, (1, 0)), NEG_BIG)
        top = jnp.max(near, axis=0, keepdims=True)
        if step:
            far = dot(keys[: step * block], q_cols, (1, 0))
            top = jnp.maximum(top, jnp.max(far, axis=0, keepdims=True))
        near = jnp.exp(near - top)
        total = jnp.sum(near, axis=0, keepdims=True)
        context = dot(values[:, here], near.astype(BF16), (1, 0))
        if step:
            far = jnp.exp(far - top)
            total = total + jnp.sum(far, axis=0, keepdims=True)
            context = context + dot(values[:, : step * block], far.astype(BF16), (1, 0))
        ctx_ref[:, here] = (context / total).astype(BF16)
        lse_ref[0, :, here] = jnp.broadcast_to(top + jnp.log(total), (8, block))


def backward_kernel(
    scale, block, q_ref, k_ref, v_ref, cos_ref, sin_ref, lse_ref, grad_ref,
    dq_ref, dk_ref, dv_ref, sum_ref, keys_acc, values_acc,
):
    length = q_ref.shape[1]
    cosine, sine = cos_ref[...], sin_ref[...]
    queries = q_ref[...] * jnp.asarray(scale, BF16)
    query_rows = jnp.transpose(q_ref[...])
    keys_t = k_ref[...]
    keys = jnp.transpose(keys_t)
    values = jnp.transpose(v_ref[...])
    grad_t = grad_ref[...]
    grad_rows = jnp.transpose(grad_t)
    allowed = causal(block)
    keys_acc[...] = jnp.zeros_like(keys_acc)
    values_acc[...] = jnp.zeros_like(values_acc)
    query_sum = 0.0
    for step in range(length // block):
        here = slice(step * block, (step + 1) * block)
        upto = slice(0, (step + 1) * block)
        lse = lse_ref[0, 0:1, here]
        scores = dot(keys[upto], queries[:, here], (1, 0))
        probs = jnp.exp(scores - lse)
        low = jnp.where(allowed, probs[step * block :], 0.0)
        probs = jnp.concatenate([probs[: step * block], low], axis=0) if step else low
        values_acc[upto, :] += dot(probs.astype(BF16), grad_rows[here], (1, 0))
        prob_grad = dot(values[upto], grad_t[:, here], (1, 0))
        row_dot = jnp.sum(probs * prob_grad, axis=0, keepdims=True)
        score_grad = (probs * (prob_grad - row_dot) * scale).astype(BF16)
        keys_acc[upto, :] += dot(score_grad, query_rows[here], (1, 0))
        dq = dot(keys_t[:, upto], score_grad, (1, 0))
        dq = rotate_rows(dq, cosine[:, here], -sine[:, here])
        dq_ref[:, here] = dq.astype(BF16)
        query_sum = query_sum + jnp.sum(dq, axis=1, keepdims=True)
    dk = rotate_rows(jnp.transpose(keys_acc[...]), cosine, -sine)
    dv = jnp.transpose(values_acc[...])
    dk_ref[...] = dk.astype(BF16)
    dv_ref[...] = dv.astype(BF16)
    sums = [query_sum, jnp.sum(dk, axis=1, keepdims=True), jnp.sum(dv, axis=1, keepdims=True)]
    for place, part in enumerate(sums):
        sum_ref[0, 0, place] = jnp.broadcast_to(part, (part.shape[0], 128))


def branch_kernel(ctx_t_ref, hidden_ref, first_ref, second_ref, branch_ref, ctx_ref):
    hidden_units = hidden_ref.shape[1]
    context = jnp.transpose(ctx_t_ref[...])
    ctx_ref[...] = context
    total = dot(context, first_ref[:, hidden_units:], (1, 1))
    total = total + dot(hidden_ref[...], second_ref[:, :hidden_units], (1, 1))
    branch_ref[...] = total.astype(BF16)


def row_sums(x):
    return jnp.sum(x.reshape(x.shape[0] // 8, 8, x.shape[1]), axis=0)


def return_kernel(
    after_ref, cot_ref, slope_ref, first_ref, second_ref,
    cot_t_ref, ctx_grad_t_ref, pre_low_ref, in_sum_ref, cot_sum_ref,
):
    hidden_units = slope_ref.shape[1]
    cot = cot_ref[...]
    cot_t_ref[...] = jnp.transpose(cot)
    ctx_grad = dot(cot, first_ref[:, hidden_units:], (1, 0))
    ctx_grad_t_ref[...] = jnp.transpose(ctx_grad).astype(BF16)
    pre_grad = dot(cot, second_ref[:, :hidden_units], (1, 0)) * slope_ref[...]
    pre_low_ref[...] = pre_grad.astype(BF16)

    @pl.when(pl.program_id(0) == 0)
    def _():
        in_sum_ref[...] = jnp.zeros_like(in_sum_ref)
        cot_sum_ref[...] = jnp.zeros_like(cot_sum_ref)

    in_sum_ref[...] += row_sums(pre_grad)
    cot_sum_ref[...] += row_sums(cot.astype(F32))


def norm_kernel(
    x_ref, dq_ref, dk_ref, dv_ref, pre_low_ref, first_ref, second_ref,
    proj_low_ref, norm_grad_ref, gain_sum_ref, shift_sum_ref,
):
    hidden_units = pre_low_ref.shape[1]
    proj_low = jnp.transpose(
        jnp.concatenate([dq_ref[...], dk_ref[...], dv_ref[...]], axis=0)
    )
    proj_low_ref[...] = proj_low
    norm_grad = dot(proj_low, second_ref[:, hidden_units:], (1, 1))
    norm_grad = norm_grad + dot(pre_low_ref[...], first_ref[:, :hidden_units], (1, 1))
    norm_grad_ref[...] = norm_grad.astype(BF16)
    unit, _ = normalize(x_ref[...])

    @pl.when(pl.program_id(0) == 0)
    def _():
        gain_sum_ref[...] = jnp.zeros_like(gain_sum_ref)
        shift_sum_ref[...] = jnp.zeros_like(shift_sum_ref)

    gain_sum_ref[...] += row_sums(norm_grad * unit)
    shift_sum_ref[...] += row_sums(norm_grad)


def weight_kernel(
    bit_ref, normed_t_ref, cot_t_ref, pre_low_ref, ctx_ref, hidden_ref, proj_low_ref,
    first_ref, second_ref,
):
    blocks, part, _ = first_ref.shape
    hidden_units = hidden_ref.shape[1]
    starts = [pl.multiple_of((2 * j + bit_ref[0]) * part, part) for j in range(blocks)]

    def rows(ref):
        return jnp.concatenate([ref[pl.ds(start, part), :] for start in starts], axis=0)

    def put(ref, columns, value):
        ref[:, :, columns] = value.reshape(blocks, part, -1).astype(ref.dtype)

    left = rows(normed_t_ref)
    put(first_ref, slice(0, hidden_units), dot(left, pre_low_ref[...], (1, 0)))
    put(second_ref, slice(hidden_units, None), dot(left, proj_low_ref[...], (1, 0)))
    left = rows(cot_t_ref)
    put(first_ref, slice(hidden_units, None), dot(left, ctx_ref[...], (1, 0)))
    put(second_ref, slice(0, hidden_units), dot(left, hidden_ref[...], (1, 0)))


def whole(x):
    return pl.BlockSpec(x.shape, lambda *_: (0,) * x.ndim)


def tokens(block, columns):
    return pl.BlockSpec((block, columns), lambda t: (t, 0))


def tokens_t(rows, block):
    return pl.BlockSpec((rows, block), lambda t: (0, t))


def cost(flops, nbytes, trans=0):
    return pl.CostEstimate(flops=flops, bytes_accessed=nbytes, transcendentals=trans)


def struct(*shape, dtype=BF16):
    return jax.ShapeDtypeStruct(shape, dtype)


def enter(x, vectors, in_bias, qkv_bias, first, second, cosine, sine, heads, head_dim):
    rows, model = x.shape
    hidden_units = in_bias.shape[1]
    proj = 3 * heads * head_dim
    block = min(256, rows)
    per_seq = cosine.shape[1] // block
    table = pl.BlockSpec((ROT // 2, block), lambda t: (0, lax.rem(t, per_seq)))
    return pl.pallas_call(
        functools.partial(enter_kernel, heads, head_dim),
        grid=(rows // block,),
        in_specs=[
            tokens(block, model), whole(vectors), whole(in_bias), whole(qkv_bias),
            whole(first), whole(second), table, table,
        ],
        out_specs=[
            tokens_t(model, block), tokens_t(proj, block),
            tokens(block, hidden_units), tokens(block, hidden_units),
        ],
        out_shape=[
            struct(model, rows), struct(proj, rows),
            struct(rows, hidden_units), struct(rows, hidden_units, dtype=F32),
        ],
        cost_estimate=cost(
            2 * rows * model * (proj + hidden_units), 2 * (first.size + second.size) + 12 * x.size,
            2 * rows * hidden_units,
        ),
        name="enter",
    )(x, vectors, in_bias, qkv_bias, first, second, cosine, sine)


def attend(proj_t, seqs, heads, head_dim, length):
    block = min(256, length)
    scale = 1.0 / math.sqrt(head_dim)

    def part(which):
        return pl.BlockSpec((head_dim, length), lambda s, h: (which * heads + h, s))

    lse_spec = pl.BlockSpec((1, 8, length), lambda s, h: (h, 0, s))
    work = seqs * heads * length * length
    return pl.pallas_call(
        functools.partial(forward_kernel, scale, block),
        grid=(seqs, heads),
        in_specs=[part(0), part(1), part(2)],
        out_specs=[part(0), lse_spec],
        out_shape=[
            struct(heads * head_dim, seqs * length),
            struct(heads, 8, seqs * length, dtype=F32),
        ],
        cost_estimate=cost(4 * work * head_dim, proj_t.size * 4, work),
        name="attend_forward",
    )(proj_t, proj_t, proj_t)


def attend_back(proj_t, cosine, sine, lse, ctx_grad_t, seqs, heads, head_dim, length):
    block = min(256, length)
    scale = 1.0 / math.sqrt(head_dim)

    def part(which):
        return pl.BlockSpec((head_dim, length), lambda s, h: (which * heads + h, s))

    table = pl.BlockSpec((ROT // 2, length), lambda s, h: (0, 0))
    lse_spec = pl.BlockSpec((1, 8, length), lambda s, h: (h, 0, s))
    sum_spec = pl.BlockSpec((1, 1, 3, head_dim, 128), lambda s, h: (s, h, 0, 0, 0))
    flat = struct(heads * head_dim, seqs * length)
    work = seqs * heads * length * length
    return pl.pallas_call(
        functools.partial(backward_kernel, scale, block),
        grid=(seqs, heads),
        in_specs=[part(0), part(1), part(2), table, table, lse_spec, part(0)],
        out_specs=[part(0), part(0), part(0), sum_spec],
        out_shape=[flat, flat, flat, struct(seqs, heads, 3, head_dim, 128, dtype=F32)],
        scratch_shapes=[pltpu.VMEM((length, head_dim), F32)] * 2,
        cost_estimate=cost(10 * work * head_dim, proj_t.size * 6, work),
        name="attend_backward",
    )(proj_t, proj_t, proj_t, cosine, sine, lse, ctx_grad_t)


def branch_sum(ctx_t, hidden, first, second):
    width, rows = ctx_t.shape
    hidden_units = hidden.shape[1]
    model = first.shape[0]
    block = min(256, rows)
    return pl.pallas_call(
        branch_kernel,
        grid=(rows // block,),
        in_specs=[
            tokens_t(width, block), tokens(block, hidden_units), whole(first), whole(second),
        ],
        out_specs=[tokens(block, model), tokens(block, width)],
        out_shape=[struct(rows, model), struct(rows, width)],
        cost_estimate=cost(2 * rows * model * (width + hidden_units), 8 * rows * model),
        name="branch",
    )(ctx_t, hidden, first, second)


def return_grads(after, cot, slopes, first, second, width):
    rows, model = cot.shape
    hidden_units = slopes.shape[1]
    block = min(256, rows)
    return pl.pallas_call(
        return_kernel,
        grid=(rows // block,),
        in_specs=[
            pl.BlockSpec(memory_space=pl.ANY), tokens(block, model), tokens(block, hidden_units), whole(first), whole(second),
        ],
        out_specs=[
            tokens_t(model, block), tokens_t(width, block), tokens(block, hidden_units),
            pl.BlockSpec((8, hidden_units), lambda t: (0, 0)),
            pl.BlockSpec((8, model), lambda t: (0, 0)),
        ],
        out_shape=[
            struct(model, rows), struct(width, rows), struct(rows, hidden_units),
            struct(8, hidden_units, dtype=F32), struct(8, model, dtype=F32),
        ],
        cost_estimate=cost(2 * rows * model * (width + hidden_units), 10 * rows * model),
        name="return_grads",
    )(after, cot, slopes, first, second)


def norm_sum(x, dq_t, dk_t, dv_t, pre_low, first, second):
    rows, model = x.shape
    width = dq_t.shape[0]
    hidden_units = pre_low.shape[1]
    block = min(256, rows)
    return pl.pallas_call(
        norm_kernel,
        grid=(rows // block,),
        in_specs=[
            tokens(block, model), tokens_t(width, block), tokens_t(width, block),
            tokens_t(width, block), tokens(block, hidden_units), whole(first), whole(second),
        ],
        out_specs=[
            tokens(block, 3 * width), tokens(block, model),
            pl.BlockSpec((8, model), lambda t: (0, 0)),
            pl.BlockSpec((8, model), lambda t: (0, 0)),
        ],
        out_shape=[
            struct(rows, 3 * width), struct(rows, model),
            struct(8, model, dtype=F32), struct(8, model, dtype=F32),
        ],
        cost_estimate=cost(2 * rows * model * (3 * width + hidden_units), 8 * rows * model),
        name="norm_grads",
    )(x, dq_t, dk_t, dv_t, pre_low, first, second)


def weight_half(bit, normed_t, cot_t, pre_low, ctx, hidden, proj_low, dp, dtype):
    model, rows = normed_t.shape
    operands = (normed_t, cot_t, pre_low, ctx, hidden, proj_low)
    columns = (hidden.shape[1] + ctx.shape[1], hidden.shape[1] + proj_low.shape[1])
    shapes = [struct(dp // 2, model // dp, c, dtype=dtype) for c in columns]
    return pl.pallas_call(
        weight_kernel,
        grid_spec=pltpu.PrefetchScalarGridSpec(
            num_scalar_prefetch=1,
            grid=(1,),
            in_specs=[whole(x) for x in operands],
            out_specs=[whole(x) for x in shapes],
        ),
        out_shape=shapes,
        cost_estimate=cost(rows * model * sum(columns), 8 * rows * model),
        name="weight_grads",
    )(bit.reshape(1).astype(jnp.int32), *operands)


def rotary_tables(length):
    half_rot = ROT // 2
    position = jnp.arange(length).astype(F32)
    inv_freq = jnp.exp(jnp.arange(half_rot).astype(F32) * (-2.0 * math.log(10000.0) / ROT))
    angles = inv_freq[:, None] * position[None, :]
    return jnp.cos(angles), jnp.sin(angles)


def body(
    dp, tensor, inputs, ln_gain, ln_bias, w_qkv, b_qkv, w_out, w_in, b_in, w_down, out_bias,
    cotangent,
):
    model = inputs.shape[-1]
    heads, head_dim = b_qkv.shape[1], b_qkv.shape[2] * dp
    width = heads * head_dim
    hidden_units = w_in.shape[1]
    seqs, length = inputs.shape[0], inputs.shape[1] * tensor
    rows = seqs * length
    own = ln_gain.shape[0]
    share = own * tensor
    slow = [1 << b for b in range(1, dp.bit_length() - 1)]
    ways = (slow + [1], slow[::-1] + [1])
    me_z = lax.axis_index("tensor")

    full_in = lax.all_gather(inputs, "tensor", axis=1, tiled=True).reshape(rows, model)
    full_cot = lax.all_gather(cotangent, "tensor", axis=1, tiled=True).reshape(rows, model)

    vector = jnp.stack([ln_gain, ln_bias, out_bias[0] + out_bias[1]])
    by_z = [vector]
    for k in range(1, tensor):
        by_z.append(
            lax.ppermute(vector, "tensor", [(i, (i + k) % tensor) for i in range(tensor)])
        )
    by_z = jnp.stack(by_z)
    order = (me_z - jnp.arange(tensor)) % tensor
    by_z = jnp.take(by_z, order, axis=0).transpose(1, 0, 2)
    small = jnp.concatenate(
        [by_z.reshape(-1), b_qkv.astype(F32).reshape(-1), b_in.astype(F32).reshape(-1)]
    )
    used = small.shape[0]
    padded = -(-used // 1024) * 1024
    small = jnp.pad(small, (0, padded - used)).reshape(-1, 128)
    small = gather_bits(small, dp, 0, ways[0]).reshape(dp, padded)
    norm_rows = small[:, : 3 * share].reshape(dp, 3, share).transpose(1, 0, 2).reshape(3, model)
    gain, out_shift = norm_rows[0], norm_rows[2]
    at = 3 * share
    qkv_count = b_qkv.size
    qkv_bias = (
        small[:, at : at + qkv_count]
        .reshape(dp, 3, heads, head_dim // dp)
        .transpose(1, 2, 0, 3)
        .reshape(3 * width)
    )
    at += qkv_count
    in_groups, in_each = b_in.shape
    in_bias = (
        small[:, at : at + b_in.size]
        .reshape(dp, in_groups, in_each)
        .transpose(1, 0, 2)
        .reshape(hidden_units)
    )

    first = gather_bits(jnp.concatenate([w_in, w_out.T], axis=1), dp, 0, ways[0])
    second = gather_bits(
        jnp.concatenate([w_down.T, w_qkv.reshape(w_qkv.shape[0], -1)], axis=1), dp, 0, ways[1]
    )
    first = first.reshape(model, -1)
    second = second.reshape(model, -1)

    cosine, sine = rotary_tables(length)
    normed_t, proj_t, hidden, slopes = enter(
        full_in, norm_rows, in_bias.reshape(1, -1), qkv_bias.reshape(1, -1), first, second,
        cosine, sine, heads, head_dim,
    )
    ctx_t, lse = attend(proj_t, seqs, heads, head_dim, length)
    branch, context = branch_sum(ctx_t, hidden, first, second)
    summed = lax.psum_scatter(
        branch.reshape(seqs, length, model), "tensor", scatter_dimension=1, tiled=True
    )
    outputs = (inputs.astype(F32) + summed.astype(F32) + out_shift).astype(BF16)

    cot_t, ctx_grad_t, pre_low, in_sum, cot_sum = return_grads(
        context, full_cot, slopes, first, second, width
    )
    dq_t, dk_t, dv_t, sums = attend_back(
        proj_t, cosine, sine, lse, ctx_grad_t, seqs, heads, head_dim, length
    )
    proj_low, norm_grad, gain_sum, shift_sum = norm_sum(
        full_in, dq_t, dk_t, dv_t, pre_low, first, second
    )
    own_grad = lax.psum_scatter(
        norm_grad.reshape(seqs, length, model), "tensor", scatter_dimension=1, tiled=True
    ).astype(F32)
    grad_qkv_bias = jnp.sum(sums[..., 0], axis=0).transpose(1, 0, 2)
    grad_in_bias = jnp.sum(in_sum, axis=0)
    gain_part, shift_part, bias_part = (
        jnp.sum(gain_sum, axis=0), jnp.sum(shift_sum, axis=0), jnp.sum(cot_sum, axis=0),
    )

    part = model // dp
    back = (slow[::-1], slow)
    core = bit_of("dp", 1)
    if dp > 1 and part % 16 == 0:
        halves = (normed_t, cot_t, pre_low, context, hidden, proj_low, dp)
        sent = weight_half(1 - core, *halves, BF16)
        got = [swap(x, "dp", dp, 1) for x in sent]
        kept = weight_half(core, *halves, F32)
    else:
        grads = (
            jnp.concatenate([dot(normed_t, pre_low, (1, 0)), dot(cot_t, context, (1, 0))], 1),
            jnp.concatenate([dot(cot_t, hidden, (1, 0)), dot(normed_t, proj_low, (1, 0))], 1),
        )
        grads = [g.reshape(dp // 2, 2, part, -1) for g in grads]
        kept = [lax.dynamic_index_in_dim(g, core, 1, keepdims=False) for g in grads]
        sent = [lax.dynamic_index_in_dim(g, 1 - core, 1, keepdims=False) for g in grads]
        got = [swap(x.astype(BF16), "dp", dp, 1) for x in sent]
    first_grad, second_grad = (
        scatter_bits(k + g.astype(F32), 0, [s // 2 for s in way], BF16, dp, 2)
        for k, g, way in zip(kept, got, back)
    )
    in_out, out_out = first_grad[:, :hidden_units], first_grad[:, hidden_units:].T
    down_out = second_grad[:, :hidden_units].T
    qkv_out = second_grad[:, hidden_units:].reshape(part, 3, width)

    small = jnp.concatenate(
        [
            jnp.stack([gain_part, shift_part, bias_part])
            .reshape(3, dp, share)
            .transpose(1, 0, 2)
            .reshape(dp, -1),
            grad_qkv_bias.reshape(3, heads, dp, head_dim // dp)
            .transpose(2, 0, 1, 3)
            .reshape(dp, -1),
            grad_in_bias.reshape(in_groups, dp, in_each).transpose(1, 0, 2).reshape(dp, -1),
        ],
        axis=1,
    )
    small = jnp.pad(small, ((0, 0), (0, padded - used))).reshape(dp, -1, 128)
    small = scatter_bits(small, 0, [1] + slow, F32, dp, 1).reshape(-1)
    vector = small[: 3 * share].reshape(3, tensor, own)
    mine = lax.dynamic_index_in_dim(vector, me_z, 1, keepdims=False)
    pair = mine[:2]
    for k in range(1, tensor):
        piece = lax.dynamic_index_in_dim(vector[:2], (me_z + k) % tensor, 1, keepdims=False)
        pair = pair + lax.ppermute(
            piece, "tensor", [(i, (i + k) % tensor) for i in range(tensor)]
        )
    bias_grad = jnp.stack([mine[2], mine[2]])
    at = 3 * share
    qkv_bias_out = small[at : at + qkv_count].reshape(b_qkv.shape)
    at += qkv_count
    in_bias_out = small[at : at + b_in.size].reshape(b_in.shape)

    local = inputs.astype(F32)
    local = local - jnp.mean(local, axis=-1, keepdims=True)
    local_inv = lax.rsqrt(jnp.mean(local * local, axis=-1, keepdims=True) + EPS)
    local = local * local_inv
    unit_grad = own_grad * gain
    input_grad = cotangent.astype(F32) + local_inv * (
        unit_grad
        - jnp.mean(unit_grad, axis=-1, keepdims=True)
        - local * jnp.mean(unit_grad * local, axis=-1, keepdims=True)
    )
    return (
        outputs,
        input_grad.astype(BF16),
        pair[0],
        pair[1],
        qkv_out,
        qkv_bias_out,
        out_out,
        in_out,
        in_bias_out,
        down_out,
        bias_grad,
    )


def solution(mesh):
    spread = P("dp", "tensor", None)
    vector = P(("dp", "tensor"))
    qkv, qkv_bias = P("dp", None, "tensor"), P(None, "tensor", "dp")
    by_out, by_in, pair = P("tensor", "dp"), P("dp", "tensor"), P(None, ("dp", "tensor"))

    def layer(*arrays):
        return body(mesh.shape["dp"], mesh.shape["tensor"], *arrays)

    return jax.shard_map(
        layer,
        mesh=mesh,
        in_specs=(
            spread, vector, vector, qkv, qkv_bias, by_out, by_in, by_out, by_out, pair, spread,
        ),
        out_specs=(
            spread, spread, vector, vector, qkv, qkv_bias, by_out, by_in, by_out, by_out, pair,
        ),
        check_vma=False,
    )
```

```python
import functools
import math

import jax
import jax.numpy as jnp
from jax import lax
from jax.experimental import pallas as pl
from jax.experimental.pallas import tpu as pltpu
from jax.sharding import PartitionSpec as P

ROT = 16
EPS = 1e-05
ROOT_HALF = 0.7071067811865476
INV_ROOT_TAU = 0.3989422804014327
NEG_BIG = -1e30
SMALL_ROWS = 16
F32 = jnp.float32
BF16 = jnp.bfloat16


def dot(a, b, contract, out=F32):
    return lax.dot_general(
        a, b, (((contract[0],), (contract[1],)), ((), ())), preferred_element_type=out
    )


def swap(x, axis_name, size, step):
    return lax.ppermute(x, axis_name, [(i, i ^ step) for i in range(size)])


def bit_of(axis_name, step):
    return (lax.axis_index(axis_name) // step) % 2


def gather_bits(x, size, axis, steps):
    done = []
    for step in steps:
        other = swap(x, "dp", size, step)
        mine_first = bit_of("dp", step) == 0
        low = jnp.where(mine_first, x, other)
        high = jnp.where(mine_first, other, x)
        place = axis + sum(1 for s in done if s > step)
        x = jnp.stack([low, high], axis=place)
        done.append(step)
    shape = x.shape
    levels = len(steps)
    return x.reshape(shape[:axis] + (size,) + shape[axis + levels :])


def scatter_bits(x, axis, steps, wire, size, unit):
    shape = x.shape
    levels = len(steps)
    x = x.reshape(shape[:axis] + (2,) * levels + shape[axis + 1 :])
    left = sorted(steps, reverse=True)
    for step in steps:
        place = axis + left.index(step)
        bit = bit_of("dp", step * unit)
        keep = lax.dynamic_index_in_dim(x, bit, place, keepdims=False)
        send = lax.dynamic_index_in_dim(x, 1 - bit, place, keepdims=False)
        got = swap(send.astype(wire), "dp", size, step * unit)
        x = keep + got.astype(F32)
        left.remove(step)
    return x


def rotate_rows(x, cosine, sine):
    half = ROT // 2
    first, second = x[:half], x[half:ROT]
    return jnp.concatenate(
        [first * cosine - second * sine, second * cosine + first * sine, x[ROT:]], axis=0
    )


def normalize(x):
    wide = x.astype(F32)
    centred = wide - jnp.mean(wide, axis=-1, keepdims=True)
    inv_sigma = lax.rsqrt(jnp.mean(centred * centred, axis=-1, keepdims=True) + EPS)
    return centred * inv_sigma, inv_sigma


def enter_kernel(
    heads, head_dim, x_ref, vec_ref, in_bias_ref, qkv_bias_ref, first_ref, second_ref,
    cos_ref, sin_ref, normed_t_ref, proj_t_ref, hidden_ref, slope_ref,
):
    width = heads * head_dim
    hidden_units = hidden_ref.shape[1]
    unit, _ = normalize(x_ref[...])
    wide = unit * vec_ref[0:1] + vec_ref[1:2]
    normed = wide.astype(BF16)
    normed_t_ref[...] = jnp.transpose(normed)
    projected = dot(normed, second_ref[:, hidden_units:], (1, 0)) + qkv_bias_ref[...]
    projected = jnp.transpose(projected)
    cosine, sine = cos_ref[...], sin_ref[...]
    for place in range(2 * heads):
        rows = slice(place * head_dim, (place + 1) * head_dim)
        proj_t_ref[rows] = rotate_rows(projected[rows], cosine, sine).astype(BF16)
    proj_t_ref[2 * width :] = projected[2 * width :].astype(BF16)
    pre_act = dot(normed, first_ref[:, :hidden_units], (1, 0)) + in_bias_ref[...]
    normal_cdf = 0.5 * (1.0 + lax.erf(pre_act * ROOT_HALF))
    normal_pdf = jnp.exp(-0.5 * pre_act * pre_act) * INV_ROOT_TAU
    hidden_ref[...] = (pre_act * normal_cdf).astype(BF16)
    slope_ref[...] = normal_cdf + pre_act * normal_pdf


def causal(block):
    key_pos = lax.broadcasted_iota(jnp.int32, (block, block), 0)
    query_pos = lax.broadcasted_iota(jnp.int32, (block, block), 1)
    return key_pos <= query_pos


def forward_kernel(scale, block, q_ref, k_ref, v_ref, ctx_ref, lse_ref):
    length = q_ref.shape[1]
    queries = q_ref[...] * jnp.asarray(scale, BF16)
    keys = jnp.transpose(k_ref[...])
    values = v_ref[...]
    allowed = causal(block)
    for step in range(length // block):
        here = slice(step * block, (step + 1) * block)
        q_cols = queries[:, here]
        near = jnp.where(allowed, dot(keys[here], q_cols, (1, 0)), NEG_BIG)
        top = jnp.max(near, axis=0, keepdims=True)
        if step:
            far = dot(keys[: step * block], q_cols, (1, 0))
            top = jnp.maximum(top, jnp.max(far, axis=0, keepdims=True))
        near = jnp.exp(near - top)
        total = jnp.sum(near, axis=0, keepdims=True)
        context = dot(values[:, here], near.astype(BF16), (1, 0))
        if step:
            far = jnp.exp(far - top)
            total = total + jnp.sum(far, axis=0, keepdims=True)
            context = context + dot(values[:, : step * block], far.astype(BF16), (1, 0))
        ctx_ref[:, here] = (context / total).astype(BF16)
        lse_ref[0, :, here] = jnp.broadcast_to(top + jnp.log(total), (8, block))


def backward_kernel(
    scale, block, q_ref, k_ref, v_ref, cos_ref, sin_ref, lse_ref, grad_ref,
    dq_ref, dk_ref, dv_ref, sum_ref, keys_acc, values_acc,
):
    length = q_ref.shape[1]
    cosine, sine = cos_ref[...], sin_ref[...]
    queries = q_ref[...] * jnp.asarray(scale, BF16)
    query_rows = jnp.transpose(q_ref[...])
    keys_t = k_ref[...]
    keys = jnp.transpose(keys_t)
    values = jnp.transpose(v_ref[...])
    grad_t = grad_ref[...]
    grad_rows = jnp.transpose(grad_t)
    allowed = causal(block)
    keys_acc[...] = jnp.zeros_like(keys_acc)
    values_acc[...] = jnp.zeros_like(values_acc)
    query_sum = 0.0
    for step in range(length // block):
        here = slice(step * block, (step + 1) * block)
        upto = slice(0, (step + 1) * block)
        lse = lse_ref[0, 0:1, here]
        scores = dot(keys[upto], queries[:, here], (1, 0))
        probs = jnp.exp(scores - lse)
        low = jnp.where(allowed, probs[step * block :], 0.0)
        probs = jnp.concatenate([probs[: step * block], low], axis=0) if step else low
        values_acc[upto, :] += dot(probs.astype(BF16), grad_rows[here], (1, 0))
        prob_grad = dot(values[upto], grad_t[:, here], (1, 0))
        row_dot = jnp.sum(probs * prob_grad, axis=0, keepdims=True)
        score_grad = (probs * (prob_grad - row_dot) * scale).astype(BF16)
        keys_acc[upto, :] += dot(score_grad, query_rows[here], (1, 0))
        dq = dot(keys_t[:, upto], score_grad, (1, 0))
        dq = rotate_rows(dq, cosine[:, here], -sine[:, here])
        dq_ref[:, here] = dq.astype(BF16)
        query_sum = query_sum + jnp.sum(dq, axis=1, keepdims=True)
    dk = rotate_rows(jnp.transpose(keys_acc[...]), cosine, -sine)
    dv = jnp.transpose(values_acc[...])
    dk_ref[...] = dk.astype(BF16)
    dv_ref[...] = dv.astype(BF16)
    sums = [query_sum, jnp.sum(dk, axis=1, keepdims=True), jnp.sum(dv, axis=1, keepdims=True)]
    for place, part in enumerate(sums):
        sum_ref[0, 0, place] = jnp.broadcast_to(part, (part.shape[0], 128))


def branch_kernel(ctx_t_ref, hidden_ref, first_ref, second_ref, branch_ref, ctx_ref):
    hidden_units = hidden_ref.shape[1]
    context = jnp.transpose(ctx_t_ref[...])
    ctx_ref[...] = context
    total = dot(context, first_ref[:, hidden_units:], (1, 1))
    total = total + dot(hidden_ref[...], second_ref[:, :hidden_units], (1, 1))
    branch_ref[...] = total.astype(BF16)


def row_sums(x):
    return jnp.sum(x.reshape(x.shape[0] // 8, 8, x.shape[1]), axis=0)


def return_kernel(
    after_ref, cot_ref, slope_ref, first_ref, second_ref,
    cot_t_ref, ctx_grad_t_ref, pre_low_ref, in_sum_ref, cot_sum_ref,
):
    hidden_units = slope_ref.shape[1]
    cot = cot_ref[...]
    cot_t_ref[...] = jnp.transpose(cot)
    ctx_grad = dot(cot, first_ref[:, hidden_units:], (1, 0))
    ctx_grad_t_ref[...] = jnp.transpose(ctx_grad).astype(BF16)
    pre_grad = dot(cot, second_ref[:, :hidden_units], (1, 0)) * slope_ref[...]
    pre_low_ref[...] = pre_grad.astype(BF16)

    @pl.when(pl.program_id(0) == 0)
    def _():
        in_sum_ref[...] = jnp.zeros_like(in_sum_ref)
        cot_sum_ref[...] = jnp.zeros_like(cot_sum_ref)

    in_sum_ref[...] += row_sums(pre_grad)
    cot_sum_ref[...] += row_sums(cot.astype(F32))


def norm_kernel(
    x_ref, dq_ref, dk_ref, dv_ref, pre_low_ref, first_ref, second_ref,
    proj_low_ref, norm_grad_ref, gain_sum_ref, shift_sum_ref,
):
    hidden_units = pre_low_ref.shape[1]
    proj_low = jnp.transpose(
        jnp.concatenate([dq_ref[...], dk_ref[...], dv_ref[...]], axis=0)
    )
    proj_low_ref[...] = proj_low
    norm_grad = dot(proj_low, second_ref[:, hidden_units:], (1, 1))
    norm_grad = norm_grad + dot(pre_low_ref[...], first_ref[:, :hidden_units], (1, 1))
    norm_grad_ref[...] = norm_grad.astype(BF16)
    unit, _ = normalize(x_ref[...])

    @pl.when(pl.program_id(0) == 0)
    def _():
        gain_sum_ref[...] = jnp.zeros_like(gain_sum_ref)
        shift_sum_ref[...] = jnp.zeros_like(shift_sum_ref)

    gain_sum_ref[...] += row_sums(norm_grad * unit)
    shift_sum_ref[...] += row_sums(norm_grad)


def half_rows(ref, bit, blocks, part):
    starts = [pl.multiple_of((2 * j + bit) * part, part) for j in range(blocks)]
    return jnp.concatenate([ref[pl.ds(start, part), :] for start in starts], axis=0)


def put(ref, columns, value):
    blocks, part, _ = ref.shape
    ref[:, :, columns] = value.reshape(blocks, part, -1).astype(ref.dtype)


def early_kernel(
    bit_ref, normed_t_ref, cot_t_ref, pre_low_ref, ctx_ref, hidden_ref, early_ref
):
    blocks, part, _ = early_ref.shape
    hidden_units = hidden_ref.shape[1]
    left = half_rows(normed_t_ref, bit_ref[0], blocks, part)
    put(early_ref, slice(0, hidden_units), dot(left, pre_low_ref[...], (1, 0)))
    left = half_rows(cot_t_ref, bit_ref[0], blocks, part)
    put(early_ref, slice(hidden_units, 2 * hidden_units), dot(left, hidden_ref[...], (1, 0)))
    put(early_ref, slice(2 * hidden_units, None), dot(left, ctx_ref[...], (1, 0)))


def late_kernel(bit_ref, normed_t_ref, proj_low_ref, small_ref, late_ref):
    blocks, total, columns = late_ref.shape
    part = total - SMALL_ROWS
    left = half_rows(normed_t_ref, bit_ref[0], blocks, part)
    value = dot(left, proj_low_ref[...], (1, 0)).reshape(blocks, part, columns)
    late_ref[:, :part] = value.astype(late_ref.dtype)
    for block in range(blocks):
        late_ref[block, part:] = small_ref[2 * block + bit_ref[0]].astype(late_ref.dtype)


def whole(x):
    return pl.BlockSpec(x.shape, lambda *_: (0,) * x.ndim)


def tokens(block, columns):
    return pl.BlockSpec((block, columns), lambda t: (t, 0))


def tokens_t(rows, block):
    return pl.BlockSpec((rows, block), lambda t: (0, t))


def cost(flops, nbytes, trans=0):
    return pl.CostEstimate(flops=flops, bytes_accessed=nbytes, transcendentals=trans)


def struct(*shape, dtype=BF16):
    return jax.ShapeDtypeStruct(shape, dtype)


def enter(x, vectors, in_bias, qkv_bias, first, second, cosine, sine, heads, head_dim):
    rows, model = x.shape
    hidden_units = in_bias.shape[1]
    proj = 3 * heads * head_dim
    block = min(256, rows)
    per_seq = cosine.shape[1] // block
    table = pl.BlockSpec((ROT // 2, block), lambda t: (0, lax.rem(t, per_seq)))
    return pl.pallas_call(
        functools.partial(enter_kernel, heads, head_dim),
        grid=(rows // block,),
        in_specs=[
            tokens(block, model), whole(vectors), whole(in_bias), whole(qkv_bias),
            whole(first), whole(second), table, table,
        ],
        out_specs=[
            tokens_t(model, block), tokens_t(proj, block),
            tokens(block, hidden_units), tokens(block, hidden_units),
        ],
        out_shape=[
            struct(model, rows), struct(proj, rows),
            struct(rows, hidden_units), struct(rows, hidden_units, dtype=F32),
        ],
        cost_estimate=cost(
            2 * rows * model * (proj + hidden_units), 2 * (first.size + second.size) + 12 * x.size,
            2 * rows * hidden_units,
        ),
        name="enter",
    )(x, vectors, in_bias, qkv_bias, first, second, cosine, sine)


def attend(proj_t, seqs, heads, head_dim, length):
    block = min(256, length)
    scale = 1.0 / math.sqrt(head_dim)

    def part(which):
        return pl.BlockSpec((head_dim, length), lambda s, h: (which * heads + h, s))

    lse_spec = pl.BlockSpec((1, 8, length), lambda s, h: (h, 0, s))
    work = seqs * heads * length * length
    return pl.pallas_call(
        functools.partial(forward_kernel, scale, block),
        grid=(seqs, heads),
        in_specs=[part(0), part(1), part(2)],
        out_specs=[part(0), lse_spec],
        out_shape=[
            struct(heads * head_dim, seqs * length),
            struct(heads, 8, seqs * length, dtype=F32),
        ],
        cost_estimate=cost(4 * work * head_dim, proj_t.size * 4, work),
        name="attend_forward",
    )(proj_t, proj_t, proj_t)


def attend_back(proj_t, cosine, sine, lse, ctx_grad_t, seqs, heads, head_dim, length):
    block = min(256, length)
    scale = 1.0 / math.sqrt(head_dim)

    def part(which):
        return pl.BlockSpec((head_dim, length), lambda s, h: (which * heads + h, s))

    table = pl.BlockSpec((ROT // 2, length), lambda s, h: (0, 0))
    lse_spec = pl.BlockSpec((1, 8, length), lambda s, h: (h, 0, s))
    sum_spec = pl.BlockSpec((1, 1, 3, head_dim, 128), lambda s, h: (s, h, 0, 0, 0))
    flat = struct(heads * head_dim, seqs * length)
    work = seqs * heads * length * length
    return pl.pallas_call(
        functools.partial(backward_kernel, scale, block),
        grid=(seqs, heads),
        in_specs=[part(0), part(1), part(2), table, table, lse_spec, part(0)],
        out_specs=[part(0), part(0), part(0), sum_spec],
        out_shape=[flat, flat, flat, struct(seqs, heads, 3, head_dim, 128, dtype=F32)],
        scratch_shapes=[pltpu.VMEM((length, head_dim), F32)] * 2,
        cost_estimate=cost(10 * work * head_dim, proj_t.size * 6, work),
        name="attend_backward",
    )(proj_t, proj_t, proj_t, cosine, sine, lse, ctx_grad_t)


def branch_sum(ctx_t, hidden, first, second):
    width, rows = ctx_t.shape
    hidden_units = hidden.shape[1]
    model = first.shape[0]
    block = min(256, rows)
    return pl.pallas_call(
        branch_kernel,
        grid=(rows // block,),
        in_specs=[
            tokens_t(width, block), tokens(block, hidden_units), whole(first), whole(second),
        ],
        out_specs=[tokens(block, model), tokens(block, width)],
        out_shape=[struct(rows, model), struct(rows, width)],
        cost_estimate=cost(2 * rows * model * (width + hidden_units), 8 * rows * model),
        name="branch",
    )(ctx_t, hidden, first, second)


def return_grads(after, cot, slopes, first, second, width):
    rows, model = cot.shape
    hidden_units = slopes.shape[1]
    block = min(256, rows)
    return pl.pallas_call(
        return_kernel,
        grid=(rows // block,),
        in_specs=[
            pl.BlockSpec(memory_space=pl.ANY), tokens(block, model), tokens(block, hidden_units), whole(first), whole(second),
        ],
        out_specs=[
            tokens_t(model, block), tokens_t(width, block), tokens(block, hidden_units),
            pl.BlockSpec((8, hidden_units), lambda t: (0, 0)),
            pl.BlockSpec((8, model), lambda t: (0, 0)),
        ],
        out_shape=[
            struct(model, rows), struct(width, rows), struct(rows, hidden_units),
            struct(8, hidden_units, dtype=F32), struct(8, model, dtype=F32),
        ],
        cost_estimate=cost(2 * rows * model * (width + hidden_units), 10 * rows * model),
        name="return_grads",
    )(after, cot, slopes, first, second)


def norm_sum(x, dq_t, dk_t, dv_t, pre_low, first, second):
    rows, model = x.shape
    width = dq_t.shape[0]
    hidden_units = pre_low.shape[1]
    block = min(256, rows)
    return pl.pallas_call(
        norm_kernel,
        grid=(rows // block,),
        in_specs=[
            tokens(block, model), tokens_t(width, block), tokens_t(width, block),
            tokens_t(width, block), tokens(block, hidden_units), whole(first), whole(second),
        ],
        out_specs=[
            tokens(block, 3 * width), tokens(block, model),
            pl.BlockSpec((8, model), lambda t: (0, 0)),
            pl.BlockSpec((8, model), lambda t: (0, 0)),
        ],
        out_shape=[
            struct(rows, 3 * width), struct(rows, model),
            struct(8, model, dtype=F32), struct(8, model, dtype=F32),
        ],
        cost_estimate=cost(2 * rows * model * (3 * width + hidden_units), 8 * rows * model),
        name="norm_grads",
    )(x, dq_t, dk_t, dv_t, pre_low, first, second)


def finish_kernel(x_ref, cot_ref, own_ref, gain_ref, grad_ref):
    unit, inv_sigma = normalize(x_ref[0])
    unit_grad = own_ref[0].astype(F32) * gain_ref[...]
    grad = cot_ref[0].astype(F32) + inv_sigma * (
        unit_grad
        - jnp.mean(unit_grad, axis=-1, keepdims=True)
        - unit * jnp.mean(unit_grad * unit, axis=-1, keepdims=True)
    )
    grad_ref[0] = grad.astype(BF16)


def finish(x, cot, own, gain):
    rows = pl.BlockSpec((1, x.shape[1] // 2, x.shape[2]), lambda s, t: (s, t, 0))
    return pl.pallas_call(
        finish_kernel,
        grid=(x.shape[0], 2),
        in_specs=[rows, rows, rows, pl.BlockSpec(gain.shape, lambda *_: (0, 0))],
        out_specs=rows,
        out_shape=struct(*x.shape),
        cost_estimate=cost(20 * x.size, 8 * x.size),
        name="finish",
    )(x, cot, own, gain)


def weight_half(kernel, bit, operands, shape, flops, dtype):
    out = struct(*shape, dtype=dtype)
    return pl.pallas_call(
        kernel,
        grid_spec=pltpu.PrefetchScalarGridSpec(
            num_scalar_prefetch=1,
            grid=(1,),
            in_specs=[whole(x) for x in operands],
            out_specs=whole(out),
        ),
        out_shape=out,
        cost_estimate=cost(flops, 4 * operands[0].size),
    )(bit.reshape(1).astype(jnp.int32), *operands)


def rotary_tables(length):
    half_rot = ROT // 2
    position = jnp.arange(length).astype(F32)
    inv_freq = jnp.exp(jnp.arange(half_rot).astype(F32) * (-2.0 * math.log(10000.0) / ROT))
    angles = inv_freq[:, None] * position[None, :]
    return jnp.cos(angles), jnp.sin(angles)


def split_core(grad, dp):
    core = bit_of("dp", 1)
    grad = grad.reshape(dp // 2, 2, -1, grad.shape[-1])
    kept = lax.dynamic_index_in_dim(grad, core, 1, keepdims=False)
    sent = lax.dynamic_index_in_dim(grad, 1 - core, 1, keepdims=False)
    return kept, sent.astype(BF16)


def exchange(kept, sent, dp):
    got = swap(sent, "dp", dp, 1)
    x = kept + got.astype(F32)
    count = dp // 2
    if count > 4:
        steps = [1 << b for b in range(count.bit_length() - 1)]
        return scatter_bits(x, 0, steps[::-1], BF16, dp, 2)
    chip = lax.axis_index("dp") // 2
    total = lax.dynamic_index_in_dim(x, chip, 0, keepdims=False)
    for k in range(1, count):
        piece = lax.dynamic_index_in_dim(x, chip ^ k, 0, keepdims=False).astype(BF16)
        got = swap(piece, "dp", dp, 2 * k)
        total = total + got.astype(F32)
    return total


def body(
    dp, tensor, inputs, ln_gain, ln_bias, w_qkv, b_qkv, w_out, w_in, b_in, w_down, out_bias,
    cotangent,
):
    model = inputs.shape[-1]
    heads, head_dim = b_qkv.shape[1], b_qkv.shape[2] * dp
    width = heads * head_dim
    hidden_units = w_in.shape[1]
    seqs, length = inputs.shape[0], inputs.shape[1] * tensor
    rows = seqs * length
    own = ln_gain.shape[0]
    share = own * tensor
    slow = [1 << b for b in range(1, dp.bit_length() - 1)]
    ways = (slow + [1], slow[::-1] + [1])
    me_z = lax.axis_index("tensor")

    full_in = lax.all_gather(inputs, "tensor", axis=1, tiled=True).reshape(rows, model)
    full_cot = lax.all_gather(cotangent, "tensor", axis=1, tiled=True).reshape(rows, model)

    vector = jnp.stack([ln_gain, ln_bias, out_bias[0] + out_bias[1]])
    by_z = [vector]
    for k in range(1, tensor):
        by_z.append(
            lax.ppermute(vector, "tensor", [(i, (i + k) % tensor) for i in range(tensor)])
        )
    by_z = jnp.stack(by_z)
    order = (me_z - jnp.arange(tensor)) % tensor
    by_z = jnp.take(by_z, order, axis=0).transpose(1, 0, 2)
    small = jnp.concatenate(
        [by_z.reshape(-1), b_qkv.astype(F32).reshape(-1), b_in.astype(F32).reshape(-1)]
    )
    used = small.shape[0]
    padded = -(-used // 1024) * 1024
    small = jnp.pad(small, (0, padded - used)).reshape(-1, 128)
    small = gather_bits(small, dp, 0, ways[0]).reshape(dp, padded)
    norm_rows = small[:, : 3 * share].reshape(dp, 3, share).transpose(1, 0, 2).reshape(3, model)
    gain, out_shift = norm_rows[0], norm_rows[2]
    at = 3 * share
    qkv_count = b_qkv.size
    qkv_bias = (
        small[:, at : at + qkv_count]
        .reshape(dp, 3, heads, head_dim // dp)
        .transpose(1, 2, 0, 3)
        .reshape(3 * width)
    )
    at += qkv_count
    in_groups, in_each = b_in.shape
    in_bias = (
        small[:, at : at + b_in.size]
        .reshape(dp, in_groups, in_each)
        .transpose(1, 0, 2)
        .reshape(hidden_units)
    )

    first = gather_bits(jnp.concatenate([w_in, w_out.T], axis=1), dp, 0, ways[0])
    second = gather_bits(
        jnp.concatenate([w_down.T, w_qkv.reshape(w_qkv.shape[0], -1)], axis=1), dp, 0, ways[1],
    )
    first = first.reshape(model, -1)
    second = second.reshape(model, -1)

    cosine, sine = rotary_tables(length)
    normed_t, proj_t, hidden, slopes = enter(
        full_in, norm_rows, in_bias.reshape(1, -1), qkv_bias.reshape(1, -1), first, second,
        cosine, sine, heads, head_dim,
    )
    ctx_t, lse = attend(proj_t, seqs, heads, head_dim, length)
    branch, context = branch_sum(ctx_t, hidden, first, second)
    summed = lax.psum_scatter(
        branch.reshape(seqs, length, model), "tensor", scatter_dimension=1, tiled=True
    )
    outputs = (inputs.astype(F32) + summed.astype(F32) + out_shift).astype(BF16)

    cot_t, ctx_grad_t, pre_low, in_sum, cot_sum = return_grads(
        context, full_cot, slopes, first, second, width
    )
    part = model // dp
    core = bit_of("dp", 1)
    aligned = dp > 1 and part % 16 == 0
    if aligned:
        operands = (normed_t, cot_t, pre_low, context, hidden)
        shape = (dp // 2, part, 2 * hidden_units + width)
        flops = rows * model * shape[2]
        early_sent = weight_half(early_kernel, 1 - core, operands, shape, flops, BF16)
        early_kept = weight_half(early_kernel, core, operands, shape, flops, F32)
    else:
        early_kept, early_sent = split_core(
            jnp.concatenate(
                [
                    dot(normed_t, pre_low, (1, 0)),
                    dot(cot_t, hidden, (1, 0)),
                    dot(cot_t, context, (1, 0)),
                ],
                axis=1,
            ),
            dp,
        )
    dq_t, dk_t, dv_t, sums = attend_back(
        proj_t, cosine, sine, lse, ctx_grad_t, seqs, heads, head_dim, length
    )
    proj_low, norm_grad, gain_sum, shift_sum = norm_sum(
        full_in, dq_t, dk_t, dv_t, pre_low, first, second
    )
    own_grad = lax.psum_scatter(
        norm_grad.reshape(seqs, length, model), "tensor", scatter_dimension=1, tiled=True
    )
    grad_qkv_bias = jnp.sum(sums[..., 0], axis=0).transpose(1, 0, 2)
    grad_in_bias = jnp.sum(in_sum, axis=0)
    bias_part = jnp.sum(cot_sum, axis=0).reshape(dp, tensor, own)
    pair = jnp.stack([gain_sum, shift_sum]).sum(axis=1).reshape(2, dp, tensor, own)
    pair_total = lax.dynamic_index_in_dim(pair, me_z, 2, keepdims=False)
    for k in range(1, tensor):
        piece = lax.dynamic_index_in_dim(pair, (me_z + k) % tensor, 2, keepdims=False)
        got = lax.ppermute(
            piece, "tensor", [(i, (i + k) % tensor) for i in range(tensor)]
        )
        pair_total = pair_total + got
    bias_total = lax.dynamic_index_in_dim(bias_part, me_z, 1, keepdims=False)
    small = jnp.concatenate(
        [
            pair_total[0], pair_total[1], bias_total,
            grad_qkv_bias.reshape(3, heads, dp, head_dim // dp)
            .transpose(2, 0, 1, 3)
            .reshape(dp, -1),
            grad_in_bias.reshape(in_groups, dp, in_each).transpose(1, 0, 2).reshape(dp, -1),
        ],
        axis=1,
    )
    columns = 3 * width
    small = jnp.pad(
        small[:, None, :], ((0, 0), (0, SMALL_ROWS - 1), (0, columns - small.shape[1]))
    )
    if aligned:
        operands = (normed_t, proj_low, small)
        shape = (dp // 2, part + SMALL_ROWS, columns)
        flops = rows * model * columns
        late_sent = weight_half(late_kernel, 1 - core, operands, shape, flops, BF16)
        late_kept = weight_half(late_kernel, core, operands, shape, flops, F32)
    else:
        late = dot(normed_t, proj_low, (1, 0)).reshape(dp, part, columns)
        late_kept, late_sent = split_core(jnp.concatenate([late, small], axis=1), dp)

    early = exchange(early_kept, early_sent, dp)
    late = exchange(late_kept, late_sent, dp)
    in_out = early[:, :hidden_units]
    down_out = early[:, hidden_units : 2 * hidden_units].T
    out_out = early[:, 2 * hidden_units :].T
    qkv_out = late[:part].reshape(part, 3, width)
    small = late[part]
    gain_out, shift_out, bias_out = (small[k * own : (k + 1) * own] for k in range(3))
    bias_grad = jnp.stack([bias_out, bias_out])
    at = 3 * own
    qkv_bias_out = small[at : at + qkv_count].reshape(b_qkv.shape)
    at += qkv_count
    in_bias_out = small[at : at + b_in.size].reshape(b_in.shape)

    input_grad = finish(inputs, cotangent, own_grad, gain.reshape(1, model))
    return (
        outputs,
        input_grad,
        gain_out,
        shift_out,
        qkv_out,
        qkv_bias_out,
        out_out,
        in_out,
        in_bias_out,
        down_out,
        bias_grad,
    )


def solution(mesh):
    spread = P("dp", "tensor", None)
    vector = P(("dp", "tensor"))
    qkv, qkv_bias = P("dp", None, "tensor"), P(None, "tensor", "dp")
    by_out, by_in, pair = P("tensor", "dp"), P("dp", "tensor"), P(None, ("dp", "tensor"))

    def layer(*arrays):
        return body(mesh.shape["dp"], mesh.shape["tensor"], *arrays)

    return jax.shard_map(
        layer,
        mesh=mesh,
        in_specs=(
            spread, vector, vector, qkv, qkv_bias, by_out, by_in, by_out, by_out, pair, spread,
        ),
        out_specs=(
            spread, spread, vector, vector, qkv, qkv_bias, by_out, by_in, by_out, by_out, pair,
        ),
        check_vma=False,
    )
```

```python
import functools
import math

import jax
import jax.numpy as jnp
from jax import lax
from jax.experimental import pallas as pl
from jax.experimental.pallas import tpu as pltpu
from jax.sharding import PartitionSpec as P

ROT = 16
EPS = 1e-05
ROOT_HALF = 0.7071067811865476
INV_ROOT_TAU = 0.3989422804014327
NEG_BIG = -1e30
SMALL_ROWS = 16
F32 = jnp.float32
BF16 = jnp.bfloat16


def dot(a, b, contract, out=F32):
    return lax.dot_general(
        a, b, (((contract[0],), (contract[1],)), ((), ())), preferred_element_type=out
    )


def swap(x, axis_name, size, step):
    return lax.ppermute(x, axis_name, [(i, i ^ step) for i in range(size)])


def bit_of(axis_name, step):
    return (lax.axis_index(axis_name) // step) % 2


def gather_bits(x, size, axis, steps):
    done = []
    for step in steps:
        other = swap(x, "dp", size, step)
        mine_first = bit_of("dp", step) == 0
        low = jnp.where(mine_first, x, other)
        high = jnp.where(mine_first, other, x)
        place = axis + sum(1 for s in done if s > step)
        x = jnp.stack([low, high], axis=place)
        done.append(step)
    shape = x.shape
    levels = len(steps)
    return x.reshape(shape[:axis] + (size,) + shape[axis + levels :])


def scatter_bits(x, axis, steps, wire, size, unit):
    shape = x.shape
    levels = len(steps)
    x = x.reshape(shape[:axis] + (2,) * levels + shape[axis + 1 :])
    left = sorted(steps, reverse=True)
    for step in steps:
        place = axis + left.index(step)
        bit = bit_of("dp", step * unit)
        keep = lax.dynamic_index_in_dim(x, bit, place, keepdims=False)
        send = lax.dynamic_index_in_dim(x, 1 - bit, place, keepdims=False)
        got = swap(send.astype(wire), "dp", size, step * unit)
        x = keep + got.astype(F32)
        left.remove(step)
    return x


def rotate_rows(x, cosine, sine):
    half = ROT // 2
    first, second = x[:half], x[half:ROT]
    return jnp.concatenate(
        [first * cosine - second * sine, second * cosine + first * sine, x[ROT:]], axis=0
    )


def normalize(x):
    wide = x.astype(F32)
    centred = wide - jnp.mean(wide, axis=-1, keepdims=True)
    inv_sigma = lax.rsqrt(jnp.mean(centred * centred, axis=-1, keepdims=True) + EPS)
    return centred * inv_sigma, inv_sigma


def enter_kernel(
    heads, head_dim, x_ref, vec_ref, in_bias_ref, qkv_bias_ref, first_ref, second_ref,
    cos_ref, sin_ref, normed_t_ref, proj_t_ref, hidden_ref, slope_ref,
):
    width = heads * head_dim
    hidden_units = hidden_ref.shape[1]
    unit, _ = normalize(x_ref[...])
    wide = unit * vec_ref[0:1] + vec_ref[1:2]
    normed = wide.astype(BF16)
    normed_t_ref[...] = jnp.transpose(normed)
    projected = dot(normed, second_ref[:, hidden_units:], (1, 0)) + qkv_bias_ref[...]
    projected = jnp.transpose(projected)
    cosine, sine = cos_ref[...], sin_ref[...]
    for place in range(2 * heads):
        rows = slice(place * head_dim, (place + 1) * head_dim)
        proj_t_ref[rows] = rotate_rows(projected[rows], cosine, sine).astype(BF16)
    proj_t_ref[2 * width :] = projected[2 * width :].astype(BF16)
    pre_act = dot(normed, first_ref[:, :hidden_units], (1, 0)) + in_bias_ref[...]
    normal_cdf = 0.5 * (1.0 + lax.erf(pre_act * ROOT_HALF))
    normal_pdf = jnp.exp(-0.5 * pre_act * pre_act) * INV_ROOT_TAU
    hidden_ref[...] = (pre_act * normal_cdf).astype(BF16)
    slope_ref[...] = normal_cdf + pre_act * normal_pdf


def causal(block):
    key_pos = lax.broadcasted_iota(jnp.int32, (block, block), 0)
    query_pos = lax.broadcasted_iota(jnp.int32, (block, block), 1)
    return key_pos <= query_pos


def forward_kernel(scale, block, q_ref, k_ref, v_ref, ctx_ref, lse_ref):
    length = q_ref.shape[1]
    queries = q_ref[...] * jnp.asarray(scale, BF16)
    keys = jnp.transpose(k_ref[...])
    values = v_ref[...]
    allowed = causal(block)
    for step in range(length // block):
        here = slice(step * block, (step + 1) * block)
        q_cols = queries[:, here]
        near = jnp.where(allowed, dot(keys[here], q_cols, (1, 0)), NEG_BIG)
        top = jnp.max(near, axis=0, keepdims=True)
        if step:
            far = dot(keys[: step * block], q_cols, (1, 0))
            top = jnp.maximum(top, jnp.max(far, axis=0, keepdims=True))
        near = jnp.exp(near - top)
        total = jnp.sum(near, axis=0, keepdims=True)
        context = dot(values[:, here], near.astype(BF16), (1, 0))
        if step:
            far = jnp.exp(far - top)
            total = total + jnp.sum(far, axis=0, keepdims=True)
            context = context + dot(values[:, : step * block], far.astype(BF16), (1, 0))
        ctx_ref[:, here] = (context / total).astype(BF16)
        lse_ref[0, :, here] = jnp.broadcast_to(top + jnp.log(total), (8, block))


def backward_kernel(
    scale, block, q_ref, k_ref, v_ref, cos_ref, sin_ref, lse_ref, grad_ref,
    dq_ref, dk_ref, dv_ref, sum_ref, keys_acc, values_acc,
):
    length = q_ref.shape[1]
    cosine, sine = cos_ref[...], sin_ref[...]
    queries = q_ref[...] * jnp.asarray(scale, BF16)
    query_rows = jnp.transpose(q_ref[...])
    keys_t = k_ref[...]
    keys = jnp.transpose(keys_t)
    values = jnp.transpose(v_ref[...])
    grad_t = grad_ref[...]
    grad_rows = jnp.transpose(grad_t)
    allowed = causal(block)
    keys_acc[...] = jnp.zeros_like(keys_acc)
    values_acc[...] = jnp.zeros_like(values_acc)
    query_sum = 0.0
    for step in range(length // block):
        here = slice(step * block, (step + 1) * block)
        upto = slice(0, (step + 1) * block)
        lse = lse_ref[0, 0:1, here]
        scores = dot(keys[upto], queries[:, here], (1, 0))
        probs = jnp.exp(scores - lse)
        low = jnp.where(allowed, probs[step * block :], 0.0)
        probs = jnp.concatenate([probs[: step * block], low], axis=0) if step else low
        values_acc[upto, :] += dot(probs.astype(BF16), grad_rows[here], (1, 0))
        prob_grad = dot(values[upto], grad_t[:, here], (1, 0))
        row_dot = jnp.sum(probs * prob_grad, axis=0, keepdims=True)
        score_grad = (probs * (prob_grad - row_dot) * scale).astype(BF16)
        keys_acc[upto, :] += dot(score_grad, query_rows[here], (1, 0))
        dq = dot(keys_t[:, upto], score_grad, (1, 0))
        dq = rotate_rows(dq, cosine[:, here], -sine[:, here])
        dq_ref[:, here] = dq.astype(BF16)
        query_sum = query_sum + jnp.sum(dq, axis=1, keepdims=True)
    dk = rotate_rows(jnp.transpose(keys_acc[...]), cosine, -sine)
    dv = jnp.transpose(values_acc[...])
    dk_ref[...] = dk.astype(BF16)
    dv_ref[...] = dv.astype(BF16)
    sums = [query_sum, jnp.sum(dk, axis=1, keepdims=True), jnp.sum(dv, axis=1, keepdims=True)]
    for place, part in enumerate(sums):
        sum_ref[0, 0, place] = jnp.broadcast_to(part, (part.shape[0], 128))


def branch_kernel(ctx_t_ref, hidden_ref, first_ref, second_ref, branch_ref, ctx_ref):
    hidden_units = hidden_ref.shape[1]
    context = jnp.transpose(ctx_t_ref[...])
    ctx_ref[...] = context
    total = dot(context, first_ref[:, hidden_units:], (1, 1))
    total = total + dot(hidden_ref[...], second_ref[:, :hidden_units], (1, 1))
    branch_ref[...] = total.astype(BF16)


def row_sums(x):
    return jnp.sum(x.reshape(x.shape[0] // 8, 8, x.shape[1]), axis=0)


def return_kernel(
    after_ref, cot_ref, slope_ref, first_ref, second_ref,
    cot_t_ref, ctx_grad_t_ref, pre_low_ref, in_sum_ref, cot_sum_ref,
):
    hidden_units = slope_ref.shape[1]
    cot = cot_ref[...]
    cot_t_ref[...] = jnp.transpose(cot)
    ctx_grad = dot(cot, first_ref[:, hidden_units:], (1, 0))
    ctx_grad_t_ref[...] = jnp.transpose(ctx_grad).astype(BF16)
    pre_grad = dot(cot, second_ref[:, :hidden_units], (1, 0)) * slope_ref[...]
    pre_low_ref[...] = pre_grad.astype(BF16)

    @pl.when(pl.program_id(0) == 0)
    def _():
        in_sum_ref[...] = jnp.zeros_like(in_sum_ref)
        cot_sum_ref[...] = jnp.zeros_like(cot_sum_ref)

    in_sum_ref[...] += row_sums(pre_grad)
    cot_sum_ref[...] += row_sums(cot.astype(F32))


def norm_kernel(
    x_ref, dq_ref, dk_ref, dv_ref, pre_low_ref, first_ref, second_ref,
    proj_low_ref, norm_grad_ref, gain_sum_ref, shift_sum_ref,
):
    hidden_units = pre_low_ref.shape[1]
    proj_low = jnp.transpose(
        jnp.concatenate([dq_ref[...], dk_ref[...], dv_ref[...]], axis=0)
    )
    proj_low_ref[...] = proj_low
    norm_grad = dot(proj_low, second_ref[:, hidden_units:], (1, 1))
    norm_grad = norm_grad + dot(pre_low_ref[...], first_ref[:, :hidden_units], (1, 1))
    norm_grad_ref[...] = norm_grad.astype(BF16)
    unit, _ = normalize(x_ref[...])

    @pl.when(pl.program_id(0) == 0)
    def _():
        gain_sum_ref[...] = jnp.zeros_like(gain_sum_ref)
        shift_sum_ref[...] = jnp.zeros_like(shift_sum_ref)

    gain_sum_ref[...] += row_sums(norm_grad * unit)
    shift_sum_ref[...] += row_sums(norm_grad)


def half_rows(ref, at_ref, blocks, part):
    chips = [lax.bitwise_xor(at_ref[1], k) for k in range(blocks)]
    starts = [pl.multiple_of((2 * chip + at_ref[0]) * part, part) for chip in chips]
    return jnp.concatenate([ref[pl.ds(start, part), :] for start in starts], axis=0)


def put(outs, got_ref, rows, columns, value):
    blocks = value.shape[0] // (rows.stop - rows.start)
    value = value.reshape(blocks, rows.stop - rows.start, -1)
    if got_ref is None:
        outs[0][:, rows, columns] = value.astype(BF16)
        return
    value = value + got_ref[:, rows, columns].astype(F32)
    for k in range(blocks):
        outs[k][rows, columns] = value[k].astype(outs[k].dtype)


def early_kernel(blocks, part, at_ref, normed_t_ref, cot_t_ref, pre_low_ref, ctx_ref, hidden_ref, *refs):
    got_ref, outs = (None, refs) if len(refs) == 1 else (refs[0], refs[1:])
    units = hidden_ref.shape[1]
    rows = slice(0, part)
    left = half_rows(normed_t_ref, at_ref, blocks, part)
    put(outs, got_ref, rows, slice(0, units), dot(left, pre_low_ref[...], (1, 0)))
    left = half_rows(cot_t_ref, at_ref, blocks, part)
    put(outs, got_ref, rows, slice(units, 2 * units), dot(left, hidden_ref[...], (1, 0)))
    put(outs, got_ref, rows, slice(2 * units, None), dot(left, ctx_ref[...], (1, 0)))


def late_kernel(blocks, part, at_ref, normed_t_ref, proj_low_ref, small_ref, *refs):
    got_ref, outs = (None, refs) if len(refs) == 1 else (refs[0], refs[1:])
    left = half_rows(normed_t_ref, at_ref, blocks, part)
    put(outs, got_ref, slice(0, part), slice(None), dot(left, proj_low_ref[...], (1, 0)))
    members = [2 * lax.bitwise_xor(at_ref[1], k) + at_ref[0] for k in range(blocks)]
    extra = jnp.concatenate([small_ref[member] for member in members], axis=0)
    put(outs, got_ref, slice(part, part + SMALL_ROWS), slice(None), extra)


def whole(x):
    return pl.BlockSpec(x.shape, lambda *_: (0,) * x.ndim)


def tokens(block, columns):
    return pl.BlockSpec((block, columns), lambda t: (t, 0))


def tokens_t(rows, block):
    return pl.BlockSpec((rows, block), lambda t: (0, t))


def cost(flops, nbytes, trans=0):
    return pl.CostEstimate(flops=flops, bytes_accessed=nbytes, transcendentals=trans)


def struct(*shape, dtype=BF16):
    return jax.ShapeDtypeStruct(shape, dtype)


def enter(x, vectors, in_bias, qkv_bias, first, second, cosine, sine, heads, head_dim):
    rows, model = x.shape
    hidden_units = in_bias.shape[1]
    proj = 3 * heads * head_dim
    block = min(256, rows)
    per_seq = cosine.shape[1] // block
    table = pl.BlockSpec((ROT // 2, block), lambda t: (0, lax.rem(t, per_seq)))
    return pl.pallas_call(
        functools.partial(enter_kernel, heads, head_dim),
        grid=(rows // block,),
        in_specs=[
            tokens(block, model), whole(vectors), whole(in_bias), whole(qkv_bias),
            whole(first), whole(second), table, table,
        ],
        out_specs=[
            tokens_t(model, block), tokens_t(proj, block),
            tokens(block, hidden_units), tokens(block, hidden_units),
        ],
        out_shape=[
            struct(model, rows), struct(proj, rows),
            struct(rows, hidden_units), struct(rows, hidden_units, dtype=F32),
        ],
        cost_estimate=cost(
            2 * rows * model * (proj + hidden_units), 2 * (first.size + second.size) + 12 * x.size,
            2 * rows * hidden_units,
        ),
        name="enter",
    )(x, vectors, in_bias, qkv_bias, first, second, cosine, sine)


def attend(proj_t, seqs, heads, head_dim, length):
    block = min(256, length)
    scale = 1.0 / math.sqrt(head_dim)

    def part(which):
        return pl.BlockSpec((head_dim, length), lambda s, h: (which * heads + h, s))

    lse_spec = pl.BlockSpec((1, 8, length), lambda s, h: (h, 0, s))
    work = seqs * heads * length * length
    return pl.pallas_call(
        functools.partial(forward_kernel, scale, block),
        grid=(seqs, heads),
        in_specs=[part(0), part(1), part(2)],
        out_specs=[part(0), lse_spec],
        out_shape=[
            struct(heads * head_dim, seqs * length),
            struct(heads, 8, seqs * length, dtype=F32),
        ],
        cost_estimate=cost(4 * work * head_dim, proj_t.size * 4, work),
        name="attend_forward",
    )(proj_t, proj_t, proj_t)


def attend_back(proj_t, cosine, sine, lse, ctx_grad_t, seqs, heads, head_dim, length):
    block = min(256, length)
    scale = 1.0 / math.sqrt(head_dim)

    def part(which):
        return pl.BlockSpec((head_dim, length), lambda s, h: (which * heads + h, s))

    table = pl.BlockSpec((ROT // 2, length), lambda s, h: (0, 0))
    lse_spec = pl.BlockSpec((1, 8, length), lambda s, h: (h, 0, s))
    sum_spec = pl.BlockSpec((1, 1, 3, head_dim, 128), lambda s, h: (s, h, 0, 0, 0))
    flat = struct(heads * head_dim, seqs * length)
    work = seqs * heads * length * length
    return pl.pallas_call(
        functools.partial(backward_kernel, scale, block),
        grid=(seqs, heads),
        in_specs=[part(0), part(1), part(2), table, table, lse_spec, part(0)],
        out_specs=[part(0), part(0), part(0), sum_spec],
        out_shape=[flat, flat, flat, struct(seqs, heads, 3, head_dim, 128, dtype=F32)],
        scratch_shapes=[pltpu.VMEM((length, head_dim), F32)] * 2,
        cost_estimate=cost(10 * work * head_dim, proj_t.size * 6, work),
        name="attend_backward",
    )(proj_t, proj_t, proj_t, cosine, sine, lse, ctx_grad_t)


def branch_sum(ctx_t, hidden, first, second):
    width, rows = ctx_t.shape
    hidden_units = hidden.shape[1]
    model = first.shape[0]
    block = min(256, rows)
    return pl.pallas_call(
        branch_kernel,
        grid=(rows // block,),
        in_specs=[
            tokens_t(width, block), tokens(block, hidden_units), whole(first), whole(second),
        ],
        out_specs=[tokens(block, model), tokens(block, width)],
        out_shape=[struct(rows, model), struct(rows, width)],
        cost_estimate=cost(2 * rows * model * (width + hidden_units), 8 * rows * model),
        name="branch",
    )(ctx_t, hidden, first, second)


def return_grads(after, cot, slopes, first, second, width):
    rows, model = cot.shape
    hidden_units = slopes.shape[1]
    block = min(256, rows)
    return pl.pallas_call(
        return_kernel,
        grid=(rows // block,),
        in_specs=[
            pl.BlockSpec(memory_space=pl.ANY), tokens(block, model), tokens(block, hidden_units), whole(first), whole(second),
        ],
        out_specs=[
            tokens_t(model, block), tokens_t(width, block), tokens(block, hidden_units),
            pl.BlockSpec((8, hidden_units), lambda t: (0, 0)),
            pl.BlockSpec((8, model), lambda t: (0, 0)),
        ],
        out_shape=[
            struct(model, rows), struct(width, rows), struct(rows, hidden_units),
            struct(8, hidden_units, dtype=F32), struct(8, model, dtype=F32),
        ],
        cost_estimate=cost(2 * rows * model * (width + hidden_units), 10 * rows * model),
        name="return_grads",
    )(after, cot, slopes, first, second)


def norm_sum(x, dq_t, dk_t, dv_t, pre_low, first, second):
    rows, model = x.shape
    width = dq_t.shape[0]
    hidden_units = pre_low.shape[1]
    block = min(256, rows)
    return pl.pallas_call(
        norm_kernel,
        grid=(rows // block,),
        in_specs=[
            tokens(block, model), tokens_t(width, block), tokens_t(width, block),
            tokens_t(width, block), tokens(block, hidden_units), whole(first), whole(second),
        ],
        out_specs=[
            tokens(block, 3 * width), tokens(block, model),
            pl.BlockSpec((8, model), lambda t: (0, 0)),
            pl.BlockSpec((8, model), lambda t: (0, 0)),
        ],
        out_shape=[
            struct(rows, 3 * width), struct(rows, model),
            struct(8, model, dtype=F32), struct(8, model, dtype=F32),
        ],
        cost_estimate=cost(2 * rows * model * (3 * width + hidden_units), 8 * rows * model),
        name="norm_grads",
    )(x, dq_t, dk_t, dv_t, pre_low, first, second)


def finish_kernel(x_ref, cot_ref, own_ref, gain_ref, grad_ref):
    unit, inv_sigma = normalize(x_ref[0])
    unit_grad = own_ref[0].astype(F32) * gain_ref[...]
    grad = cot_ref[0].astype(F32) + inv_sigma * (
        unit_grad
        - jnp.mean(unit_grad, axis=-1, keepdims=True)
        - unit * jnp.mean(unit_grad * unit, axis=-1, keepdims=True)
    )
    grad_ref[0] = grad.astype(BF16)


def finish(x, cot, own, gain):
    rows = pl.BlockSpec((1, x.shape[1] // 2, x.shape[2]), lambda s, t: (s, t, 0))
    return pl.pallas_call(
        finish_kernel,
        grid=(x.shape[0], 2),
        in_specs=[rows, rows, rows, pl.BlockSpec(gain.shape, lambda *_: (0, 0))],
        out_specs=rows,
        out_shape=struct(*x.shape),
        cost_estimate=cost(20 * x.size, 8 * x.size),
        name="finish",
    )(x, cot, own, gain)


def weight_half(kernel, at, operands, got, blocks, part, shape, flops):
    if got is None:
        outs = [struct(blocks, *shape)]
    else:
        operands = operands + (got,)
        outs = [struct(*shape, dtype=F32)] + [struct(*shape)] * (blocks - 1)
    return pl.pallas_call(
        functools.partial(kernel, blocks, part),
        grid_spec=pltpu.PrefetchScalarGridSpec(
            num_scalar_prefetch=1,
            grid=(1,),
            in_specs=[whole(x) for x in operands],
            out_specs=[whole(x) for x in outs],
        ),
        out_shape=outs,
        cost_estimate=cost(flops, 4 * operands[0].size),
    )(jnp.stack(at).astype(jnp.int32), *operands)


def rotary_tables(length):
    half_rot = ROT // 2
    position = jnp.arange(length).astype(F32)
    inv_freq = jnp.exp(jnp.arange(half_rot).astype(F32) * (-2.0 * math.log(10000.0) / ROT))
    angles = inv_freq[:, None] * position[None, :]
    return jnp.cos(angles), jnp.sin(angles)


def split_core(grad, dp):
    core = bit_of("dp", 1)
    grad = grad.reshape(dp // 2, 2, -1, grad.shape[-1])
    kept = lax.dynamic_index_in_dim(grad, core, 1, keepdims=False)
    sent = lax.dynamic_index_in_dim(grad, 1 - core, 1, keepdims=False)
    return kept, sent.astype(BF16)


def swap_core(sent, dp):
    return swap(sent, "dp", dp, 1)


def add_pieces(pieces, dp):
    total = pieces[0]
    for k in range(1, len(pieces)):
        got = swap(pieces[k], "dp", dp, 2 * k)
        total = total + got.astype(F32)
    return total


def exchange(grad, dp):
    kept, sent = split_core(grad, dp)
    x = kept + swap_core(sent, dp).astype(F32)
    steps = [1 << b for b in range((dp // 2).bit_length() - 1)]
    return scatter_bits(x, 0, steps[::-1], BF16, dp, 2)


def body(
    dp, tensor, inputs, ln_gain, ln_bias, w_qkv, b_qkv, w_out, w_in, b_in, w_down, out_bias,
    cotangent,
):
    model = inputs.shape[-1]
    heads, head_dim = b_qkv.shape[1], b_qkv.shape[2] * dp
    width = heads * head_dim
    hidden_units = w_in.shape[1]
    seqs, length = inputs.shape[0], inputs.shape[1] * tensor
    rows = seqs * length
    own = ln_gain.shape[0]
    share = own * tensor
    slow = [1 << b for b in range(1, dp.bit_length() - 1)]
    ways = (slow + [1], slow[::-1] + [1])
    me_z = lax.axis_index("tensor")

    full_in = lax.all_gather(inputs, "tensor", axis=1, tiled=True).reshape(rows, model)
    full_cot = lax.all_gather(cotangent, "tensor", axis=1, tiled=True).reshape(rows, model)

    vector = jnp.stack([ln_gain, ln_bias, out_bias[0] + out_bias[1]])
    by_z = [vector]
    for k in range(1, tensor):
        by_z.append(
            lax.ppermute(vector, "tensor", [(i, (i + k) % tensor) for i in range(tensor)])
        )
    by_z = jnp.stack(by_z)
    order = (me_z - jnp.arange(tensor)) % tensor
    by_z = jnp.take(by_z, order, axis=0).transpose(1, 0, 2)
    small = jnp.concatenate(
        [by_z.reshape(-1), b_qkv.astype(F32).reshape(-1), b_in.astype(F32).reshape(-1)]
    )
    used = small.shape[0]
    padded = -(-used // 1024) * 1024
    small = jnp.pad(small, (0, padded - used)).reshape(-1, 128)
    small = gather_bits(small, dp, 0, ways[0]).reshape(dp, padded)
    norm_rows = small[:, : 3 * share].reshape(dp, 3, share).transpose(1, 0, 2).reshape(3, model)
    gain, out_shift = norm_rows[0], norm_rows[2]
    at = 3 * share
    qkv_count = b_qkv.size
    qkv_bias = (
        small[:, at : at + qkv_count]
        .reshape(dp, 3, heads, head_dim // dp)
        .transpose(1, 2, 0, 3)
        .reshape(3 * width)
    )
    at += qkv_count
    in_groups, in_each = b_in.shape
    in_bias = (
        small[:, at : at + b_in.size]
        .reshape(dp, in_groups, in_each)
        .transpose(1, 0, 2)
        .reshape(hidden_units)
    )

    first = gather_bits(jnp.concatenate([w_in, w_out.T], axis=1), dp, 0, ways[0])
    second = gather_bits(
        jnp.concatenate([w_down.T, w_qkv.reshape(w_qkv.shape[0], -1)], axis=1), dp, 0, ways[1],
    )
    first = first.reshape(model, -1)
    second = second.reshape(model, -1)

    cosine, sine = rotary_tables(length)
    normed_t, proj_t, hidden, slopes = enter(
        full_in, norm_rows, in_bias.reshape(1, -1), qkv_bias.reshape(1, -1), first, second,
        cosine, sine, heads, head_dim,
    )
    ctx_t, lse = attend(proj_t, seqs, heads, head_dim, length)
    branch, context = branch_sum(ctx_t, hidden, first, second)
    summed = lax.psum_scatter(
        branch.reshape(seqs, length, model), "tensor", scatter_dimension=1, tiled=True
    )
    outputs = (inputs.astype(F32) + summed.astype(F32) + out_shift).astype(BF16)

    cot_t, ctx_grad_t, pre_low, in_sum, cot_sum = return_grads(
        context, full_cot, slopes, first, second, width
    )
    part = model // dp
    core = bit_of("dp", 1)
    aligned = 2 <= dp <= 8 and part % 16 == 0
    chip = lax.axis_index("dp") // 2
    blocks = dp // 2
    if aligned:
        operands = (normed_t, cot_t, pre_low, context, hidden)
        shape = (part, 2 * hidden_units + width)
        flops = rows * model * shape[1]
        (early_sent,) = weight_half(
            early_kernel, (1 - core, chip), operands, None, blocks, part, shape, flops
        )
        early_got = swap_core(early_sent, dp)
        early_pieces = weight_half(
            early_kernel, (core, chip), operands, early_got, blocks, part,
            shape, flops,
        )
        early = add_pieces(early_pieces, dp)
    else:
        early = jnp.concatenate(
            [
                dot(normed_t, pre_low, (1, 0)),
                dot(cot_t, hidden, (1, 0)),
                dot(cot_t, context, (1, 0)),
            ],
            axis=1,
        )
        early = exchange(early, dp)
    dq_t, dk_t, dv_t, sums = attend_back(
        proj_t, cosine, sine, lse, ctx_grad_t, seqs, heads, head_dim, length
    )
    proj_low, norm_grad, gain_sum, shift_sum = norm_sum(
        full_in, dq_t, dk_t, dv_t, pre_low, first, second
    )
    own_grad = lax.psum_scatter(
        norm_grad.reshape(seqs, length, model), "tensor", scatter_dimension=1, tiled=True
    )
    grad_qkv_bias = jnp.sum(sums[..., 0], axis=0).transpose(1, 0, 2)
    grad_in_bias = jnp.sum(in_sum, axis=0)
    bias_part = jnp.sum(cot_sum, axis=0).reshape(dp, tensor, own)
    pair = jnp.stack([gain_sum, shift_sum]).sum(axis=1).reshape(2, dp, tensor, own)
    pair_total = lax.dynamic_index_in_dim(pair, me_z, 2, keepdims=False)
    for k in range(1, tensor):
        piece = lax.dynamic_index_in_dim(pair, (me_z + k) % tensor, 2, keepdims=False)
        got = lax.ppermute(
            piece, "tensor", [(i, (i + k) % tensor) for i in range(tensor)]
        )
        pair_total = pair_total + got
    bias_total = lax.dynamic_index_in_dim(bias_part, me_z, 1, keepdims=False)
    small = jnp.concatenate(
        [
            pair_total[0], pair_total[1], bias_total,
            grad_qkv_bias.reshape(3, heads, dp, head_dim // dp)
            .transpose(2, 0, 1, 3)
            .reshape(dp, -1),
            grad_in_bias.reshape(in_groups, dp, in_each).transpose(1, 0, 2).reshape(dp, -1),
        ],
        axis=1,
    )
    columns = 3 * width
    small = jnp.pad(
        small[:, None, :], ((0, 0), (0, SMALL_ROWS - 1), (0, columns - small.shape[1]))
    )
    if aligned:
        operands = (normed_t, proj_low, small)
        shape = (part + SMALL_ROWS, columns)
        flops = rows * model * columns
        (late_sent,) = weight_half(
            late_kernel, (1 - core, chip), operands, None, blocks, part, shape,
            flops,
        )
        late_got = swap_core(late_sent, dp)
        late_pieces = weight_half(
            late_kernel, (core, chip), operands, late_got, blocks, part, shape,
            flops,
        )
        late = add_pieces(late_pieces, dp)
    else:
        late = dot(normed_t, proj_low, (1, 0)).reshape(dp, part, columns)
        late = exchange(jnp.concatenate([late, small], axis=1), dp)
    in_out = early[:, :hidden_units]
    down_out = early[:, hidden_units : 2 * hidden_units].T
    out_out = early[:, 2 * hidden_units :].T
    qkv_out = late[:part].reshape(part, 3, width)
    small = late[part]
    gain_out, shift_out, bias_out = (small[k * own : (k + 1) * own] for k in range(3))
    bias_grad = jnp.stack([bias_out, bias_out])
    at = 3 * own
    qkv_bias_out = small[at : at + qkv_count].reshape(b_qkv.shape)
    at += qkv_count
    in_bias_out = small[at : at + b_in.size].reshape(b_in.shape)

    input_grad = finish(inputs, cotangent, own_grad, gain.reshape(1, model))
    return (
        outputs,
        input_grad,
        gain_out,
        shift_out,
        qkv_out,
        qkv_bias_out,
        out_out,
        in_out,
        in_bias_out,
        down_out,
        bias_grad,
    )


def solution(mesh):
    spread = P("dp", "tensor", None)
    vector = P(("dp", "tensor"))
    qkv, qkv_bias = P("dp", None, "tensor"), P(None, "tensor", "dp")
    by_out, by_in, pair = P("tensor", "dp"), P("dp", "tensor"), P(None, ("dp", "tensor"))

    def layer(*arrays):
        return body(mesh.shape["dp"], mesh.shape["tensor"], *arrays)

    return jax.shard_map(
        layer,
        mesh=mesh,
        in_specs=(
            spread, vector, vector, qkv, qkv_bias, by_out, by_in, by_out, by_out, pair, spread,
        ),
        out_specs=(
            spread, spread, vector, vector, qkv, qkv_bias, by_out, by_in, by_out, by_out, pair,
        ),
        check_vma=False,
    )
```

```python
import functools
import math

import jax
import jax.numpy as jnp
from jax import lax
from jax.experimental import pallas as pl
from jax.experimental.pallas import tpu as pltpu
from jax.sharding import PartitionSpec as P

ROT = 16
EPS = 1e-05
ROOT_HALF = 0.7071067811865476
INV_ROOT_TAU = 0.3989422804014327
NEG_BIG = -1e30
F32 = jnp.float32
BF16 = jnp.bfloat16


def dot(a, b, contract, out=F32):
    return lax.dot_general(
        a, b, (((contract[0],), (contract[1],)), ((), ())), preferred_element_type=out
    )


def swap(x, axis_name, size, step):
    return lax.ppermute(x, axis_name, [(i, i ^ step) for i in range(size)])


def bit_of(axis_name, step):
    return (lax.axis_index(axis_name) // step) % 2


def gather_bits(x, size, axis, steps):
    done = []
    for step in steps:
        other = swap(x, "dp", size, step)
        mine_first = bit_of("dp", step) == 0
        low = jnp.where(mine_first, x, other)
        high = jnp.where(mine_first, other, x)
        place = axis + sum(1 for s in done if s > step)
        x = jnp.stack([low, high], axis=place)
        done.append(step)
    shape = x.shape
    levels = len(steps)
    return x.reshape(shape[:axis] + (size,) + shape[axis + levels :])


def scatter_bits(x, axis, steps, wire, size, unit):
    shape = x.shape
    levels = len(steps)
    x = x.reshape(shape[:axis] + (2,) * levels + shape[axis + 1 :])
    left = sorted(steps, reverse=True)
    for step in steps:
        place = axis + left.index(step)
        bit = bit_of("dp", step * unit)
        keep = lax.dynamic_index_in_dim(x, bit, place, keepdims=False)
        send = lax.dynamic_index_in_dim(x, 1 - bit, place, keepdims=False)
        got = swap(send.astype(wire), "dp", size, step * unit)
        x = keep + got.astype(F32)
        left.remove(step)
    return x


def rotate_rows(x, cosine, sine):
    half = ROT // 2
    first, second = x[:half], x[half:ROT]
    return jnp.concatenate(
        [first * cosine - second * sine, second * cosine + first * sine, x[ROT:]], axis=0
    )


def normalize(x):
    wide = x.astype(F32)
    centred = wide - jnp.mean(wide, axis=-1, keepdims=True)
    inv_sigma = lax.rsqrt(jnp.mean(centred * centred, axis=-1, keepdims=True) + EPS)
    return centred * inv_sigma, inv_sigma


def enter_kernel(
    heads, head_dim, qkv_cols, x_ref, vec_ref, in_bias_ref, qkv_bias_ref, first_ref, second_ref,
    cos_ref, sin_ref, normed_t_ref, proj_t_ref, hidden_ref, slope_ref,
):
    width = heads * head_dim
    unit, _ = normalize(x_ref[...])
    wide = unit * vec_ref[0:1] + vec_ref[1:2]
    normed = wide.astype(BF16)
    normed_t_ref[...] = jnp.transpose(normed)
    projected = dot(normed, second_ref[:, qkv_cols], (1, 0)) + qkv_bias_ref[...]
    projected = jnp.transpose(projected)
    cosine, sine = cos_ref[...], sin_ref[...]
    for place in range(2 * heads):
        rows = slice(place * head_dim, (place + 1) * head_dim)
        proj_t_ref[rows] = rotate_rows(projected[rows], cosine, sine).astype(BF16)
    proj_t_ref[2 * width :] = projected[2 * width :].astype(BF16)
    pre_act = dot(normed, first_ref[...], (1, 0)) + in_bias_ref[...]
    normal_cdf = 0.5 * (1.0 + lax.erf(pre_act * ROOT_HALF))
    normal_pdf = jnp.exp(-0.5 * pre_act * pre_act) * INV_ROOT_TAU
    hidden_ref[...] = (pre_act * normal_cdf).astype(BF16)
    slope_ref[...] = normal_cdf + pre_act * normal_pdf


def causal(block):
    key_pos = lax.broadcasted_iota(jnp.int32, (block, block), 0)
    query_pos = lax.broadcasted_iota(jnp.int32, (block, block), 1)
    return key_pos <= query_pos


def forward_kernel(scale, block, q_ref, k_ref, v_ref, ctx_ref, prob_ref):
    length = q_ref.shape[1]
    queries = q_ref[...] * jnp.asarray(scale, BF16)
    keys = jnp.transpose(k_ref[...])
    values = v_ref[...]
    allowed = causal(block)
    for step in range(length // block):
        here = slice(step * block, (step + 1) * block)
        before = slice(0, step * block)
        q_cols = queries[:, here]
        near = jnp.where(allowed, dot(keys[here], q_cols, (1, 0)), NEG_BIG)
        top = jnp.max(near, axis=0, keepdims=True)
        if step:
            far = dot(keys[before], q_cols, (1, 0))
            top = jnp.maximum(top, jnp.max(far, axis=0, keepdims=True))
        near = jnp.exp(near - top)
        total = jnp.sum(near, axis=0, keepdims=True)
        if step:
            far = jnp.exp(far - top)
            total = total + jnp.sum(far, axis=0, keepdims=True)
        inverse = 1.0 / total
        near = (near * inverse).astype(BF16)
        prob_ref[0, 0, here, here] = near
        context = dot(values[:, here], near, (1, 0))
        if step:
            far = (far * inverse).astype(BF16)
            prob_ref[0, 0, before, here] = far
            context = context + dot(values[:, before], far, (1, 0))
        ctx_ref[:, here] = context.astype(BF16)


def backward_kernel(
    scale, block, q_ref, k_ref, v_ref, cos_ref, sin_ref, prob_ref, grad_ref,
    dq_ref, dk_ref, dv_ref, sum_ref, keys_acc, values_acc,
):
    length = q_ref.shape[1]
    cosine, sine = cos_ref[...], sin_ref[...]
    query_rows = jnp.transpose(q_ref[...] * jnp.asarray(scale, BF16))
    keys_t = k_ref[...]
    values = jnp.transpose(v_ref[...])
    grad_t = grad_ref[...]
    grad_rows = jnp.transpose(grad_t)
    query_sum = 0.0
    for step in reversed(range(length // block)):
        here = slice(step * block, (step + 1) * block)
        upto = slice(0, (step + 1) * block)
        probs = prob_ref[0, 0, upto, here]
        value_part = dot(probs, grad_rows[here], (1, 0))
        prob_grad = dot(values[upto], grad_t[:, here], (1, 0))
        probs = probs.astype(F32)
        row_dot = jnp.sum(probs * prob_grad, axis=0, keepdims=True)
        score_grad = (probs * (prob_grad - row_dot)).astype(BF16)
        key_part = dot(score_grad, query_rows[here], (1, 0))
        if (step + 1) * block == length:
            values_acc[...] = value_part
            keys_acc[...] = key_part
        else:
            values_acc[upto, :] += value_part
            keys_acc[upto, :] += key_part
        dq = dot(keys_t[:, upto], score_grad, (1, 0)) * scale
        dq = rotate_rows(dq, cosine[:, here], -sine[:, here])
        dq_ref[:, here] = dq.astype(BF16)
        query_sum = query_sum + jnp.sum(dq, axis=1, keepdims=True)
    dk = rotate_rows(jnp.transpose(keys_acc[...]), cosine, -sine)
    dv = jnp.transpose(values_acc[...])
    dk_ref[...] = dk.astype(BF16)
    dv_ref[...] = dv.astype(BF16)
    sums = [query_sum, jnp.sum(dk, axis=1, keepdims=True), jnp.sum(dv, axis=1, keepdims=True)]
    for place, part in enumerate(sums):
        sum_ref[0, 0, place] = jnp.broadcast_to(part, (part.shape[0], 128))


def branch_kernel(out_cols, ctx_t_ref, hidden_ref, first_ref, second_ref, branch_ref, ctx_ref):
    context = jnp.transpose(ctx_t_ref[...])
    ctx_ref[...] = context
    total = dot(context, first_ref[:, out_cols], (1, 1))
    total = total + dot(hidden_ref[...], second_ref[...], (1, 1))
    branch_ref[...] = total.astype(BF16)


def row_sums(x):
    return jnp.sum(x.reshape(x.shape[0] // 8, 8, x.shape[1]), axis=0)


def return_kernel(
    out_cols, after_ref, cot_ref, slope_ref, first_ref, second_ref,
    cot_t_ref, ctx_grad_t_ref, pre_low_ref, in_sum_ref, cot_sum_ref,
):
    cot = cot_ref[...]
    cot_t_ref[...] = jnp.transpose(cot)
    ctx_grad = dot(cot, first_ref[:, out_cols], (1, 0))
    ctx_grad_t_ref[...] = jnp.transpose(ctx_grad).astype(BF16)
    pre_grad = dot(cot, second_ref[...], (1, 0)) * slope_ref[...]
    pre_low_ref[...] = pre_grad.astype(BF16)

    @pl.when(pl.program_id(0) == 0)
    def _():
        in_sum_ref[...] = jnp.zeros_like(in_sum_ref)
        cot_sum_ref[...] = jnp.zeros_like(cot_sum_ref)

    in_sum_ref[...] += row_sums(pre_grad)
    cot_sum_ref[...] += row_sums(cot.astype(F32))


def norm_kernel(
    qkv_cols, x_ref, dq_ref, dk_ref, dv_ref, pre_low_ref, first_ref, second_ref,
    proj_low_ref, norm_grad_ref, gain_sum_ref, shift_sum_ref,
):
    proj_low = jnp.transpose(
        jnp.concatenate([dq_ref[...], dk_ref[...], dv_ref[...]], axis=0)
    )
    proj_low_ref[...] = proj_low
    norm_grad = dot(proj_low, second_ref[:, qkv_cols], (1, 1))
    norm_grad = norm_grad + dot(pre_low_ref[...], first_ref[...], (1, 1))
    norm_grad_ref[...] = norm_grad.astype(BF16)
    unit, _ = normalize(x_ref[...])

    @pl.when(pl.program_id(0) == 0)
    def _():
        gain_sum_ref[...] = jnp.zeros_like(gain_sum_ref)
        shift_sum_ref[...] = jnp.zeros_like(shift_sum_ref)

    gain_sum_ref[...] += row_sums(norm_grad * unit)
    shift_sum_ref[...] += row_sums(norm_grad)


def half_rows(ref, at_ref, blocks, part):
    chips = [lax.bitwise_xor(at_ref[1], k) for k in range(blocks)]
    starts = [pl.multiple_of((2 * chip + at_ref[0]) * part, part) for chip in chips]
    return jnp.concatenate([ref[pl.ds(start, part), :] for start in starts], axis=0)


def put(outs, got_ref, columns, value):
    blocks, part = (outs[0].shape[0], outs[0].shape[1]) if got_ref is None else got_ref.shape[:2]
    value = value.reshape(blocks, part, -1)
    if got_ref is None:
        outs[0][:, :, columns] = value.astype(BF16)
        return
    value = value + got_ref[:, :, columns].astype(F32)
    for k in range(blocks):
        outs[k][:, columns] = value[k].astype(outs[k].dtype)


def early_kernel(blocks, part, at_ref, normed_t_ref, cot_t_ref, pre_low_ref, ctx_ref, hidden_ref, *refs):
    got_ref, outs = (None, refs) if len(refs) == 1 else (refs[0], refs[1:])
    units = hidden_ref.shape[1]
    left = half_rows(normed_t_ref, at_ref, blocks, part)
    put(outs, got_ref, slice(0, units), dot(left, pre_low_ref[...], (1, 0)))
    left = half_rows(cot_t_ref, at_ref, blocks, part)
    put(outs, got_ref, slice(units, 2 * units), dot(left, hidden_ref[...], (1, 0)))
    put(outs, got_ref, slice(2 * units, None), dot(left, ctx_ref[...], (1, 0)))


def late_kernel(blocks, part, at_ref, normed_t_ref, proj_low_ref, *refs):
    got_ref, outs = (None, refs) if len(refs) == 1 else (refs[0], refs[1:])
    left = half_rows(normed_t_ref, at_ref, blocks, part)
    put(outs, got_ref, slice(None), dot(left, proj_low_ref[...], (1, 0)))


def whole(x):
    return pl.BlockSpec(x.shape, lambda *_: (0,) * x.ndim)


def tokens(block, columns):
    return pl.BlockSpec((block, columns), lambda t: (t, 0))


def tokens_t(rows, block):
    return pl.BlockSpec((rows, block), lambda t: (0, t))


def columns(x, start, count):
    for wide in range(-(-count // 128) * 128, start + 1, 128):
        if start % wide == 0:
            return pl.BlockSpec((x.shape[0], wide), lambda *_: (0, start // wide)), slice(0, count)
    if start == 0:
        return pl.BlockSpec((x.shape[0], count), lambda *_: (0, 0)), slice(0, count)
    return whole(x), slice(start, start + count)


def cost(flops, nbytes, trans=0):
    return pl.CostEstimate(flops=flops, bytes_accessed=nbytes, transcendentals=trans)


def struct(*shape, dtype=BF16):
    return jax.ShapeDtypeStruct(shape, dtype)


def enter(x, vectors, in_bias, qkv_bias, first, second, cosine, sine, heads, head_dim):
    rows, model = x.shape
    hidden_units = in_bias.shape[1]
    proj = 3 * heads * head_dim
    block = min(256, rows)
    per_seq = cosine.shape[1] // block
    table = pl.BlockSpec((ROT // 2, block), lambda t: (0, lax.rem(t, per_seq)))
    first_spec, _ = columns(first, 0, hidden_units)
    second_spec, qkv_cols = columns(second, hidden_units, proj)
    return pl.pallas_call(
        functools.partial(enter_kernel, heads, head_dim, qkv_cols),
        grid=(rows // block,),
        in_specs=[
            tokens(block, model), whole(vectors), whole(in_bias), whole(qkv_bias),
            first_spec, second_spec, table, table,
        ],
        out_specs=[
            tokens_t(model, block), tokens_t(proj, block),
            tokens(block, hidden_units), tokens(block, hidden_units),
        ],
        out_shape=[
            struct(model, rows), struct(proj, rows),
            struct(rows, hidden_units), struct(rows, hidden_units, dtype=F32),
        ],
        cost_estimate=cost(
            2 * rows * model * (proj + hidden_units), 2 * (first.size + second.size) + 12 * x.size,
            2 * rows * hidden_units,
        ),
        name="enter",
    )(x, vectors, in_bias, qkv_bias, first, second, cosine, sine)


def attend(proj_t, seqs, heads, head_dim, length):
    block = min(256, length)
    scale = 1.0 / math.sqrt(head_dim)

    def part(which):
        return pl.BlockSpec((head_dim, length), lambda s, h: (which * heads + h, s))

    prob_spec = pl.BlockSpec((1, 1, length, length), lambda s, h: (s, h, 0, 0))
    work = seqs * heads * length * length
    return pl.pallas_call(
        functools.partial(forward_kernel, scale, block),
        grid=(seqs, heads),
        in_specs=[part(0), part(1), part(2)],
        out_specs=[part(0), prob_spec],
        out_shape=[
            struct(heads * head_dim, seqs * length),
            struct(seqs, heads, length, length),
        ],
        cost_estimate=cost(4 * work * head_dim, proj_t.size * 4, work),
        name="attend_forward",
    )(proj_t, proj_t, proj_t)


def attend_back(proj_t, cosine, sine, probs, ctx_grad_t, seqs, heads, head_dim, length):
    block = min(256, length)
    scale = 1.0 / math.sqrt(head_dim)

    def part(which):
        return pl.BlockSpec((head_dim, length), lambda s, h: (which * heads + h, s))

    table = pl.BlockSpec((ROT // 2, length), lambda s, h: (0, 0))
    prob_spec = pl.BlockSpec((1, 1, length, length), lambda s, h: (s, h, 0, 0))
    sum_spec = pl.BlockSpec((1, 1, 3, head_dim, 128), lambda s, h: (s, h, 0, 0, 0))
    flat = struct(heads * head_dim, seqs * length)
    work = seqs * heads * length * length
    return pl.pallas_call(
        functools.partial(backward_kernel, scale, block),
        grid=(seqs, heads),
        in_specs=[part(0), part(1), part(2), table, table, prob_spec, part(0)],
        out_specs=[part(0), part(0), part(0), sum_spec],
        out_shape=[flat, flat, flat, struct(seqs, heads, 3, head_dim, 128, dtype=F32)],
        scratch_shapes=[pltpu.VMEM((length, head_dim), F32)] * 2,
        cost_estimate=cost(10 * work * head_dim, proj_t.size * 6, work),
        name="attend_backward",
    )(proj_t, proj_t, proj_t, cosine, sine, probs, ctx_grad_t)


def branch_sum(ctx_t, hidden, first, second):
    width, rows = ctx_t.shape
    hidden_units = hidden.shape[1]
    model = first.shape[0]
    block = min(256, rows)
    first_spec, out_cols = columns(first, hidden_units, width)
    second_spec, _ = columns(second, 0, hidden_units)
    return pl.pallas_call(
        functools.partial(branch_kernel, out_cols),
        grid=(rows // block,),
        in_specs=[
            tokens_t(width, block), tokens(block, hidden_units), first_spec, second_spec,
        ],
        out_specs=[tokens(block, model), tokens(block, width)],
        out_shape=[struct(rows, model), struct(rows, width)],
        cost_estimate=cost(2 * rows * model * (width + hidden_units), 8 * rows * model),
        name="branch",
    )(ctx_t, hidden, first, second)


def return_grads(after, cot, slopes, first, second, width):
    rows, model = cot.shape
    hidden_units = slopes.shape[1]
    block = min(256, rows)
    first_spec, out_cols = columns(first, hidden_units, width)
    second_spec, _ = columns(second, 0, hidden_units)
    return pl.pallas_call(
        functools.partial(return_kernel, out_cols),
        grid=(rows // block,),
        in_specs=[
            pl.BlockSpec(memory_space=pl.ANY), tokens(block, model), tokens(block, hidden_units), first_spec, second_spec,
        ],
        out_specs=[
            tokens_t(model, block), tokens_t(width, block), tokens(block, hidden_units),
            pl.BlockSpec((8, hidden_units), lambda t: (0, 0)),
            pl.BlockSpec((8, model), lambda t: (0, 0)),
        ],
        out_shape=[
            struct(model, rows), struct(width, rows), struct(rows, hidden_units),
            struct(8, hidden_units, dtype=F32), struct(8, model, dtype=F32),
        ],
        cost_estimate=cost(2 * rows * model * (width + hidden_units), 10 * rows * model),
        name="return_grads",
    )(after, cot, slopes, first, second)


def norm_sum(x, dq_t, dk_t, dv_t, pre_low, first, second):
    rows, model = x.shape
    width = dq_t.shape[0]
    hidden_units = pre_low.shape[1]
    block = min(256, rows)
    first_spec, _ = columns(first, 0, hidden_units)
    second_spec, qkv_cols = columns(second, hidden_units, 3 * width)
    return pl.pallas_call(
        functools.partial(norm_kernel, qkv_cols),
        grid=(rows // block,),
        in_specs=[
            tokens(block, model), tokens_t(width, block), tokens_t(width, block),
            tokens_t(width, block), tokens(block, hidden_units), first_spec, second_spec,
        ],
        out_specs=[
            tokens(block, 3 * width), tokens(block, model),
            pl.BlockSpec((8, model), lambda t: (0, 0)),
            pl.BlockSpec((8, model), lambda t: (0, 0)),
        ],
        out_shape=[
            struct(rows, 3 * width), struct(rows, model),
            struct(8, model, dtype=F32), struct(8, model, dtype=F32),
        ],
        cost_estimate=cost(2 * rows * model * (3 * width + hidden_units), 8 * rows * model),
        name="norm_grads",
    )(x, dq_t, dk_t, dv_t, pre_low, first, second)


def finish_kernel(x_ref, cot_ref, own_ref, gain_ref, grad_ref):
    unit, inv_sigma = normalize(x_ref[0])
    unit_grad = own_ref[0].astype(F32) * gain_ref[...]
    grad = cot_ref[0].astype(F32) + inv_sigma * (
        unit_grad
        - jnp.mean(unit_grad, axis=-1, keepdims=True)
        - unit * jnp.mean(unit_grad * unit, axis=-1, keepdims=True)
    )
    grad_ref[0] = grad.astype(BF16)


def finish(x, cot, own, gain):
    rows = pl.BlockSpec((1, x.shape[1] // 2, x.shape[2]), lambda s, t: (s, t, 0))
    return pl.pallas_call(
        finish_kernel,
        grid=(x.shape[0], 2),
        in_specs=[rows, rows, rows, pl.BlockSpec(gain.shape, lambda *_: (0, 0))],
        out_specs=rows,
        out_shape=struct(*x.shape),
        cost_estimate=cost(20 * x.size, 8 * x.size),
        name="finish",
    )(x, cot, own, gain)


def weight_half(kernel, at, operands, got, blocks, part, shape, flops):
    if got is None:
        outs = [struct(blocks, *shape)]
    else:
        operands = operands + (got,)
        outs = [struct(*shape, dtype=F32)] + [struct(*shape)] * (blocks - 1)
    return pl.pallas_call(
        functools.partial(kernel, blocks, part),
        grid_spec=pltpu.PrefetchScalarGridSpec(
            num_scalar_prefetch=1,
            grid=(1,),
            in_specs=[whole(x) for x in operands],
            out_specs=[whole(x) for x in outs],
        ),
        out_shape=outs,
        cost_estimate=cost(flops, 4 * operands[0].size),
    )(jnp.stack(at).astype(jnp.int32), *operands)


def rotary_tables(length):
    half_rot = ROT // 2
    position = jnp.arange(length).astype(F32)
    inv_freq = jnp.exp(jnp.arange(half_rot).astype(F32) * (-2.0 * math.log(10000.0) / ROT))
    angles = inv_freq[:, None] * position[None, :]
    return jnp.cos(angles), jnp.sin(angles)


def split_core(grad, dp):
    core = bit_of("dp", 1)
    grad = grad.reshape(dp // 2, 2, -1, grad.shape[-1])
    kept = lax.dynamic_index_in_dim(grad, core, 1, keepdims=False)
    sent = lax.dynamic_index_in_dim(grad, 1 - core, 1, keepdims=False)
    return kept, sent.astype(BF16)


def swap_core(sent, dp):
    return swap(sent, "dp", dp, 1)


def add_pieces(pieces, dp):
    total = pieces[0]
    for k in range(1, len(pieces)):
        got = swap(pieces[k], "dp", dp, 2 * k)
        total = total + got.astype(F32)
    return total


def exchange_small(small, dp):
    core, chip = bit_of("dp", 1), lax.axis_index("dp") // 2
    count = dp // 2
    small = small.reshape(count, 2, -1)
    kept = lax.dynamic_index_in_dim(small, core, 1, keepdims=False)
    sent = lax.dynamic_index_in_dim(small, 1 - core, 1, keepdims=False)
    got = swap_core(sent, dp)
    x = kept + got
    if count > 4:
        steps = [1 << b for b in range(count.bit_length() - 1)]
        return scatter_bits(x, 0, steps[::-1], F32, dp, 2)
    pieces = [
        lax.dynamic_index_in_dim(x, chip ^ k, 0, keepdims=False) for k in range(count)
    ]
    return add_pieces(pieces, dp)


def exchange(grad, dp):
    kept, sent = split_core(grad, dp)
    x = kept + swap_core(sent, dp).astype(F32)
    steps = [1 << b for b in range((dp // 2).bit_length() - 1)]
    return scatter_bits(x, 0, steps[::-1], BF16, dp, 2)


def body(
    dp, tensor, inputs, ln_gain, ln_bias, w_qkv, b_qkv, w_out, w_in, b_in, w_down, out_bias,
    cotangent,
):
    model = inputs.shape[-1]
    heads, head_dim = b_qkv.shape[1], b_qkv.shape[2] * dp
    width = heads * head_dim
    hidden_units = w_in.shape[1]
    seqs, length = inputs.shape[0], inputs.shape[1] * tensor
    rows = seqs * length
    own = ln_gain.shape[0]
    share = own * tensor
    slow = [1 << b for b in range(1, dp.bit_length() - 1)]
    ways = (slow + [1], slow[::-1] + [1])
    me_z = lax.axis_index("tensor")

    full_in = lax.all_gather(inputs, "tensor", axis=1, tiled=True).reshape(rows, model)
    full_cot = lax.all_gather(cotangent, "tensor", axis=1, tiled=True).reshape(rows, model)

    vector = jnp.stack([ln_gain, ln_bias, out_bias[0] + out_bias[1]])
    by_z = [vector]
    for k in range(1, tensor):
        by_z.append(
            lax.ppermute(vector, "tensor", [(i, (i + k) % tensor) for i in range(tensor)])
        )
    by_z = jnp.stack(by_z)
    order = (me_z - jnp.arange(tensor)) % tensor
    by_z = jnp.take(by_z, order, axis=0).transpose(1, 0, 2)
    small = jnp.concatenate(
        [by_z.reshape(-1), b_qkv.astype(F32).reshape(-1), b_in.astype(F32).reshape(-1)]
    )
    used = small.shape[0]
    padded = -(-used // 1024) * 1024
    small = jnp.pad(small, (0, padded - used)).reshape(-1, 128)
    small = gather_bits(small, dp, 0, ways[0]).reshape(dp, padded)
    norm_rows = small[:, : 3 * share].reshape(dp, 3, share).transpose(1, 0, 2).reshape(3, model)
    gain, out_shift = norm_rows[0], norm_rows[2]
    at = 3 * share
    qkv_count = b_qkv.size
    qkv_bias = (
        small[:, at : at + qkv_count]
        .reshape(dp, 3, heads, head_dim // dp)
        .transpose(1, 2, 0, 3)
        .reshape(3 * width)
    )
    at += qkv_count
    in_groups, in_each = b_in.shape
    in_bias = (
        small[:, at : at + b_in.size]
        .reshape(dp, in_groups, in_each)
        .transpose(1, 0, 2)
        .reshape(hidden_units)
    )

    first = gather_bits(jnp.concatenate([w_in, w_out.T], axis=1), dp, 0, ways[0])
    second = gather_bits(
        jnp.concatenate([w_down.T, w_qkv.reshape(w_qkv.shape[0], -1)], axis=1), dp, 0, ways[1],
    )
    first = first.reshape(model, -1)
    second = second.reshape(model, -1)

    cosine, sine = rotary_tables(length)
    normed_t, proj_t, hidden, slopes = enter(
        full_in, norm_rows, in_bias.reshape(1, -1), qkv_bias.reshape(1, -1), first, second,
        cosine, sine, heads, head_dim,
    )
    ctx_t, probs = attend(proj_t, seqs, heads, head_dim, length)
    branch, context = branch_sum(ctx_t, hidden, first, second)
    summed = lax.psum_scatter(
        branch.reshape(seqs, length, model), "tensor", scatter_dimension=1, tiled=True
    )
    outputs = (inputs.astype(F32) + summed.astype(F32) + out_shift).astype(BF16)

    cot_t, ctx_grad_t, pre_low, in_sum, cot_sum = return_grads(
        context, full_cot, slopes, first, second, width
    )
    part = model // dp
    core = bit_of("dp", 1)
    aligned = 2 <= dp <= 8 and part % 16 == 0
    chip = lax.axis_index("dp") // 2
    blocks = dp // 2
    if aligned:
        operands = (normed_t, cot_t, pre_low, context, hidden)
        shape = (part, 2 * hidden_units + width)
        flops = rows * model * shape[1]
        (early_sent,) = weight_half(
            early_kernel, (1 - core, chip), operands, None, blocks, part, shape, flops
        )
        early_got = swap_core(early_sent, dp)
        early_pieces = weight_half(
            early_kernel, (core, chip), operands, early_got, blocks, part,
            shape, flops,
        )
        early = add_pieces(early_pieces, dp)
    else:
        early = jnp.concatenate(
            [
                dot(normed_t, pre_low, (1, 0)),
                dot(cot_t, hidden, (1, 0)),
                dot(cot_t, context, (1, 0)),
            ],
            axis=1,
        )
        early = exchange(early, dp)
    dq_t, dk_t, dv_t, sums = attend_back(
        proj_t, cosine, sine, probs, ctx_grad_t, seqs, heads, head_dim, length
    )
    proj_low, norm_grad, gain_sum, shift_sum = norm_sum(
        full_in, dq_t, dk_t, dv_t, pre_low, first, second
    )
    own_grad = lax.psum_scatter(
        norm_grad.reshape(seqs, length, model), "tensor", scatter_dimension=1, tiled=True
    )
    grad_qkv_bias = jnp.sum(sums[..., 0], axis=0).transpose(1, 0, 2)
    grad_in_bias = jnp.sum(in_sum, axis=0)
    bias_part = jnp.sum(cot_sum, axis=0).reshape(dp, tensor, own)
    pair = jnp.stack([gain_sum, shift_sum]).sum(axis=1).reshape(2, dp, tensor, own)
    pair_total = lax.dynamic_index_in_dim(pair, me_z, 2, keepdims=False)
    for k in range(1, tensor):
        piece = lax.dynamic_index_in_dim(pair, (me_z + k) % tensor, 2, keepdims=False)
        got = lax.ppermute(
            piece, "tensor", [(i, (i + k) % tensor) for i in range(tensor)]
        )
        pair_total = pair_total + got
    bias_total = lax.dynamic_index_in_dim(bias_part, me_z, 1, keepdims=False)
    small = jnp.concatenate(
        [
            pair_total[0], pair_total[1], bias_total,
            grad_qkv_bias.reshape(3, heads, dp, head_dim // dp)
            .transpose(2, 0, 1, 3)
            .reshape(dp, -1),
            grad_in_bias.reshape(in_groups, dp, in_each).transpose(1, 0, 2).reshape(dp, -1),
        ],
        axis=1,
    )
    small = exchange_small(
        jnp.pad(small, ((0, 0), (0, -small.shape[1] % 128))), dp
    )
    if aligned:
        operands = (normed_t, proj_low)
        shape = (part, 3 * width)
        flops = rows * model * shape[1]
        (late_sent,) = weight_half(
            late_kernel, (1 - core, chip), operands, None, blocks, part, shape,
            flops,
        )
        late_got = swap_core(late_sent, dp)
        late_pieces = weight_half(
            late_kernel, (core, chip), operands, late_got, blocks, part, shape,
            flops,
        )
        late = add_pieces(late_pieces, dp)
    else:
        late = exchange(dot(normed_t, proj_low, (1, 0)), dp)
    in_out = early[:, :hidden_units]
    down_out = early[:, hidden_units : 2 * hidden_units].T
    out_out = early[:, 2 * hidden_units :].T
    qkv_out = late.reshape(part, 3, width)
    gain_out, shift_out, bias_out = (small[k * own : (k + 1) * own] for k in range(3))
    bias_grad = jnp.stack([bias_out, bias_out])
    at = 3 * own
    qkv_bias_out = small[at : at + qkv_count].reshape(b_qkv.shape)
    at += qkv_count
    in_bias_out = small[at : at + b_in.size].reshape(b_in.shape)

    input_grad = finish(inputs, cotangent, own_grad, gain.reshape(1, model))
    return (
        outputs,
        input_grad,
        gain_out,
        shift_out,
        qkv_out,
        qkv_bias_out,
        out_out,
        in_out,
        in_bias_out,
        down_out,
        bias_grad,
    )


def solution(mesh):
    spread = P("dp", "tensor", None)
    vector = P(("dp", "tensor"))
    qkv, qkv_bias = P("dp", None, "tensor"), P(None, "tensor", "dp")
    by_out, by_in, pair = P("tensor", "dp"), P("dp", "tensor"), P(None, ("dp", "tensor"))

    def layer(*arrays):
        return body(mesh.shape["dp"], mesh.shape["tensor"], *arrays)

    return jax.shard_map(
        layer,
        mesh=mesh,
        in_specs=(
            spread, vector, vector, qkv, qkv_bias, by_out, by_in, by_out, by_out, pair, spread,
        ),
        out_specs=(
            spread, spread, vector, vector, qkv, qkv_bias, by_out, by_in, by_out, by_out, pair,
        ),
        check_vma=False,
    )
```

```python
import functools
import math

import jax
import jax.numpy as jnp
from jax import lax
from jax.experimental import pallas as pl
from jax.experimental.pallas import tpu as pltpu
from jax.sharding import PartitionSpec as P

ROT = 16
EPS = 1e-05
ROOT_HALF = 0.7071067811865476
INV_ROOT_TAU = 0.3989422804014327
NEG_BIG = -1e30
F32 = jnp.float32
BF16 = jnp.bfloat16


def dot(a, b, contract, out=F32):
    return lax.dot_general(
        a, b, (((contract[0],), (contract[1],)), ((), ())), preferred_element_type=out
    )


def swap(x, axis_name, size, step):
    return lax.ppermute(x, axis_name, [(i, i ^ step) for i in range(size)])


def bit_of(axis_name, step):
    return (lax.axis_index(axis_name) // step) % 2


def gather_bits(x, size, axis, steps):
    done = []
    for step in steps:
        other = swap(x, "dp", size, step)
        mine_first = bit_of("dp", step) == 0
        low = jnp.where(mine_first, x, other)
        high = jnp.where(mine_first, other, x)
        place = axis + sum(1 for s in done if s > step)
        x = jnp.stack([low, high], axis=place)
        done.append(step)
    shape = x.shape
    levels = len(steps)
    return x.reshape(shape[:axis] + (size,) + shape[axis + levels :])


def scatter_bits(x, axis, steps, wire, size, unit):
    shape = x.shape
    levels = len(steps)
    x = x.reshape(shape[:axis] + (2,) * levels + shape[axis + 1 :])
    left = sorted(steps, reverse=True)
    for step in steps:
        place = axis + left.index(step)
        bit = bit_of("dp", step * unit)
        keep = lax.dynamic_index_in_dim(x, bit, place, keepdims=False)
        send = lax.dynamic_index_in_dim(x, 1 - bit, place, keepdims=False)
        got = swap(send.astype(wire), "dp", size, step * unit)
        x = keep + got.astype(F32)
        left.remove(step)
    return x


def rotate_rows(x, cosine, sine):
    half = ROT // 2
    first, second = x[:half], x[half:ROT]
    return jnp.concatenate(
        [first * cosine - second * sine, second * cosine + first * sine, x[ROT:]], axis=0
    )


def normalize(x):
    wide = x.astype(F32)
    centred = wide - jnp.mean(wide, axis=-1, keepdims=True)
    inv_sigma = lax.rsqrt(jnp.mean(centred * centred, axis=-1, keepdims=True) + EPS)
    return centred * inv_sigma, inv_sigma


def enter_kernel(
    heads, head_dim, qkv_cols, x_ref, vec_ref, in_bias_ref, qkv_bias_ref, first_ref, second_ref,
    cos_ref, sin_ref, unit_ref, normed_t_ref, proj_t_ref, hidden_ref, slope_ref,
):
    width = heads * head_dim
    unit, _ = normalize(x_ref[...])
    unit_ref[...] = unit.astype(BF16)
    wide = unit * vec_ref[0:1] + vec_ref[1:2]
    normed = wide.astype(BF16)
    normed_t_ref[...] = jnp.transpose(normed)
    projected = dot(normed, second_ref[:, qkv_cols], (1, 0)) + qkv_bias_ref[...]
    projected = jnp.transpose(projected)
    cosine, sine = cos_ref[...], sin_ref[...]
    for place in range(2 * heads):
        rows = slice(place * head_dim, (place + 1) * head_dim)
        proj_t_ref[rows] = rotate_rows(projected[rows], cosine, sine).astype(BF16)
    proj_t_ref[2 * width :] = projected[2 * width :].astype(BF16)
    pre_act = dot(normed, first_ref[...], (1, 0)) + in_bias_ref[...]
    normal_cdf = 0.5 * (1.0 + lax.erf(pre_act * ROOT_HALF))
    normal_pdf = jnp.exp(-0.5 * pre_act * pre_act) * INV_ROOT_TAU
    hidden_ref[...] = (pre_act * normal_cdf).astype(BF16)
    slope_ref[...] = normal_cdf + pre_act * normal_pdf


def causal(block):
    key_pos = lax.broadcasted_iota(jnp.int32, (block, block), 0)
    query_pos = lax.broadcasted_iota(jnp.int32, (block, block), 1)
    return key_pos <= query_pos


def forward_kernel(scale, block, q_ref, k_ref, v_ref, ctx_ref, prob_ref):
    length = q_ref.shape[1]
    queries = q_ref[...] * jnp.asarray(scale, BF16)
    keys = jnp.transpose(k_ref[...])
    values = v_ref[...]
    allowed = causal(block)
    for step in range(length // block):
        here = slice(step * block, (step + 1) * block)
        before = slice(0, step * block)
        q_cols = queries[:, here]
        near = jnp.where(allowed, dot(keys[here], q_cols, (1, 0)), NEG_BIG)
        top = jnp.max(near, axis=0, keepdims=True)
        if step:
            far = dot(keys[before], q_cols, (1, 0))
            top = jnp.maximum(top, jnp.max(far, axis=0, keepdims=True))
        near = jnp.exp(near - top)
        total = jnp.sum(near, axis=0, keepdims=True)
        if step:
            far = jnp.exp(far - top)
            total = total + jnp.sum(far, axis=0, keepdims=True)
        inverse = 1.0 / total
        near = (near * inverse).astype(BF16)
        prob_ref[0, 0, here, here] = near
        context = dot(values[:, here], near, (1, 0))
        if step:
            far = (far * inverse).astype(BF16)
            prob_ref[0, 0, before, here] = far
            context = context + dot(values[:, before], far, (1, 0))
        ctx_ref[:, here] = context.astype(BF16)


def backward_kernel(
    scale, block, q_ref, k_ref, v_ref, cos_ref, sin_ref, prob_ref, grad_ref,
    dq_ref, dk_ref, dv_ref, sum_ref, keys_acc, values_acc,
):
    length = q_ref.shape[1]
    cosine, sine = cos_ref[...], sin_ref[...]
    query_rows = jnp.transpose(q_ref[...] * jnp.asarray(scale, BF16))
    keys_t = k_ref[...]
    values = jnp.transpose(v_ref[...])
    grad_t = grad_ref[...]
    grad_rows = jnp.transpose(grad_t)
    query_sum = 0.0
    for step in reversed(range(length // block)):
        here = slice(step * block, (step + 1) * block)
        upto = slice(0, (step + 1) * block)
        probs = prob_ref[0, 0, upto, here]
        value_part = dot(probs, grad_rows[here], (1, 0))
        prob_grad = dot(values[upto], grad_t[:, here], (1, 0))
        probs = probs.astype(F32)
        row_dot = jnp.sum(probs * prob_grad, axis=0, keepdims=True)
        score_grad = (probs * (prob_grad - row_dot)).astype(BF16)
        key_part = dot(score_grad, query_rows[here], (1, 0))
        if (step + 1) * block == length:
            values_acc[...] = value_part
            keys_acc[...] = key_part
        else:
            values_acc[upto, :] += value_part
            keys_acc[upto, :] += key_part
        dq = dot(keys_t[:, upto], score_grad, (1, 0)) * scale
        dq = rotate_rows(dq, cosine[:, here], -sine[:, here])
        dq_ref[:, here] = dq.astype(BF16)
        query_sum = query_sum + jnp.sum(dq, axis=1, keepdims=True)
    dk = rotate_rows(jnp.transpose(keys_acc[...]), cosine, -sine)
    dv = jnp.transpose(values_acc[...])
    dk_ref[...] = dk.astype(BF16)
    dv_ref[...] = dv.astype(BF16)
    sums = [query_sum, jnp.sum(dk, axis=1, keepdims=True), jnp.sum(dv, axis=1, keepdims=True)]
    for place, part in enumerate(sums):
        sum_ref[0, 0, place] = jnp.broadcast_to(part, (part.shape[0], 128))


def branch_kernel(out_cols, ctx_t_ref, hidden_ref, first_ref, second_ref, branch_ref, ctx_ref):
    context = jnp.transpose(ctx_t_ref[...])
    ctx_ref[...] = context
    total = dot(context, first_ref[:, out_cols], (1, 1))
    total = total + dot(hidden_ref[...], second_ref[...], (1, 1))
    branch_ref[...] = total.astype(BF16)


def row_sums(x):
    return jnp.sum(x.reshape(x.shape[0] // 8, 8, x.shape[1]), axis=0)


def return_kernel(
    out_cols, after_ref, places_ref, cot_ref, slope_ref, first_ref, second_ref,
    cot_t_ref, ctx_grad_t_ref, pre_low_ref, in_sum_ref, cot_sum_ref,
):
    cot = cot_ref[...]
    cot_t_ref[...] = jnp.transpose(cot)
    ctx_grad = dot(cot, first_ref[:, out_cols], (1, 0))
    ctx_grad_t_ref[...] = jnp.transpose(ctx_grad).astype(BF16)
    pre_grad = dot(cot, second_ref[...], (1, 0)) * slope_ref[...]
    pre_low_ref[...] = pre_grad.astype(BF16)

    @pl.when(pl.program_id(0) == 0)
    def _():
        in_sum_ref[...] = jnp.zeros_like(in_sum_ref)
        cot_sum_ref[...] = jnp.zeros_like(cot_sum_ref)

    in_sum_ref[...] += row_sums(pre_grad)
    cot_sum_ref[...] += row_sums(cot.astype(F32))


def norm_kernel(
    qkv_cols, unit_ref, dq_ref, dk_ref, dv_ref, pre_low_ref, first_ref, second_ref,
    proj_low_ref, norm_grad_ref, gain_sum_ref, shift_sum_ref,
):
    proj_low = jnp.transpose(
        jnp.concatenate([dq_ref[...], dk_ref[...], dv_ref[...]], axis=0)
    )
    proj_low_ref[...] = proj_low
    norm_grad = dot(proj_low, second_ref[:, qkv_cols], (1, 1))
    norm_grad = norm_grad + dot(pre_low_ref[...], first_ref[...], (1, 1))
    norm_grad_ref[...] = norm_grad.astype(BF16)
    unit = unit_ref[...].astype(F32)

    @pl.when(pl.program_id(0) == 0)
    def _():
        gain_sum_ref[...] = jnp.zeros_like(gain_sum_ref)
        shift_sum_ref[...] = jnp.zeros_like(shift_sum_ref)

    gain_sum_ref[...] += row_sums(norm_grad * unit)
    shift_sum_ref[...] += row_sums(norm_grad)


def half_rows(ref, places_ref, row, blocks, part):
    chips = [lax.bitwise_xor(places_ref[1], k) for k in range(blocks)]
    starts = [pl.multiple_of((2 * chip + places_ref[2 * row]) * part, part) for chip in chips]
    return jnp.concatenate([ref[pl.ds(start, part), :] for start in starts], axis=0)


def put(outs, got_ref, columns, value):
    blocks, part = (outs[0].shape[0], outs[0].shape[1]) if got_ref is None else got_ref.shape[:2]
    value = value.reshape(blocks, part, -1)
    if got_ref is None:
        outs[0][:, :, columns] = value.astype(BF16)
        return
    value = value + got_ref[:, :, columns].astype(F32)
    for k in range(blocks):
        outs[k][:, columns] = value[k].astype(outs[k].dtype)


def early_kernel(blocks, part, row, at_ref, normed_t_ref, cot_t_ref, pre_low_ref, ctx_ref, hidden_ref, *refs):
    got_ref, outs = (None, refs) if len(refs) == 1 else (refs[0], refs[1:])
    units = hidden_ref.shape[1]
    left = half_rows(normed_t_ref, at_ref, row, blocks, part)
    put(outs, got_ref, slice(0, units), dot(left, pre_low_ref[...], (1, 0)))
    left = half_rows(cot_t_ref, at_ref, row, blocks, part)
    put(outs, got_ref, slice(units, 2 * units), dot(left, hidden_ref[...], (1, 0)))
    put(outs, got_ref, slice(2 * units, None), dot(left, ctx_ref[...], (1, 0)))


def late_kernel(blocks, part, row, at_ref, normed_t_ref, proj_low_ref, *refs):
    got_ref, outs = (None, refs) if len(refs) == 1 else (refs[0], refs[1:])
    left = half_rows(normed_t_ref, at_ref, row, blocks, part)
    put(outs, got_ref, slice(None), dot(left, proj_low_ref[...], (1, 0)))


def whole(x):
    return pl.BlockSpec(x.shape, lambda *_: (0,) * x.ndim)


def tokens(block, columns):
    return pl.BlockSpec((block, columns), lambda t: (t, 0))


def tokens_t(rows, block):
    return pl.BlockSpec((rows, block), lambda t: (0, t))


def columns(x, start, count):
    for wide in range(-(-count // 128) * 128, start + 1, 128):
        if start % wide == 0:
            return pl.BlockSpec((x.shape[0], wide), lambda *_: (0, start // wide)), slice(0, count)
    if start == 0:
        return pl.BlockSpec((x.shape[0], count), lambda *_: (0, 0)), slice(0, count)
    return whole(x), slice(start, start + count)


def cost(flops, nbytes, trans=0):
    return pl.CostEstimate(flops=flops, bytes_accessed=nbytes, transcendentals=trans)


def struct(*shape, dtype=BF16):
    return jax.ShapeDtypeStruct(shape, dtype)


def enter(x, vectors, in_bias, qkv_bias, first, second, cosine, sine, heads, head_dim):
    rows, model = x.shape
    hidden_units = in_bias.shape[1]
    proj = 3 * heads * head_dim
    block = min(256, rows)
    per_seq = cosine.shape[1] // block
    table = pl.BlockSpec((ROT // 2, block), lambda t: (0, lax.rem(t, per_seq)))
    first_spec, _ = columns(first, 0, hidden_units)
    second_spec, qkv_cols = columns(second, hidden_units, proj)
    return pl.pallas_call(
        functools.partial(enter_kernel, heads, head_dim, qkv_cols),
        grid=(rows // block,),
        in_specs=[
            tokens(block, model), whole(vectors), whole(in_bias), whole(qkv_bias),
            first_spec, second_spec, table, table,
        ],
        out_specs=[
            tokens(block, model), tokens_t(model, block), tokens_t(proj, block),
            tokens(block, hidden_units), tokens(block, hidden_units),
        ],
        out_shape=[
            struct(rows, model), struct(model, rows), struct(proj, rows),
            struct(rows, hidden_units), struct(rows, hidden_units, dtype=F32),
        ],
        cost_estimate=cost(
            2 * rows * model * (proj + hidden_units), 2 * (first.size + second.size) + 12 * x.size,
            2 * rows * hidden_units,
        ),
        name="enter",
    )(x, vectors, in_bias, qkv_bias, first, second, cosine, sine)


def attend(proj_t, seqs, heads, head_dim, length):
    block = min(256, length)
    scale = 1.0 / math.sqrt(head_dim)

    def part(which):
        return pl.BlockSpec((head_dim, length), lambda s, h: (which * heads + h, s))

    prob_spec = pl.BlockSpec((1, 1, length, length), lambda s, h: (s, h, 0, 0))
    work = seqs * heads * length * length
    return pl.pallas_call(
        functools.partial(forward_kernel, scale, block),
        grid=(seqs, heads),
        in_specs=[part(0), part(1), part(2)],
        out_specs=[part(0), prob_spec],
        out_shape=[
            struct(heads * head_dim, seqs * length),
            struct(seqs, heads, length, length),
        ],
        cost_estimate=cost(4 * work * head_dim, proj_t.size * 4, work),
        name="attend_forward",
    )(proj_t, proj_t, proj_t)


def attend_back(proj_t, cosine, sine, probs, ctx_grad_t, seqs, heads, head_dim, length):
    block = min(256, length)
    scale = 1.0 / math.sqrt(head_dim)

    def part(which):
        return pl.BlockSpec((head_dim, length), lambda s, h: (which * heads + h, s))

    table = pl.BlockSpec((ROT // 2, length), lambda s, h: (0, 0))
    prob_spec = pl.BlockSpec((1, 1, length, length), lambda s, h: (s, h, 0, 0))
    sum_spec = pl.BlockSpec((1, 1, 3, head_dim, 128), lambda s, h: (s, h, 0, 0, 0))
    flat = struct(heads * head_dim, seqs * length)
    work = seqs * heads * length * length
    return pl.pallas_call(
        functools.partial(backward_kernel, scale, block),
        grid=(seqs, heads),
        in_specs=[part(0), part(1), part(2), table, table, prob_spec, part(0)],
        out_specs=[part(0), part(0), part(0), sum_spec],
        out_shape=[flat, flat, flat, struct(seqs, heads, 3, head_dim, 128, dtype=F32)],
        scratch_shapes=[pltpu.VMEM((length, head_dim), F32)] * 2,
        cost_estimate=cost(10 * work * head_dim, proj_t.size * 6, work),
        name="attend_backward",
    )(proj_t, proj_t, proj_t, cosine, sine, probs, ctx_grad_t)


def branch_sum(ctx_t, hidden, first, second):
    width, rows = ctx_t.shape
    hidden_units = hidden.shape[1]
    model = first.shape[0]
    block = min(256, rows)
    first_spec, out_cols = columns(first, hidden_units, width)
    second_spec, _ = columns(second, 0, hidden_units)
    return pl.pallas_call(
        functools.partial(branch_kernel, out_cols),
        grid=(rows // block,),
        in_specs=[
            tokens_t(width, block), tokens(block, hidden_units), first_spec, second_spec,
        ],
        out_specs=[tokens(block, model), tokens(block, width)],
        out_shape=[struct(rows, model), struct(rows, width)],
        cost_estimate=cost(2 * rows * model * (width + hidden_units), 8 * rows * model),
        name="branch",
    )(ctx_t, hidden, first, second)


def return_grads(after, places, cot, slopes, first, second, width):
    rows, model = cot.shape
    hidden_units = slopes.shape[1]
    block = min(256, rows)
    first_spec, out_cols = columns(first, hidden_units, width)
    second_spec, _ = columns(second, 0, hidden_units)
    return pl.pallas_call(
        functools.partial(return_kernel, out_cols),
        grid=(rows // block,),
        in_specs=[
            pl.BlockSpec(memory_space=pl.ANY), pl.BlockSpec(memory_space=pl.ANY),
            tokens(block, model), tokens(block, hidden_units), first_spec, second_spec,
        ],
        out_specs=[
            tokens_t(model, block), tokens_t(width, block), tokens(block, hidden_units),
            pl.BlockSpec((8, hidden_units), lambda t: (0, 0)),
            pl.BlockSpec((8, model), lambda t: (0, 0)),
        ],
        out_shape=[
            struct(model, rows), struct(width, rows), struct(rows, hidden_units),
            struct(8, hidden_units, dtype=F32), struct(8, model, dtype=F32),
        ],
        cost_estimate=cost(2 * rows * model * (width + hidden_units), 10 * rows * model),
        name="return_grads",
    )(after, places, cot, slopes, first, second)


def norm_sum(x, dq_t, dk_t, dv_t, pre_low, first, second):
    rows, model = x.shape
    width = dq_t.shape[0]
    hidden_units = pre_low.shape[1]
    block = min(256, rows)
    first_spec, _ = columns(first, 0, hidden_units)
    second_spec, qkv_cols = columns(second, hidden_units, 3 * width)
    return pl.pallas_call(
        functools.partial(norm_kernel, qkv_cols),
        grid=(rows // block,),
        in_specs=[
            tokens(block, model), tokens_t(width, block), tokens_t(width, block),
            tokens_t(width, block), tokens(block, hidden_units), first_spec, second_spec,
        ],
        out_specs=[
            tokens(block, 3 * width), tokens(block, model),
            pl.BlockSpec((8, model), lambda t: (0, 0)),
            pl.BlockSpec((8, model), lambda t: (0, 0)),
        ],
        out_shape=[
            struct(rows, 3 * width), struct(rows, model),
            struct(8, model, dtype=F32), struct(8, model, dtype=F32),
        ],
        cost_estimate=cost(2 * rows * model * (3 * width + hidden_units), 8 * rows * model),
        name="norm_grads",
    )(x, dq_t, dk_t, dv_t, pre_low, first, second)


def finish_kernel(x_ref, cot_ref, own_ref, gain_ref, grad_ref):
    unit, inv_sigma = normalize(x_ref[0])
    unit_grad = own_ref[0].astype(F32) * gain_ref[...]
    grad = cot_ref[0].astype(F32) + inv_sigma * (
        unit_grad
        - jnp.mean(unit_grad, axis=-1, keepdims=True)
        - unit * jnp.mean(unit_grad * unit, axis=-1, keepdims=True)
    )
    grad_ref[0] = grad.astype(BF16)


def finish(x, cot, own, gain):
    rows = pl.BlockSpec((1, x.shape[1] // 2, x.shape[2]), lambda s, t: (s, t, 0))
    return pl.pallas_call(
        finish_kernel,
        grid=(x.shape[0], 2),
        in_specs=[rows, rows, rows, pl.BlockSpec(gain.shape, lambda *_: (0, 0))],
        out_specs=rows,
        out_shape=struct(*x.shape),
        cost_estimate=cost(20 * x.size, 8 * x.size),
        name="finish",
    )(x, cot, own, gain)


def weight_half(kernel, places, row, operands, got, blocks, part, shape, flops):
    if got is None:
        outs = [struct(blocks, *shape)]
    else:
        operands = operands + (got,)
        outs = [struct(*shape, dtype=F32)] + [struct(*shape)] * (blocks - 1)
    return pl.pallas_call(
        functools.partial(kernel, blocks, part, row),
        grid_spec=pltpu.PrefetchScalarGridSpec(
            num_scalar_prefetch=1,
            grid=(1,),
            in_specs=[whole(x) for x in operands],
            out_specs=[whole(x) for x in outs],
        ),
        out_shape=outs,
        cost_estimate=cost(flops, 4 * operands[0].size),
    )(places, *operands)


def rotary_tables(length):
    half_rot = ROT // 2
    position = jnp.arange(length).astype(F32)
    inv_freq = jnp.exp(jnp.arange(half_rot).astype(F32) * (-2.0 * math.log(10000.0) / ROT))
    angles = inv_freq[:, None] * position[None, :]
    return jnp.cos(angles), jnp.sin(angles)


def split_core(grad, dp):
    core = bit_of("dp", 1)
    grad = grad.reshape(dp // 2, 2, -1, grad.shape[-1])
    kept = lax.dynamic_index_in_dim(grad, core, 1, keepdims=False)
    sent = lax.dynamic_index_in_dim(grad, 1 - core, 1, keepdims=False)
    return kept, sent.astype(BF16)


def swap_core(sent, dp):
    return swap(sent, "dp", dp, 1)


def add_pieces(pieces, dp):
    total = pieces[0]
    for k in range(1, len(pieces)):
        got = swap(pieces[k], "dp", dp, 2 * k)
        total = total + got.astype(F32)
    return total


def exchange_small(small, dp):
    core, chip = bit_of("dp", 1), lax.axis_index("dp") // 2
    count = dp // 2
    small = small.reshape(count, 2, -1)
    kept = lax.dynamic_index_in_dim(small, core, 1, keepdims=False)
    sent = lax.dynamic_index_in_dim(small, 1 - core, 1, keepdims=False)
    got = swap_core(sent, dp)
    x = kept + got
    if count > 4:
        steps = [1 << b for b in range(count.bit_length() - 1)]
        return scatter_bits(x, 0, steps[::-1], F32, dp, 2)
    pieces = [
        lax.dynamic_index_in_dim(x, chip ^ k, 0, keepdims=False) for k in range(count)
    ]
    return add_pieces(pieces, dp)


def exchange(grad, dp):
    kept, sent = split_core(grad, dp)
    x = kept + swap_core(sent, dp).astype(F32)
    steps = [1 << b for b in range((dp // 2).bit_length() - 1)]
    return scatter_bits(x, 0, steps[::-1], BF16, dp, 2)


def body(
    dp, tensor, inputs, ln_gain, ln_bias, w_qkv, b_qkv, w_out, w_in, b_in, w_down, out_bias,
    cotangent,
):
    model = inputs.shape[-1]
    heads, head_dim = b_qkv.shape[1], b_qkv.shape[2] * dp
    width = heads * head_dim
    hidden_units = w_in.shape[1]
    seqs, length = inputs.shape[0], inputs.shape[1] * tensor
    rows = seqs * length
    own = ln_gain.shape[0]
    share = own * tensor
    slow = [1 << b for b in range(1, dp.bit_length() - 1)]
    ways = (slow + [1], slow[::-1] + [1])
    me_z = lax.axis_index("tensor")

    full_in = lax.all_gather(inputs, "tensor", axis=1, tiled=True).reshape(rows, model)
    full_cot = lax.all_gather(cotangent, "tensor", axis=1, tiled=True).reshape(rows, model)

    vector = jnp.stack([ln_gain, ln_bias, out_bias[0] + out_bias[1]])
    by_z = [vector]
    for k in range(1, tensor):
        by_z.append(
            lax.ppermute(vector, "tensor", [(i, (i + k) % tensor) for i in range(tensor)])
        )
    by_z = jnp.stack(by_z)
    order = (me_z - jnp.arange(tensor)) % tensor
    by_z = jnp.take(by_z, order, axis=0).transpose(1, 0, 2)
    small = jnp.concatenate(
        [by_z.reshape(-1), b_qkv.astype(F32).reshape(-1), b_in.astype(F32).reshape(-1)]
    )
    used = small.shape[0]
    padded = -(-used // 1024) * 1024
    small = jnp.pad(small, (0, padded - used)).reshape(-1, 128)
    small = gather_bits(small, dp, 0, ways[0]).reshape(dp, padded)
    norm_rows = small[:, : 3 * share].reshape(dp, 3, share).transpose(1, 0, 2).reshape(3, model)
    gain, out_shift = norm_rows[0], norm_rows[2]
    at = 3 * share
    qkv_count = b_qkv.size
    qkv_bias = (
        small[:, at : at + qkv_count]
        .reshape(dp, 3, heads, head_dim // dp)
        .transpose(1, 2, 0, 3)
        .reshape(3 * width)
    )
    at += qkv_count
    in_groups, in_each = b_in.shape
    in_bias = (
        small[:, at : at + b_in.size]
        .reshape(dp, in_groups, in_each)
        .transpose(1, 0, 2)
        .reshape(hidden_units)
    )

    first = gather_bits(jnp.concatenate([w_in, w_out.T], axis=1), dp, 0, ways[0])
    second = gather_bits(
        jnp.concatenate([w_down.T, w_qkv.reshape(w_qkv.shape[0], -1)], axis=1), dp, 0, ways[1],
    )
    first = first.reshape(model, -1)
    second = second.reshape(model, -1)

    cosine, sine = rotary_tables(length)
    unit, normed_t, proj_t, hidden, slopes = enter(
        full_in, norm_rows, in_bias.reshape(1, -1), qkv_bias.reshape(1, -1), first, second,
        cosine, sine, heads, head_dim,
    )
    ctx_t, probs = attend(proj_t, seqs, heads, head_dim, length)
    branch, context = branch_sum(ctx_t, hidden, first, second)
    summed = lax.psum_scatter(
        branch.reshape(seqs, length, model), "tensor", scatter_dimension=1, tiled=True
    )
    outputs = (inputs.astype(F32) + summed.astype(F32) + out_shift).astype(BF16)

    core, chip = bit_of("dp", 1), lax.axis_index("dp") // 2
    places = jnp.stack([1 - core, chip, core, chip]).astype(jnp.int32)
    cot_t, ctx_grad_t, pre_low, in_sum, cot_sum = return_grads(
        context, places, full_cot, slopes, first, second, width
    )
    part = model // dp
    aligned = 2 <= dp <= 8 and part % 16 == 0
    blocks = dp // 2
    if aligned:
        operands = (normed_t, cot_t, pre_low, context, hidden)
        shape = (part, 2 * hidden_units + width)
        flops = rows * model * shape[1]
        (early_sent,) = weight_half(
            early_kernel, places, 0, operands, None, blocks, part, shape, flops
        )
        early_got = swap_core(early_sent, dp)
        early_pieces = weight_half(
            early_kernel, places, 1, operands, early_got, blocks, part,
            shape, flops,
        )
        early = add_pieces(early_pieces, dp)
    else:
        early = jnp.concatenate(
            [
                dot(normed_t, pre_low, (1, 0)),
                dot(cot_t, hidden, (1, 0)),
                dot(cot_t, context, (1, 0)),
            ],
            axis=1,
        )
        early = exchange(early, dp)
    dq_t, dk_t, dv_t, sums = attend_back(
        proj_t, cosine, sine, probs, ctx_grad_t, seqs, heads, head_dim, length
    )
    proj_low, norm_grad, gain_sum, shift_sum = norm_sum(
        unit, dq_t, dk_t, dv_t, pre_low, first, second
    )
    own_grad = lax.psum_scatter(
        norm_grad.reshape(seqs, length, model), "tensor", scatter_dimension=1, tiled=True
    )
    grad_qkv_bias = jnp.sum(sums[..., 0], axis=0).transpose(1, 0, 2)
    grad_in_bias = jnp.sum(in_sum, axis=0)
    bias_part = jnp.sum(cot_sum, axis=0).reshape(dp, tensor, own)
    pair = jnp.stack([gain_sum, shift_sum]).sum(axis=1).reshape(2, dp, tensor, own)
    pair_total = lax.dynamic_index_in_dim(pair, me_z, 2, keepdims=False)
    for k in range(1, tensor):
        piece = lax.dynamic_index_in_dim(pair, (me_z + k) % tensor, 2, keepdims=False)
        got = lax.ppermute(
            piece, "tensor", [(i, (i + k) % tensor) for i in range(tensor)]
        )
        pair_total = pair_total + got
    bias_total = lax.dynamic_index_in_dim(bias_part, me_z, 1, keepdims=False)
    small = jnp.concatenate(
        [
            pair_total[0], pair_total[1], bias_total,
            grad_qkv_bias.reshape(3, heads, dp, head_dim // dp)
            .transpose(2, 0, 1, 3)
            .reshape(dp, -1),
            grad_in_bias.reshape(in_groups, dp, in_each).transpose(1, 0, 2).reshape(dp, -1),
        ],
        axis=1,
    )
    small = exchange_small(
        jnp.pad(small, ((0, 0), (0, -small.shape[1] % 128))), dp
    )
    if aligned:
        operands = (normed_t, proj_low)
        shape = (part, 3 * width)
        flops = rows * model * shape[1]
        (late_sent,) = weight_half(
            late_kernel, places, 0, operands, None, blocks, part, shape,
            flops,
        )
        late_got = swap_core(late_sent, dp)
        late_pieces = weight_half(
            late_kernel, places, 1, operands, late_got, blocks, part, shape,
            flops,
        )
        late = add_pieces(late_pieces, dp)
    else:
        late = exchange(dot(normed_t, proj_low, (1, 0)), dp)
    in_out = early[:, :hidden_units]
    down_out = early[:, hidden_units : 2 * hidden_units].T
    out_out = early[:, 2 * hidden_units :].T
    qkv_out = late.reshape(part, 3, width)
    gain_out, shift_out, bias_out = (small[k * own : (k + 1) * own] for k in range(3))
    bias_grad = jnp.stack([bias_out, bias_out])
    at = 3 * own
    qkv_bias_out = small[at : at + qkv_count].reshape(b_qkv.shape)
    at += qkv_count
    in_bias_out = small[at : at + b_in.size].reshape(b_in.shape)

    input_grad = finish(inputs, cotangent, own_grad, gain.reshape(1, model))
    return (
        outputs,
        input_grad,
        gain_out,
        shift_out,
        qkv_out,
        qkv_bias_out,
        out_out,
        in_out,
        in_bias_out,
        down_out,
        bias_grad,
    )


def solution(mesh):
    spread = P("dp", "tensor", None)
    vector = P(("dp", "tensor"))
    qkv, qkv_bias = P("dp", None, "tensor"), P(None, "tensor", "dp")
    by_out, by_in, pair = P("tensor", "dp"), P("dp", "tensor"), P(None, ("dp", "tensor"))

    def layer(*arrays):
        return body(mesh.shape["dp"], mesh.shape["tensor"], *arrays)

    return jax.shard_map(
        layer,
        mesh=mesh,
        in_specs=(
            spread, vector, vector, qkv, qkv_bias, by_out, by_in, by_out, by_out, pair, spread,
        ),
        out_specs=(
            spread, spread, vector, vector, qkv, qkv_bias, by_out, by_in, by_out, by_out, pair,
        ),
        check_vma=False,
    )
```

```python
import functools
import math

import jax
import jax.numpy as jnp
from jax import lax
from jax.experimental import pallas as pl
from jax.experimental.pallas import tpu as pltpu
from jax.sharding import PartitionSpec as P

ROT = 16
EPS = 1e-05
ROOT_HALF = 0.7071067811865476
INV_ROOT_TAU = 0.3989422804014327
NEG_BIG = -1e30
F32 = jnp.float32
BF16 = jnp.bfloat16


def dot(a, b, contract, out=F32):
    return lax.dot_general(
        a, b, (((contract[0],), (contract[1],)), ((), ())), preferred_element_type=out
    )


def swap(x, axis_name, size, step):
    return lax.ppermute(x, axis_name, [(i, i ^ step) for i in range(size)])


def bit_of(axis_name, step):
    return (lax.axis_index(axis_name) // step) % 2


def gather_bits(x, size, axis, steps):
    done = []
    for step in steps:
        other = swap(x, "dp", size, step)
        mine_first = bit_of("dp", step) == 0
        low = jnp.where(mine_first, x, other)
        high = jnp.where(mine_first, other, x)
        place = axis + sum(1 for s in done if s > step)
        x = jnp.stack([low, high], axis=place)
        done.append(step)
    shape = x.shape
    levels = len(steps)
    return x.reshape(shape[:axis] + (size,) + shape[axis + levels :])


def scatter_bits(x, axis, steps, wire, size, unit):
    shape = x.shape
    levels = len(steps)
    x = x.reshape(shape[:axis] + (2,) * levels + shape[axis + 1 :])
    left = sorted(steps, reverse=True)
    for step in steps:
        place = axis + left.index(step)
        bit = bit_of("dp", step * unit)
        keep = lax.dynamic_index_in_dim(x, bit, place, keepdims=False)
        send = lax.dynamic_index_in_dim(x, 1 - bit, place, keepdims=False)
        got = swap(send.astype(wire), "dp", size, step * unit)
        x = keep + got.astype(F32)
        left.remove(step)
    return x


def rotate_rows(x, cosine, sine):
    half = ROT // 2
    first, second = x[:half], x[half:ROT]
    return jnp.concatenate(
        [first * cosine - second * sine, second * cosine + first * sine, x[ROT:]], axis=0
    )


def normalize(x):
    wide = x.astype(F32)
    centred = wide - jnp.mean(wide, axis=-1, keepdims=True)
    inv_sigma = lax.rsqrt(jnp.mean(centred * centred, axis=-1, keepdims=True) + EPS)
    return centred * inv_sigma, inv_sigma


def enter_kernel(
    heads, head_dim, qkv_cols, x_ref, vec_ref, in_bias_ref, qkv_bias_ref, first_ref, second_ref,
    cos_ref, sin_ref, unit_ref, normed_t_ref, proj_t_ref, hidden_ref, slope_ref,
):
    width = heads * head_dim
    unit, _ = normalize(x_ref[...])
    unit_ref[...] = unit.astype(BF16)
    wide = unit * vec_ref[0:1] + vec_ref[1:2]
    normed = wide.astype(BF16)
    normed_t_ref[...] = jnp.transpose(normed)
    projected = dot(normed, second_ref[:, qkv_cols], (1, 0)) + qkv_bias_ref[...]
    projected = jnp.transpose(projected)
    cosine, sine = cos_ref[...], sin_ref[...]
    for place in range(2 * heads):
        rows = slice(place * head_dim, (place + 1) * head_dim)
        proj_t_ref[rows] = rotate_rows(projected[rows], cosine, sine).astype(BF16)
    proj_t_ref[2 * width :] = projected[2 * width :].astype(BF16)
    pre_act = dot(normed, first_ref[...], (1, 0)) + in_bias_ref[...]
    normal_cdf = 0.5 * (1.0 + lax.erf(pre_act * ROOT_HALF))
    normal_pdf = jnp.exp(-0.5 * pre_act * pre_act) * INV_ROOT_TAU
    hidden_ref[...] = (pre_act * normal_cdf).astype(BF16)
    slope_ref[...] = normal_cdf + pre_act * normal_pdf


def causal(block):
    key_pos = lax.broadcasted_iota(jnp.int32, (block, block), 0)
    query_pos = lax.broadcasted_iota(jnp.int32, (block, block), 1)
    return key_pos <= query_pos


def forward_kernel(scale, block, q_ref, k_ref, v_ref, ctx_ref, prob_ref):
    length = q_ref.shape[1]
    queries = q_ref[...] * jnp.asarray(scale, BF16)
    keys = jnp.transpose(k_ref[...])
    values = v_ref[...]
    allowed = causal(block)
    for step in range(length // block):
        here = slice(step * block, (step + 1) * block)
        before = slice(0, step * block)
        q_cols = queries[:, here]
        near = jnp.where(allowed, dot(keys[here], q_cols, (1, 0)), NEG_BIG)
        top = jnp.max(near, axis=0, keepdims=True)
        if step:
            far = dot(keys[before], q_cols, (1, 0))
            top = jnp.maximum(top, jnp.max(far, axis=0, keepdims=True))
        near = jnp.exp(near - top)
        total = jnp.sum(near, axis=0, keepdims=True)
        if step:
            far = jnp.exp(far - top)
            total = total + jnp.sum(far, axis=0, keepdims=True)
        inverse = 1.0 / total
        near = (near * inverse).astype(BF16)
        prob_ref[0, 0, here, here] = near
        context = dot(values[:, here], near, (1, 0))
        if step:
            far = (far * inverse).astype(BF16)
            prob_ref[0, 0, before, here] = far
            context = context + dot(values[:, before], far, (1, 0))
        ctx_ref[:, here] = context.astype(BF16)


def backward_kernel(
    scale, block, q_ref, k_ref, v_ref, cos_ref, sin_ref, prob_ref, grad_ref,
    dq_ref, dk_ref, dv_ref, sum_ref, keys_acc, values_acc,
):
    length = q_ref.shape[1]
    cosine, sine = cos_ref[...], sin_ref[...]
    query_rows = jnp.transpose(q_ref[...] * jnp.asarray(scale, BF16))
    keys_t = k_ref[...]
    values = jnp.transpose(v_ref[...])
    grad_t = grad_ref[...]
    grad_rows = jnp.transpose(grad_t)
    query_sum = 0.0
    for step in reversed(range(length // block)):
        here = slice(step * block, (step + 1) * block)
        upto = slice(0, (step + 1) * block)
        probs = prob_ref[0, 0, upto, here]
        value_part = dot(probs, grad_rows[here], (1, 0))
        prob_grad = dot(values[upto], grad_t[:, here], (1, 0))
        probs = probs.astype(F32)
        row_dot = jnp.sum(probs * prob_grad, axis=0, keepdims=True)
        score_grad = (probs * (prob_grad - row_dot)).astype(BF16)
        key_part = dot(score_grad, query_rows[here], (1, 0))
        if (step + 1) * block == length:
            values_acc[...] = value_part
            keys_acc[...] = key_part
        else:
            values_acc[upto, :] += value_part
            keys_acc[upto, :] += key_part
        dq = dot(keys_t[:, upto], score_grad, (1, 0)) * scale
        dq = rotate_rows(dq, cosine[:, here], -sine[:, here])
        dq_ref[:, here] = dq.astype(BF16)
        query_sum = query_sum + jnp.sum(dq, axis=1, keepdims=True)
    dk = rotate_rows(jnp.transpose(keys_acc[...]), cosine, -sine)
    dv = jnp.transpose(values_acc[...])
    dk_ref[...] = dk.astype(BF16)
    dv_ref[...] = dv.astype(BF16)
    sums = [query_sum, jnp.sum(dk, axis=1, keepdims=True), jnp.sum(dv, axis=1, keepdims=True)]
    for place, part in enumerate(sums):
        sum_ref[0, 0, place] = jnp.broadcast_to(part, (part.shape[0], 128))


def branch_kernel(out_cols, ctx_t_ref, hidden_ref, first_ref, second_ref, branch_ref, ctx_ref):
    context = jnp.transpose(ctx_t_ref[...])
    ctx_ref[...] = context
    total = dot(context, first_ref[:, out_cols], (1, 1))
    total = total + dot(hidden_ref[...], second_ref[...], (1, 1))
    branch_ref[...] = total.astype(BF16)


def row_sums(x):
    return jnp.sum(x.reshape(x.shape[0] // 8, 8, x.shape[1]), axis=0)


def return_kernel(
    out_cols, after_ref, places_ref, cot_ref, slope_ref, first_ref, second_ref,
    cot_t_ref, ctx_grad_t_ref, pre_low_ref, in_sum_ref, cot_sum_ref,
):
    cot = cot_ref[...]
    cot_t_ref[...] = jnp.transpose(cot)
    ctx_grad = dot(cot, first_ref[:, out_cols], (1, 0))
    ctx_grad_t_ref[...] = jnp.transpose(ctx_grad).astype(BF16)
    pre_grad = dot(cot, second_ref[...], (1, 0)) * slope_ref[...]
    pre_low_ref[...] = pre_grad.astype(BF16)

    @pl.when(pl.program_id(0) == 0)
    def _():
        in_sum_ref[...] = jnp.zeros_like(in_sum_ref)
        cot_sum_ref[...] = jnp.zeros_like(cot_sum_ref)

    in_sum_ref[...] += row_sums(pre_grad)
    cot_sum_ref[...] += row_sums(cot.astype(F32))


def norm_kernel(
    qkv_cols, unit_ref, dq_ref, dk_ref, dv_ref, pre_low_ref, first_ref, second_ref,
    proj_low_ref, norm_grad_ref, gain_sum_ref, shift_sum_ref,
):
    proj_low = jnp.transpose(
        jnp.concatenate([dq_ref[...], dk_ref[...], dv_ref[...]], axis=0)
    )
    proj_low_ref[...] = proj_low
    norm_grad = dot(proj_low, second_ref[:, qkv_cols], (1, 1))
    norm_grad = norm_grad + dot(pre_low_ref[...], first_ref[...], (1, 1))
    norm_grad_ref[...] = norm_grad.astype(BF16)
    unit = unit_ref[...].astype(F32)

    @pl.when(pl.program_id(0) == 0)
    def _():
        gain_sum_ref[...] = jnp.zeros_like(gain_sum_ref)
        shift_sum_ref[...] = jnp.zeros_like(shift_sum_ref)

    gain_sum_ref[...] += row_sums(norm_grad * unit)
    shift_sum_ref[...] += row_sums(norm_grad)


def half_rows(ref, places_ref, row, blocks, part):
    chips = [lax.bitwise_xor(places_ref[1], k) for k in range(blocks)]
    starts = [pl.multiple_of((2 * chip + places_ref[2 * row]) * part, part) for chip in chips]
    return jnp.concatenate([ref[pl.ds(start, part), :] for start in starts], axis=0)


def put(outs, got_ref, columns, value):
    blocks, part = (outs[0].shape[0], outs[0].shape[1]) if got_ref is None else got_ref.shape[:2]
    value = value.reshape(blocks, part, -1)
    if got_ref is None:
        outs[0][:, :, columns] = value.astype(BF16)
        return
    value = value + got_ref[:, :, columns].astype(F32)
    for k in range(blocks):
        outs[k][:, columns] = value[k].astype(outs[k].dtype)


def early_kernel(blocks, part, row, at_ref, normed_t_ref, cot_t_ref, pre_low_ref, ctx_ref, hidden_ref, *refs):
    got_ref, outs = (None, refs) if len(refs) == 1 else (refs[0], refs[1:])
    units = hidden_ref.shape[1]
    left = half_rows(normed_t_ref, at_ref, row, blocks, part)
    put(outs, got_ref, slice(0, units), dot(left, pre_low_ref[...], (1, 0)))
    left = half_rows(cot_t_ref, at_ref, row, blocks, part)
    put(outs, got_ref, slice(units, 2 * units), dot(left, hidden_ref[...], (1, 0)))
    put(outs, got_ref, slice(2 * units, None), dot(left, ctx_ref[...], (1, 0)))


def late_kernel(blocks, part, row, at_ref, normed_t_ref, proj_low_ref, *refs):
    got_ref, outs = (None, refs) if len(refs) == 1 else (refs[0], refs[1:])
    left = half_rows(normed_t_ref, at_ref, row, blocks, part)
    put(outs, got_ref, slice(None), dot(left, proj_low_ref[...], (1, 0)))


def whole(x):
    return pl.BlockSpec(x.shape, lambda *_: (0,) * x.ndim)


def tokens(block, columns):
    return pl.BlockSpec((block, columns), lambda t: (t, 0))


def tokens_t(rows, block):
    return pl.BlockSpec((rows, block), lambda t: (0, t))


def columns(x, start, count):
    for wide in range(-(-count // 128) * 128, start + 1, 128):
        if start % wide == 0:
            return pl.BlockSpec((x.shape[0], wide), lambda *_: (0, start // wide)), slice(0, count)
    if start == 0:
        return pl.BlockSpec((x.shape[0], count), lambda *_: (0, 0)), slice(0, count)
    return whole(x), slice(start, start + count)


def cost(flops, nbytes, trans=0):
    return pl.CostEstimate(flops=flops, bytes_accessed=nbytes, transcendentals=trans)


def struct(*shape, dtype=BF16):
    return jax.ShapeDtypeStruct(shape, dtype)


def enter(x, vectors, in_bias, qkv_bias, first, second, cosine, sine, heads, head_dim):
    rows, model = x.shape
    hidden_units = in_bias.shape[1]
    proj = 3 * heads * head_dim
    block = min(256, rows)
    per_seq = cosine.shape[1] // block
    table = pl.BlockSpec((ROT // 2, block), lambda t: (0, lax.rem(t, per_seq)))
    first_spec, _ = columns(first, 0, hidden_units)
    second_spec, qkv_cols = columns(second, hidden_units, proj)
    return pl.pallas_call(
        functools.partial(enter_kernel, heads, head_dim, qkv_cols),
        grid=(rows // block,),
        in_specs=[
            tokens(block, model), whole(vectors), whole(in_bias), whole(qkv_bias),
            first_spec, second_spec, table, table,
        ],
        out_specs=[
            tokens(block, model), tokens_t(model, block), tokens_t(proj, block),
            tokens(block, hidden_units), tokens(block, hidden_units),
        ],
        out_shape=[
            struct(rows, model), struct(model, rows), struct(proj, rows),
            struct(rows, hidden_units), struct(rows, hidden_units, dtype=F32),
        ],
        cost_estimate=cost(
            2 * rows * model * (proj + hidden_units), 2 * (first.size + second.size) + 12 * x.size,
            2 * rows * hidden_units,
        ),
        name="enter",
    )(x, vectors, in_bias, qkv_bias, first, second, cosine, sine)


def attend(proj_t, seqs, heads, head_dim, length):
    block = min(256, length)
    scale = 1.0 / math.sqrt(head_dim)

    def part(which):
        return pl.BlockSpec((head_dim, length), lambda s, h: (which * heads + h, s))

    prob_spec = pl.BlockSpec((1, 1, length, length), lambda s, h: (s, h, 0, 0))
    work = seqs * heads * length * length
    return pl.pallas_call(
        functools.partial(forward_kernel, scale, block),
        grid=(seqs, heads),
        in_specs=[part(0), part(1), part(2)],
        out_specs=[part(0), prob_spec],
        out_shape=[
            struct(heads * head_dim, seqs * length),
            struct(seqs, heads, length, length),
        ],
        cost_estimate=cost(4 * work * head_dim, proj_t.size * 4, work),
        name="attend_forward",
    )(proj_t, proj_t, proj_t)


def attend_back(proj_t, cosine, sine, probs, ctx_grad_t, seqs, heads, head_dim, length):
    block = min(256, length)
    scale = 1.0 / math.sqrt(head_dim)

    def part(which):
        return pl.BlockSpec((head_dim, length), lambda s, h: (which * heads + h, s))

    table = pl.BlockSpec((ROT // 2, length), lambda s, h: (0, 0))
    prob_spec = pl.BlockSpec((1, 1, length, length), lambda s, h: (s, h, 0, 0))
    sum_spec = pl.BlockSpec((1, 1, 3, head_dim, 128), lambda s, h: (s, h, 0, 0, 0))
    flat = struct(heads * head_dim, seqs * length)
    work = seqs * heads * length * length
    return pl.pallas_call(
        functools.partial(backward_kernel, scale, block),
        grid=(seqs, heads),
        in_specs=[part(0), part(1), part(2), table, table, prob_spec, part(0)],
        out_specs=[part(0), part(0), part(0), sum_spec],
        out_shape=[flat, flat, flat, struct(seqs, heads, 3, head_dim, 128, dtype=F32)],
        scratch_shapes=[pltpu.VMEM((length, head_dim), F32)] * 2,
        cost_estimate=cost(10 * work * head_dim, proj_t.size * 6, work),
        name="attend_backward",
    )(proj_t, proj_t, proj_t, cosine, sine, probs, ctx_grad_t)


def branch_sum(ctx_t, hidden, first, second):
    width, rows = ctx_t.shape
    hidden_units = hidden.shape[1]
    model = first.shape[0]
    block = min(256, rows)
    first_spec, out_cols = columns(first, hidden_units, width)
    second_spec, _ = columns(second, 0, hidden_units)
    return pl.pallas_call(
        functools.partial(branch_kernel, out_cols),
        grid=(rows // block,),
        in_specs=[
            tokens_t(width, block), tokens(block, hidden_units), first_spec, second_spec,
        ],
        out_specs=[tokens(block, model), tokens(block, width)],
        out_shape=[struct(rows, model), struct(rows, width)],
        cost_estimate=cost(2 * rows * model * (width + hidden_units), 8 * rows * model),
        name="branch",
    )(ctx_t, hidden, first, second)


def return_grads(after, places, cot, slopes, first, second, width):
    rows, model = cot.shape
    hidden_units = slopes.shape[1]
    block = min(256, rows)
    first_spec, out_cols = columns(first, hidden_units, width)
    second_spec, _ = columns(second, 0, hidden_units)
    return pl.pallas_call(
        functools.partial(return_kernel, out_cols),
        grid=(rows // block,),
        in_specs=[
            pl.BlockSpec(memory_space=pl.ANY), pl.BlockSpec(memory_space=pl.ANY),
            tokens(block, model), tokens(block, hidden_units), first_spec, second_spec,
        ],
        out_specs=[
            tokens_t(model, block), tokens_t(width, block), tokens(block, hidden_units),
            pl.BlockSpec((8, hidden_units), lambda t: (0, 0)),
            pl.BlockSpec((8, model), lambda t: (0, 0)),
        ],
        out_shape=[
            struct(model, rows), struct(width, rows), struct(rows, hidden_units),
            struct(8, hidden_units, dtype=F32), struct(8, model, dtype=F32),
        ],
        cost_estimate=cost(2 * rows * model * (width + hidden_units), 10 * rows * model),
        name="return_grads",
    )(after, places, cot, slopes, first, second)


def norm_sum(x, dq_t, dk_t, dv_t, pre_low, first, second):
    rows, model = x.shape
    width = dq_t.shape[0]
    hidden_units = pre_low.shape[1]
    block = min(256, rows)
    first_spec, _ = columns(first, 0, hidden_units)
    second_spec, qkv_cols = columns(second, hidden_units, 3 * width)
    return pl.pallas_call(
        functools.partial(norm_kernel, qkv_cols),
        grid=(rows // block,),
        in_specs=[
            tokens(block, model), tokens_t(width, block), tokens_t(width, block),
            tokens_t(width, block), tokens(block, hidden_units), first_spec, second_spec,
        ],
        out_specs=[
            tokens(block, 3 * width), tokens(block, model),
            pl.BlockSpec((8, model), lambda t: (0, 0)),
            pl.BlockSpec((8, model), lambda t: (0, 0)),
        ],
        out_shape=[
            struct(rows, 3 * width), struct(rows, model),
            struct(8, model, dtype=F32), struct(8, model, dtype=F32),
        ],
        cost_estimate=cost(2 * rows * model * (3 * width + hidden_units), 8 * rows * model),
        name="norm_grads",
    )(x, dq_t, dk_t, dv_t, pre_low, first, second)


def finish_kernel(x_ref, cot_ref, own_ref, vec_ref, grad_ref):
    unit, inv_sigma = normalize(x_ref[0])
    unit_grad = own_ref[0].astype(F32) * vec_ref[0:1]
    grad = cot_ref[0].astype(F32) + inv_sigma * (
        unit_grad
        - jnp.mean(unit_grad, axis=-1, keepdims=True)
        - unit * jnp.mean(unit_grad * unit, axis=-1, keepdims=True)
    )
    grad_ref[0] = grad.astype(BF16)


def finish(x, cot, own, vectors):
    rows = pl.BlockSpec((1, x.shape[1] // 2, x.shape[2]), lambda s, t: (s, t, 0))
    return pl.pallas_call(
        finish_kernel,
        grid=(x.shape[0], 2),
        in_specs=[rows, rows, rows, whole(vectors)],
        out_specs=rows,
        out_shape=struct(*x.shape),
        cost_estimate=cost(20 * x.size, 8 * x.size),
        name="finish",
    )(x, cot, own, vectors)


def weight_half(kernel, places, row, operands, got, blocks, part, shape, flops):
    if got is None:
        outs = [struct(blocks, *shape)]
    else:
        operands = operands + (got,)
        outs = [struct(*shape, dtype=F32)] + [struct(*shape)] * (blocks - 1)
    return pl.pallas_call(
        functools.partial(kernel, blocks, part, row),
        grid_spec=pltpu.PrefetchScalarGridSpec(
            num_scalar_prefetch=1,
            grid=(1,),
            in_specs=[whole(x) for x in operands],
            out_specs=[whole(x) for x in outs],
        ),
        out_shape=outs,
        cost_estimate=cost(flops, 4 * operands[0].size),
    )(places, *operands)


def rotary_tables(length):
    half_rot = ROT // 2
    position = jnp.arange(length).astype(F32)
    inv_freq = jnp.exp(jnp.arange(half_rot).astype(F32) * (-2.0 * math.log(10000.0) / ROT))
    angles = inv_freq[:, None] * position[None, :]
    return jnp.cos(angles), jnp.sin(angles)


def split_core(grad, dp):
    core = bit_of("dp", 1)
    grad = grad.reshape(dp // 2, 2, -1, grad.shape[-1])
    kept = lax.dynamic_index_in_dim(grad, core, 1, keepdims=False)
    sent = lax.dynamic_index_in_dim(grad, 1 - core, 1, keepdims=False)
    return kept, sent.astype(BF16)


def swap_core(sent, dp):
    return swap(sent, "dp", dp, 1)


def add_pieces(pieces, dp):
    total = pieces[0]
    for k in range(1, len(pieces)):
        got = swap(pieces[k], "dp", dp, 2 * k)
        total = total + got.astype(F32)
    return total


def exchange_small(small, dp):
    core, chip = bit_of("dp", 1), lax.axis_index("dp") // 2
    count = dp // 2
    small = small.reshape(count, 2, -1)
    kept = lax.dynamic_index_in_dim(small, core, 1, keepdims=False)
    sent = lax.dynamic_index_in_dim(small, 1 - core, 1, keepdims=False)
    got = swap_core(sent, dp)
    x = kept + got
    if count > 4:
        steps = [1 << b for b in range(count.bit_length() - 1)]
        return scatter_bits(x, 0, steps[::-1], F32, dp, 2)
    pieces = [
        lax.dynamic_index_in_dim(x, chip ^ k, 0, keepdims=False) for k in range(count)
    ]
    return add_pieces(pieces, dp)


def exchange(grad, dp):
    kept, sent = split_core(grad, dp)
    x = kept + swap_core(sent, dp).astype(F32)
    steps = [1 << b for b in range((dp // 2).bit_length() - 1)]
    return scatter_bits(x, 0, steps[::-1], BF16, dp, 2)


def body(
    dp, tensor, inputs, ln_gain, ln_bias, w_qkv, b_qkv, w_out, w_in, b_in, w_down, out_bias,
    cotangent,
):
    model = inputs.shape[-1]
    heads, head_dim = b_qkv.shape[1], b_qkv.shape[2] * dp
    width = heads * head_dim
    hidden_units = w_in.shape[1]
    seqs, length = inputs.shape[0], inputs.shape[1] * tensor
    rows = seqs * length
    own = ln_gain.shape[0]
    share = own * tensor
    slow = [1 << b for b in range(1, dp.bit_length() - 1)]
    ways = (slow + [1], slow[::-1] + [1])
    me_z = lax.axis_index("tensor")

    full_in = lax.all_gather(inputs, "tensor", axis=1, tiled=True).reshape(rows, model)
    full_cot = lax.all_gather(cotangent, "tensor", axis=1, tiled=True).reshape(rows, model)

    vector = jnp.stack([ln_gain, ln_bias, out_bias[0] + out_bias[1]])
    by_z = [vector]
    for k in range(1, tensor):
        by_z.append(
            lax.ppermute(vector, "tensor", [(i, (i + k) % tensor) for i in range(tensor)])
        )
    by_z = jnp.stack(by_z)
    order = (me_z - jnp.arange(tensor)) % tensor
    by_z = jnp.take(by_z, order, axis=0).transpose(1, 0, 2)
    small = jnp.concatenate(
        [by_z.reshape(-1), b_qkv.astype(F32).reshape(-1), b_in.astype(F32).reshape(-1)]
    )
    used = small.shape[0]
    padded = -(-used // 1024) * 1024
    small = jnp.pad(small, (0, padded - used)).reshape(-1, 128)
    small = gather_bits(small, dp, 0, ways[0]).reshape(dp, padded)
    norm_rows = small[:, : 3 * share].reshape(dp, 3, share).transpose(1, 0, 2).reshape(3, model)
    out_shift = norm_rows[2]
    at = 3 * share
    qkv_count = b_qkv.size
    qkv_bias = (
        small[:, at : at + qkv_count]
        .reshape(dp, 3, heads, head_dim // dp)
        .transpose(1, 2, 0, 3)
        .reshape(3 * width)
    )
    at += qkv_count
    in_groups, in_each = b_in.shape
    in_bias = (
        small[:, at : at + b_in.size]
        .reshape(dp, in_groups, in_each)
        .transpose(1, 0, 2)
        .reshape(hidden_units)
    )

    first = gather_bits(jnp.concatenate([w_in, w_out.T], axis=1), dp, 0, ways[0])
    second = gather_bits(
        jnp.concatenate([w_down.T, w_qkv.reshape(w_qkv.shape[0], -1)], axis=1), dp, 0, ways[1],
    )
    first = first.reshape(model, -1)
    second = second.reshape(model, -1)

    cosine, sine = rotary_tables(length)
    unit, normed_t, proj_t, hidden, slopes = enter(
        full_in, norm_rows, in_bias.reshape(1, -1), qkv_bias.reshape(1, -1), first, second,
        cosine, sine, heads, head_dim,
    )
    ctx_t, probs = attend(proj_t, seqs, heads, head_dim, length)
    branch, context = branch_sum(ctx_t, hidden, first, second)
    summed = lax.psum_scatter(
        branch.reshape(seqs, length, model), "tensor", scatter_dimension=1, tiled=True
    )
    outputs = (inputs.astype(F32) + summed.astype(F32) + out_shift).astype(BF16)

    core, chip = bit_of("dp", 1), lax.axis_index("dp") // 2
    places = jnp.stack([1 - core, chip, core, chip]).astype(jnp.int32)
    cot_t, ctx_grad_t, pre_low, in_sum, cot_sum = return_grads(
        context, places, full_cot, slopes, first, second, width
    )
    part = model // dp
    aligned = 2 <= dp <= 8 and part % 16 == 0
    blocks = dp // 2
    if aligned:
        operands = (normed_t, cot_t, pre_low, context, hidden)
        shape = (part, 2 * hidden_units + width)
        flops = rows * model * shape[1]
        (early_sent,) = weight_half(
            early_kernel, places, 0, operands, None, blocks, part, shape, flops
        )
        early_got = swap_core(early_sent, dp)
        early_pieces = weight_half(
            early_kernel, places, 1, operands, early_got, blocks, part,
            shape, flops,
        )
        early = add_pieces(early_pieces, dp)
    else:
        early = jnp.concatenate(
            [
                dot(normed_t, pre_low, (1, 0)),
                dot(cot_t, hidden, (1, 0)),
                dot(cot_t, context, (1, 0)),
            ],
            axis=1,
        )
        early = exchange(early, dp)
    dq_t, dk_t, dv_t, sums = attend_back(
        proj_t, cosine, sine, probs, ctx_grad_t, seqs, heads, head_dim, length
    )
    proj_low, norm_grad, gain_sum, shift_sum = norm_sum(
        unit, dq_t, dk_t, dv_t, pre_low, first, second
    )
    own_grad = lax.psum_scatter(
        norm_grad.reshape(seqs, length, model), "tensor", scatter_dimension=1, tiled=True
    )
    grad_qkv_bias = jnp.sum(sums[..., 0], axis=0).transpose(1, 0, 2)
    grad_in_bias = jnp.sum(in_sum, axis=0)
    bias_part = jnp.sum(cot_sum, axis=0).reshape(dp, tensor, own)
    pair = jnp.stack([gain_sum, shift_sum]).sum(axis=1).reshape(2, dp, tensor, own)
    pair_total = lax.dynamic_index_in_dim(pair, me_z, 2, keepdims=False)
    for k in range(1, tensor):
        piece = lax.dynamic_index_in_dim(pair, (me_z + k) % tensor, 2, keepdims=False)
        got = lax.ppermute(
            piece, "tensor", [(i, (i + k) % tensor) for i in range(tensor)]
        )
        pair_total = pair_total + got
    bias_total = lax.dynamic_index_in_dim(bias_part, me_z, 1, keepdims=False)
    small = jnp.concatenate(
        [
            pair_total[0], pair_total[1], bias_total,
            grad_qkv_bias.reshape(3, heads, dp, head_dim // dp)
            .transpose(2, 0, 1, 3)
            .reshape(dp, -1),
            grad_in_bias.reshape(in_groups, dp, in_each).transpose(1, 0, 2).reshape(dp, -1),
        ],
        axis=1,
    )
    small = exchange_small(
        jnp.pad(small, ((0, 0), (0, -small.shape[1] % 128))), dp
    )
    if aligned:
        operands = (normed_t, proj_low)
        shape = (part, 3 * width)
        flops = rows * model * shape[1]
        (late_sent,) = weight_half(
            late_kernel, places, 0, operands, None, blocks, part, shape,
            flops,
        )
        late_got = swap_core(late_sent, dp)
        late_pieces = weight_half(
            late_kernel, places, 1, operands, late_got, blocks, part, shape,
            flops,
        )
        late = add_pieces(late_pieces, dp)
    else:
        late = exchange(dot(normed_t, proj_low, (1, 0)), dp)
    in_out = early[:, :hidden_units]
    down_out = early[:, hidden_units : 2 * hidden_units].T
    out_out = early[:, 2 * hidden_units :].T
    qkv_out = late.reshape(part, 3, width)
    gain_out, shift_out, bias_out = (small[k * own : (k + 1) * own] for k in range(3))
    bias_grad = jnp.stack([bias_out, bias_out])
    at = 3 * own
    qkv_bias_out = small[at : at + qkv_count].reshape(b_qkv.shape)
    at += qkv_count
    in_bias_out = small[at : at + b_in.size].reshape(b_in.shape)

    input_grad = finish(inputs, cotangent, own_grad, norm_rows)
    return (
        outputs,
        input_grad,
        gain_out,
        shift_out,
        qkv_out,
        qkv_bias_out,
        out_out,
        in_out,
        in_bias_out,
        down_out,
        bias_grad,
    )


def solution(mesh):
    spread = P("dp", "tensor", None)
    vector = P(("dp", "tensor"))
    qkv, qkv_bias = P("dp", None, "tensor"), P(None, "tensor", "dp")
    by_out, by_in, pair = P("tensor", "dp"), P("dp", "tensor"), P(None, ("dp", "tensor"))

    def layer(*arrays):
        return body(mesh.shape["dp"], mesh.shape["tensor"], *arrays)

    return jax.shard_map(
        layer,
        mesh=mesh,
        in_specs=(
            spread, vector, vector, qkv, qkv_bias, by_out, by_in, by_out, by_out, pair, spread,
        ),
        out_specs=(
            spread, spread, vector, vector, qkv, qkv_bias, by_out, by_in, by_out, by_out, pair,
        ),
        check_vma=False,
    )
```
